32 devices in a mesh: seq: 4 (over x, core), fsdp: 8 (over z, y).
Axes of the slice: x: 2, y: 2, z: 4, core: 2. Of those that a mesh axis runs over, the one named last changes fastest.
Arguments:
- tokens: bfloat16 [8, 2560, 2048], P('fsdp', 'seq'), may hold values from -6 to 6
- cont_lengths: int32 [8, 2], P('fsdp'), may hold values from 1 to 384, as said below
- project_in: bfloat16 [2048, 6144], P('fsdp'), may hold values from -0.125 to 0.125
- project_out: bfloat16 [2048, 2048], P('fsdp'), may hold values from -1.5 to 1.5
- gate_weight: bfloat16 [2048, 5632], P('fsdp'), may hold values from -0.125 to 0.125
- up_weight: bfloat16 [2048, 5632], P('fsdp'), may hold values from -0.125 to 0.125
- down_weight: bfloat16 [5632, 2048], P('fsdp'), may hold values from -0.078125 to 0.078125
- first_gain: bfloat16 [2048], P('fsdp'), may hold values from 0.099609375 to 1.8984375
- first_bias: bfloat16 [2048], P('fsdp'), may hold values from -3 to 3
- second_gain: bfloat16 [2048], P('fsdp'), may hold values from 0.099609375 to 1.8984375
- second_bias: bfloat16 [2048], P('fsdp'), may hold values from -3 to 3
- grad_output: bfloat16 [8, 2560, 2048], P('fsdp', 'seq'), may hold values from -6 to 6
Outputs:
- layer_out: bfloat16 [8, 2560, 2048], P('fsdp', 'seq')
- input_gradient: float32 [8, 2560, 2048], P('fsdp', 'seq')
- grad_project_in: float32 [2048, 6144], P('fsdp')
- grad_project_out: float32 [2048, 2048], P('fsdp')
- grad_gate_weight: float32 [2048, 5632], P('fsdp')
- grad_up_weight: float32 [2048, 5632], P('fsdp')
- grad_down_weight: float32 [5632, 2048], P('fsdp')
- grad_first_gain: float32 [2048], P('fsdp')
- grad_first_bias: float32 [2048], P('fsdp')
- grad_second_gain: float32 [2048], P('fsdp')
- grad_second_bias: float32 [2048], P('fsdp')
The draws below stay inside these ranges and needn't reach their ends.
Inputs may be any that keep to these rules, and one draw needn't show every extreme that they name: `cont_lengths`: each group's row sums to 512; exactly one of its entries, at a drawn place, equals 384, and every other entry is under 384.
All inputs are finite; a program needn't handle non-finite values.
Results may differ from the reference program's by a relative error of at most 0.018.
Values may be sent and summed in bfloat16 or wider, within the bound.
A program may use at most 512 MiB of HBM per device.

```python
import jax
import jax.numpy as jnp
from jax import lax

D = 2048
FF = 5632
HEAD_DIM = 64
ROT = 16
PROMPT = 2048
CLEN = 256
CONTS = 2
LONGEST = 384
GROUP_TOK = 2560
GROUPS = 8


def lengths_row(row_key):
    rest_count = CONTS - 1
    remain = CONTS * CLEN - LONGEST
    even_share = remain // rest_count
    leftover = remain % rest_count
    index_rest = jnp.arange(rest_count, dtype=jnp.int32)
    others = (even_share + (index_rest < leftover).astype(jnp.int32)).astype(jnp.int32)
    pair_count = rest_count // 2
    move_key, place_key = jax.random.split(row_key)
    if pair_count > 0:
        reach = min(even_share - 1, LONGEST - even_share - 2)
        moves = jax.random.randint(move_key, (pair_count,), -reach, reach + 1, dtype=jnp.int32)
        paired = jnp.stack([moves, -moves], axis=1).reshape(2 * pair_count)
        padding = jnp.zeros((rest_count - 2 * pair_count,), jnp.int32)
        others = others + jnp.concatenate([paired, padding]).astype(jnp.int32)
    place = jax.random.randint(place_key, (), 0, CONTS, dtype=jnp.int32)
    index_all = jnp.arange(CONTS, dtype=jnp.int32)
    rest_index = jnp.clip(index_all - (index_all > place).astype(jnp.int32), 0, rest_count - 1)
    return jnp.where(index_all == place, LONGEST, others[rest_index]).astype(jnp.int32)


def draw_cont_lengths(key, part):
    row_keys = jax.random.split(jax.random.fold_in(key, 7151), GROUPS)
    return jax.vmap(lengths_row)(row_keys).astype(jnp.int32)


def block_scale(own_key, dims, pieces, smallest, largest):
    loudness, own = 1.0, jax.random.fold_in(own_key, 6)
    for dim, shards_of in pieces:
        draws = jnp.exp(jax.random.uniform(jax.random.fold_in(own, dim), (shards_of,), jnp.float32, smallest / len(pieces), largest / len(pieces)))
        loudness = loudness * jnp.repeat(draws, dims[dim] // shards_of).reshape([-1 if axis == dim else 1 for axis in range(len(dims))])
    return loudness


def normal_values(stream_key, dims, scale, limit, pieces=(), held_as=jnp.bfloat16):
    array = scale * jax.random.normal(stream_key, dims, jnp.float32)
    if pieces:
        array = array * block_scale(stream_key, dims, pieces, -0.22, 0.18)
    return jnp.clip(array, -limit, limit).astype(held_as)


def setup_inputs(seed: int = 0) -> dict:
    arg_keys = jax.random.split(jax.random.key(seed), 13)
    tokens = normal_values(arg_keys[0], (GROUPS, GROUP_TOK, D), 1.0, 6.0, ((0, 8), (1, 4)))
    cont_lengths = draw_cont_lengths(jax.random.fold_in(arg_keys[12], 71), 0)
    project_in = normal_values(arg_keys[2], (D, 3 * D), D ** -0.5, 0.125, ((0, 8),))
    project_out = normal_values(arg_keys[3], (D, D), 16 ** -0.5, 1.5, ((0, 8),))
    gate_weight = normal_values(arg_keys[4], (D, FF), D ** -0.5, 0.125, ((0, 8),))
    up_weight = normal_values(arg_keys[5], (D, FF), D ** -0.5, 0.125, ((0, 8),))
    down_weight = normal_values(arg_keys[6], (FF, D), FF ** -0.5, 0.078125, ((0, 8),))
    first_gain = jnp.clip(1.0 + 0.18 * jax.random.normal(arg_keys[7], (D,), jnp.float32), 0.099609375, 1.8984375).astype(jnp.bfloat16)
    first_bias = normal_values(arg_keys[8], (D,), 0.5, 3.0, ((0, 8),))
    second_gain = jnp.clip(1.0 + 0.18 * jax.random.normal(arg_keys[9], (D,), jnp.float32), 0.099609375, 1.8984375).astype(jnp.bfloat16)
    second_bias = normal_values(arg_keys[10], (D,), 0.5, 3.0, ((0, 8),))
    grad_output = normal_values(arg_keys[11], (GROUPS, GROUP_TOK, D), 1.0, 6.0, ((0, 8), (1, 4)))
    return dict(tokens=tokens, cont_lengths=cont_lengths, project_in=project_in, project_out=project_out, gate_weight=gate_weight, up_weight=up_weight, down_weight=down_weight, first_gain=first_gain, first_bias=first_bias, second_gain=second_gain, second_bias=second_bias, grad_output=grad_output)


epsilon = 1e-05
rope_base = 10000.0
block_limit = 512

@jax.custom_vjp
def low(v):
    return lax.optimization_barrier(v.astype(jnp.bfloat16)).astype(jnp.float32)

@jax.custom_vjp
def low_back(v):
    return v

def low_keep(v):
    return (low(v), None)

def low_pass(kept, grad):
    return (grad,)

def back_keep(v):
    return (v, None)

def back_low(kept, grad):
    return (low(grad),)
low.defvjp(low_keep, low_pass)
low_back.defvjp(back_keep, back_low)

def matmul(left_side, right_side):
    return jnp.dot(left_side, right_side, precision=lax.Precision.HIGHEST, preferred_element_type=jnp.float32)

def layout(lengths, total_rows):
    indices = jnp.arange(total_rows, dtype=jnp.int32)
    seg_ends = jnp.cumsum(lengths).astype(jnp.int32)
    starts = (seg_ends - lengths).astype(jnp.int32)
    offset = (indices - PROMPT).astype(jnp.int32)
    inside = (offset[:, None] >= starts[None, :]) & (offset[:, None] < seg_ends[None, :])
    numbers = jnp.arange(1, lengths.shape[0] + 1, dtype=jnp.int32)
    segment = lax.optimization_barrier(jnp.sum(jnp.where(inside, numbers[None, :], 0), axis=1)).astype(jnp.int32)
    seg_begin = lax.optimization_barrier(jnp.sum(jnp.where(inside, starts[None, :], 0), axis=1)).astype(jnp.int32)
    position = jnp.where(indices < PROMPT, indices, PROMPT + offset - seg_begin).astype(jnp.int32)
    return (segment, position)

def rotate(rows_in, position, sign):
    row_count = rows_in.shape[0]
    heads = rows_in.shape[1] // HEAD_DIM
    half = ROT // 2
    frequency = rope_base ** (-2.0 * jnp.arange(half, dtype=jnp.float32) / ROT)
    angles = position.astype(jnp.float32)[:, None] * frequency[None, :]
    cosine = jnp.cos(angles)[:, None, :]
    sine_part = sign * jnp.sin(angles)[:, None, :]
    shaped = rows_in.reshape(row_count, heads, HEAD_DIM)
    first_half = shaped[:, :, :half]
    second = shaped[:, :, half:ROT]
    turned = jnp.concatenate([first_half * cosine - second * sine_part, second * cosine + first_half * sine_part, shaped[:, :, ROT:]], axis=2)
    return turned.reshape(row_count, heads * HEAD_DIM)

def apply_layer_norm(rows_in):
    mean_value = lax.optimization_barrier(jnp.mean(rows_in, axis=-1, keepdims=True))
    centered = rows_in - mean_value
    inverse_deviation = lax.rsqrt(lax.optimization_barrier(jnp.mean(centered * centered, axis=-1, keepdims=True)) + epsilon)
    return centered * inverse_deviation

def attend_group(operands):
    query_rows, key_rows, value_rows, segment = operands
    total_rows = query_rows.shape[0]
    heads = query_rows.shape[1] // HEAD_DIM
    block_rows = min(block_limit, total_rows)
    blocks = total_rows // block_rows
    key_heads = key_rows.reshape(total_rows, heads, HEAD_DIM)
    value_heads = value_rows.reshape(total_rows, heads, HEAD_DIM)
    indices = jnp.arange(total_rows, dtype=jnp.int32)
    factor = HEAD_DIM ** (-0.5)

    @jax.checkpoint
    def one_block(query_block, block_start):
        rows_here = block_start + jnp.arange(block_rows, dtype=jnp.int32)
        seg_here = lax.dynamic_slice_in_dim(segment, block_start, block_rows, 0)
        allowed = (indices[None, :] <= rows_here[:, None]) & ((segment[None, :] == 0) | (segment[None, :] == seg_here[:, None]))
        scores = jnp.einsum('qhd,khd->hqk', query_block, key_heads, precision=lax.Precision.HIGHEST) * factor
        scores = jnp.where(allowed[None], low_back(scores), -1e+30)
        chances = jax.nn.softmax(scores, axis=-1)
        return jnp.einsum('hqk,khd->qhd', low(chances), value_heads, precision=lax.Precision.HIGHEST)
    query_blocks = query_rows.reshape(blocks, block_rows, heads, HEAD_DIM)
    block_starts = jnp.arange(blocks, dtype=jnp.int32) * block_rows
    results = lax.map(lambda pair: one_block(pair[0], pair[1]), (query_blocks, block_starts))
    return results.reshape(total_rows, heads * HEAD_DIM)

def forward(tokens, project_in, project_out, gate_weight, up_weight, down_weight, first_gain, first_bias, second_gain, second_bias, segment, position):
    groups, total_rows, width = tokens.shape
    rows_in = tokens.reshape(groups * total_rows, width)
    flat_position = position.reshape(-1)
    normed_first = low(apply_layer_norm(rows_in) * first_gain + first_bias)
    mixed = low_back(matmul(normed_first, project_in))
    query_rows = low(rotate(mixed[:, :width], flat_position, 1.0))
    key_rows = low(rotate(mixed[:, width:2 * width], flat_position, 1.0))
    value_rows = low(mixed[:, 2 * width:])
    group_shape = (groups, total_rows, width)
    attended = lax.map(attend_group, (query_rows.reshape(group_shape), key_rows.reshape(group_shape), value_rows.reshape(group_shape), segment))
    attended = low(low_back(attended.reshape(groups * total_rows, width)))
    hidden_state = rows_in + low_back(matmul(attended, project_out))
    normed_second = low(apply_layer_norm(hidden_state) * second_gain + second_bias)
    gate_pre = low_back(matmul(normed_second, gate_weight))
    up_pre = low_back(matmul(normed_second, up_weight))
    product = low(jax.nn.silu(gate_pre) * up_pre)
    layer_rows = hidden_state + low_back(matmul(product, down_weight))
    return layer_rows.reshape(groups, total_rows, width)

def reference(tokens, cont_lengths, project_in, project_out, gate_weight, up_weight, down_weight, first_gain, first_bias, second_gain, second_bias, grad_output):
    total_rows = tokens.shape[1]
    segment, position = jax.vmap(lambda lengths: layout(lengths, total_rows))(cont_lengths)
    floats = tuple((array_in.astype(jnp.float32) for array_in in (tokens, project_in, project_out, gate_weight, up_weight, down_weight, first_gain, first_bias, second_gain, second_bias)))

    def wrapped(tokens_f, proj_in_f, proj_out_f, gate_f, up_f, down_f, first_norm_gain, first_norm_bias, second_norm_gain, second_norm_bias):
        return forward(tokens_f, proj_in_f, proj_out_f, gate_f, up_f, down_f, first_norm_gain, first_norm_bias, second_norm_gain, second_norm_bias, segment, position)
    layer_rows, pullback = jax.vjp(wrapped, *floats)
    grads = pullback(grad_output.astype(jnp.float32))
    return (layer_rows.astype(jnp.bfloat16), grads[0], grads[1], grads[2], grads[3], grads[4], grads[5], grads[6], grads[7], grads[8], grads[9])
```

```python
import functools

import jax
import jax.numpy as jnp
from jax import lax
from jax.experimental import pallas as pl
from jax.experimental.pallas import tpu as pltpu
from jax.sharding import PartitionSpec as P

HEAD_DIM = 64
ROT = 16
PROMPT = 2048
LANES = 128

epsilon = 1e-05
rope_base = 10000.0

BF16 = jnp.bfloat16
F32 = jnp.float32
CORES = 2
VMEM_LIMIT = 56 * 1024 * 1024


def dot_last(left_side, right_side):
    return lax.dot_general(
        left_side, right_side, (((1,), (1,)), ((), ())), preferred_element_type=F32
    )


def dot_first(left_side, right_side):
    return lax.dot_general(
        left_side, right_side, (((0,), (0,)), ((), ())), preferred_element_type=F32
    )


def dot(left_side, right_side):
    return jnp.dot(left_side, right_side, preferred_element_type=F32)


def cont_ends(lengths):
    count = lengths.shape[0]
    before = jnp.arange(count)[None, :] <= jnp.arange(count)[:, None]
    return jnp.sum(jnp.where(before, lengths[None, :], 0), axis=1)


def rope_tables(lengths, total_rows):
    ends = cont_ends(lengths)
    starts = ends - lengths
    indices = jnp.arange(total_rows, dtype=jnp.int32)
    offset = indices - PROMPT
    inside = (offset[:, None] >= starts[None, :]) & (offset[:, None] < ends[None, :])
    seg_begin = jnp.sum(jnp.where(inside, starts[None, :], 0), axis=1)
    position = jnp.where(indices < PROMPT, indices, PROMPT + offset - seg_begin)
    half = ROT // 2
    within = jnp.arange(LANES, dtype=jnp.int32) % HEAD_DIM
    frequency = rope_base ** (-2.0 * (within % half).astype(F32) / ROT)
    angles = position.astype(F32)[:, None] * frequency[None, :]
    turning = (within < ROT)[None, :]
    sign = jnp.where(within < half, -1.0, 1.0)[None, :]
    cosine = jnp.where(turning, jnp.cos(angles), 1.0)
    sine = jnp.where(turning, sign * jnp.sin(angles), 0.0)
    return cosine, sine, ends


def turn(rows_in, cosine, sine):
    half = ROT // 2
    lane = lax.broadcasted_iota(jnp.int32, rows_in.shape, 1) % HEAD_DIM
    partner = jnp.where(
        lane < half,
        pltpu.roll(rows_in, LANES - half, 1),
        pltpu.roll(rows_in, half, 1),
    )
    return rows_in * cosine + partner * sine


def project_kernel(x_ref, w_ref, cos_ref, sin_ref, out_ref):
    cosine = cos_ref[...]
    sine = sin_ref[...]
    pairs = out_ref.shape[1] // (3 * LANES)
    x = x_ref[...]
    for pair in range(pairs):
        base = 3 * LANES * pair
        mixed = dot(x, w_ref[:, base : base + 3 * LANES])
        query = turn(mixed[:, :LANES], cosine, sine) * HEAD_DIM ** (-0.5)
        key = turn(mixed[:, LANES : 2 * LANES], cosine, sine)
        out_ref[:, base : base + LANES] = query.astype(BF16)
        out_ref[:, base + LANES : base + 2 * LANES] = key.astype(BF16)
        out_ref[:, base + 2 * LANES : base + 3 * LANES] = mixed[:, 2 * LANES :].astype(BF16)


def project(x, weight, cosine, sine):
    rows, depth = x.shape
    columns = weight.shape[1]
    block = 512
    return pl.pallas_call(
        project_kernel,
        grid=(rows // block,),
        in_specs=[
            pl.BlockSpec((block, depth), lambda i: (i, 0)),
            pl.BlockSpec((depth, columns), lambda i: (0, 0), pipeline_mode=pl.Buffered(1)),
            pl.BlockSpec((block, LANES), lambda i: (i, 0)),
            pl.BlockSpec((block, LANES), lambda i: (i, 0)),
        ],
        out_specs=pl.BlockSpec((block, columns), lambda i: (i, 0)),
        out_shape=jax.ShapeDtypeStruct((rows, columns), BF16),
        compiler_params=pltpu.CompilerParams(vmem_limit_bytes=VMEM_LIMIT),
        cost_estimate=pl.CostEstimate(
            flops=2 * rows * depth * columns,
            bytes_accessed=2 * (rows * depth + depth * columns + rows * columns),
            transcendentals=0,
        ),
        name="project_in_rope",
    )(x, weight, cosine, sine)


BLOCK = 512
NEG = -1e30


def segment_of(index, ends_ref):
    count = jnp.zeros_like(index)
    for c in range(ends_ref.shape[0] - 1):
        count = count + (index >= PROMPT + ends_ref[c]).astype(jnp.int32)
    return count


def attend_kernel(ends_ref, q_ref, k_ref, v_ref, o_ref, qx_ref):
    number = pl.program_id(1)
    lane = lax.broadcasted_iota(jnp.int32, (BLOCK, LANES), 1)
    q = q_ref[...]
    inside = [lane < HEAD_DIM, lane >= HEAD_DIM]
    q_head = [jnp.where(inside[h], q, jnp.zeros_like(q)) for h in range(2)]

    def step(start, carry, masked):
        k = k_ref[pl.ds(start, BLOCK), :]
        v = v_ref[pl.ds(start, BLOCK), :]
        if masked:
            row = lax.broadcasted_iota(jnp.int32, (BLOCK, 1), 0) + start
            col = lax.broadcasted_iota(jnp.int32, (1, BLOCK), 1) + start
            visible = (col <= row) & (segment_of(row, ends_ref) == segment_of(col, ends_ref))
        new = []
        for h in range(2):
            peak, acc = carry[h]
            scores = dot_last(q_head[h], k)
            if masked:
                scores = jnp.where(visible, scores, NEG)
            higher = jnp.maximum(peak, jnp.max(scores, axis=1, keepdims=True))
            weights = jnp.exp(scores - higher)
            shrink = jnp.exp(peak - higher)
            v_one = jnp.where(inside[h], v, jnp.ones_like(v))
            acc = acc * shrink + dot(weights.astype(BF16), v_one)
            new.append((higher, acc))
        return tuple(new)

    init = tuple(
        (jnp.full((BLOCK, 1), NEG, F32), jnp.zeros((BLOCK, LANES), F32)) for _ in range(2)
    )
    carry = lax.fori_loop(
        0, number, lambda j, c: step(pl.multiple_of(j * BLOCK, BLOCK), c, False), init
    )
    carry = step(pl.multiple_of(number * BLOCK, BLOCK), carry, True)
    outs = []
    for h in range(2):
        peak, acc = carry[h]
        outs.append(acc / pltpu.roll(acc, HEAD_DIM, 1))
        total = jnp.where(inside[h], 1.0, acc)
        minus = -(peak + jnp.log(total))
        high = minus.astype(BF16)
        rest = minus - high.astype(F32)
        mid = rest.astype(BF16)
        low = (rest - mid.astype(F32)).astype(BF16)
        base = HEAD_DIM * (1 - h)
        zero = jnp.zeros_like(high)
        spare = jnp.where(lane == base, high, jnp.where(lane == base + 1, mid, zero))
        spare = jnp.where(lane == base + 2, low, spare)
        qx_ref[h] = jnp.where(inside[h], q, spare)
    o_ref[...] = jnp.where(inside[0], outs[0], outs[1]).astype(BF16)


def attend(ends, qkv):
    rows, columns = qkv.shape
    pairs = columns // (3 * LANES)
    blocks = rows // BLOCK
    work = rows * rows // 2 * pairs * 2
    return pl.pallas_call(
        attend_kernel,
        grid_spec=pltpu.PrefetchScalarGridSpec(
            num_scalar_prefetch=1,
            grid=(pairs, blocks),
            in_specs=[
                pl.BlockSpec((BLOCK, LANES), lambda p, i, e: (i, 3 * p)),
                pl.BlockSpec((rows, LANES), lambda p, i, e: (0, 3 * p + 1)),
                pl.BlockSpec((rows, LANES), lambda p, i, e: (0, 3 * p + 2)),
            ],
            out_specs=[
                pl.BlockSpec((BLOCK, LANES), lambda p, i, e: (i, p)),
                pl.BlockSpec((2, BLOCK, LANES), lambda p, i, e: (p, i, 0)),
            ],
        ),
        out_shape=[
            jax.ShapeDtypeStruct((rows, pairs * LANES), BF16),
            jax.ShapeDtypeStruct((2 * pairs, rows, LANES), BF16),
        ],
        compiler_params=pltpu.CompilerParams(vmem_limit_bytes=VMEM_LIMIT),
        cost_estimate=pl.CostEstimate(
            flops=work * 1024, bytes_accessed=2 * rows * columns * 3, transcendentals=work
        ),
        name="attend",
    )(ends, qkv, qkv, qkv)


def attend_back_kernel(
    ends_ref, qx_ref, k_ref, v_ref, g_ref, o_ref, cos_ref, sin_ref, out_ref,
    gx_ref, dq_ref, dk_ref, dv_ref,
):
    number = pl.program_id(1)
    blocks = pl.num_programs(1)
    rows = qx_ref.shape[1]
    lane = lax.broadcasted_iota(jnp.int32, (BLOCK, LANES), 1)
    inside = [lane < HEAD_DIM, lane >= HEAD_DIM]

    @pl.when(number == 0)
    def _():
        dq_ref[...] = jnp.zeros_like(dq_ref)

        @pl.loop(0, rows // BLOCK)
        def _(j):
            here = pl.ds(pl.multiple_of(j * BLOCK, BLOCK), BLOCK)
            g = g_ref[here, :]
            both = g.astype(F32) * o_ref[here, :].astype(F32)
            for h in range(2):
                minus = -jnp.sum(jnp.where(inside[h], both, 0.0), axis=1, keepdims=True)
                high = minus.astype(BF16)
                rest = minus - high.astype(F32)
                mid = rest.astype(BF16)
                low = (rest - mid.astype(F32)).astype(BF16)
                base = HEAD_DIM * (1 - h)
                spare = jnp.where(
                    lane == base, high, jnp.where(lane == base + 1, mid, jnp.zeros_like(g))
                )
                spare = jnp.where(lane == base + 2, low, spare)
                gx_ref[h, here, :] = jnp.where(inside[h], g, spare)

    k = k_ref[...]
    v = v_ref[...]
    k_one = [jnp.where(inside[h], k, jnp.ones_like(k)) for h in range(2)]
    v_one = [jnp.where(inside[h], v, jnp.ones_like(v)) for h in range(2)]
    k_turned = [jnp.where(inside[h], k, jnp.zeros_like(k)).T for h in range(2)]
    dk_ref[...] = jnp.zeros_like(dk_ref)
    dv_ref[...] = jnp.zeros_like(dv_ref)

    def step(start, masked):
        here = pl.ds(start, BLOCK)
        if masked:
            row = lax.broadcasted_iota(jnp.int32, (1, BLOCK), 1) + start
            col = lax.broadcasted_iota(jnp.int32, (BLOCK, 1), 0) + start
            visible = (col <= row) & (segment_of(row, ends_ref) == segment_of(col, ends_ref))
        total = None
        for h in range(2):
            qx = qx_ref[h, here, :]
            gx = gx_ref[h, here, :]
            chances = jnp.exp(dot_last(k_one[h], qx))
            if masked:
                chances = jnp.where(visible, chances, 0.0)
            dv_ref[h] += dot(chances.astype(BF16), gx)
            grad_scores = (chances * dot_last(v_one[h], gx)).astype(BF16)
            dk_ref[h] += dot(grad_scores, qx)
            part = dot(k_turned[h], grad_scores)
            total = part if total is None else total + part
        dq_ref[:, here] += total

    step(pl.multiple_of(number * BLOCK, BLOCK), True)

    @pl.loop(number + 1, blocks)
    def _(j):
        step(pl.multiple_of(j * BLOCK, BLOCK), False)

    here = pl.ds(pl.multiple_of(number * BLOCK, BLOCK), BLOCK)
    dk = jnp.where(inside[0], dk_ref[0], dk_ref[1])
    dk = turn(dk, cos_ref[here, :], -sin_ref[here, :])
    out_ref[here, LANES : 2 * LANES] = dk.astype(BF16)
    out_ref[here, 2 * LANES :] = jnp.where(inside[0], dv_ref[0], dv_ref[1]).astype(BF16)

    @pl.when(number == blocks - 1)
    def _():
        for j in range(rows // BLOCK):
            here = slice(j * BLOCK, (j + 1) * BLOCK)
            dq = dq_ref[:, here].T * HEAD_DIM ** (-0.5)
            dq = turn(dq, cos_ref[here, :], -sin_ref[here, :])
            out_ref[here, :LANES] = dq.astype(BF16)


def attend_back(ends, qkv, qx, grad, attended, cosine, sine):
    rows, columns = qkv.shape
    pairs = columns // (3 * LANES)
    blocks = rows // BLOCK
    work = rows * rows // 2 * pairs * 2
    return pl.pallas_call(
        attend_back_kernel,
        grid_spec=pltpu.PrefetchScalarGridSpec(
            num_scalar_prefetch=1,
            grid=(pairs, blocks),
            in_specs=[
                pl.BlockSpec((2, rows, LANES), lambda p, i, e: (p, 0, 0)),
                pl.BlockSpec((BLOCK, LANES), lambda p, i, e: (i, 3 * p + 1)),
                pl.BlockSpec((BLOCK, LANES), lambda p, i, e: (i, 3 * p + 2)),
                pl.BlockSpec((rows, LANES), lambda p, i, e: (0, p)),
                pl.BlockSpec((rows, LANES), lambda p, i, e: (0, p)),
                pl.BlockSpec((rows, LANES), lambda p, i, e: (0, 0)),
                pl.BlockSpec((rows, LANES), lambda p, i, e: (0, 0)),
            ],
            out_specs=pl.BlockSpec((rows, 3 * LANES), lambda p, i, e: (0, p)),
            scratch_shapes=[
                pltpu.VMEM((2, rows, LANES), BF16),
                pltpu.VMEM((LANES, rows), F32),
                pltpu.VMEM((2, BLOCK, LANES), F32),
                pltpu.VMEM((2, BLOCK, LANES), F32),
            ],
        ),
        out_shape=jax.ShapeDtypeStruct((rows, columns), BF16),
        compiler_params=pltpu.CompilerParams(vmem_limit_bytes=VMEM_LIMIT),
        cost_estimate=pl.CostEstimate(
            flops=work * 2560, bytes_accessed=2 * rows * columns * 4, transcendentals=work
        ),
        name="attend_back",
    )(ends, qx, qkv, qkv, grad, attended, cosine, sine)


def seq_shift(value, chips, shift):
    size = chips * CORES
    return lax.ppermute(
        value, "seq", [(i, (i + shift * CORES) % size) for i in range(size)]
    )


def core_swap(value, chips):
    return lax.ppermute(value, "seq", [(i, i ^ 1) for i in range(chips * CORES)])


def gather_rows(block, chips):
    rows = block.shape[0]
    me = lax.axis_index("seq")
    core = me % CORES
    chip = me // CORES
    whole = jnp.zeros((rows * chips * CORES,) + block.shape[1:], block.dtype)
    for shift in range(chips):
        mine = block if shift == 0 else seq_shift(block, chips, shift)
        other = core_swap(mine, chips)
        source = (chip + chips - shift) % chips
        for held, which in ((mine, core), (other, 1 - core)):
            start = (source * CORES + which) * rows
            whole = lax.dynamic_update_slice_in_dim(whole, held, start, 0)
    return whole


def scatter_rows(partial, chips):
    rows = partial.shape[0] // (chips * CORES)
    me = lax.axis_index("seq")
    core = me % CORES
    chip = me // CORES

    def block_of(which_chip, which_core):
        start = (which_chip * CORES + which_core) * rows
        return lax.dynamic_slice_in_dim(partial, start, rows, 0)

    summed = []
    for shift in range(chips):
        target = (chip + shift) % chips
        theirs = core_swap(block_of(target, 1 - core), chips)
        summed.append(block_of(target, core).astype(F32) + theirs.astype(F32))
    total = summed[0]
    for shift in range(1, chips):
        total = total + seq_shift(summed[shift].astype(BF16), chips, shift).astype(F32)
    return total


def exchange_shards(value, seq_size, fsdp_size, back):
    ratio = fsdp_size // seq_size
    pairs = []
    for shard in range(fsdp_size):
        for copy in range(seq_size):
            source = copy * fsdp_size + shard
            target = (shard // ratio) * fsdp_size + (shard % ratio) * seq_size + copy
            pairs.append((target, source) if back else (source, target))
    return lax.ppermute(value, ("seq", "fsdp"), pairs)


def unit_rows(rows_in):
    mean_value = jnp.mean(rows_in, axis=-1, keepdims=True)
    centered = rows_in - mean_value
    inverse = lax.rsqrt(jnp.mean(centered * centered, axis=-1, keepdims=True) + epsilon)
    return centered * inverse, inverse


def norm_backward(gradient, unit, inverse, gain):
    scaled = gradient * gain
    mean_value = jnp.mean(scaled, axis=-1, keepdims=True)
    along = jnp.mean(scaled * unit, axis=-1, keepdims=True)
    return inverse * (scaled - mean_value - unit * along)


def gather_fsdp(value):
    return lax.all_gather(value, "fsdp", axis=0, tiled=True)


def scatter_fsdp(value):
    return lax.psum_scatter(value, "fsdp", scatter_dimension=0, tiled=True)


def local(
    tokens,
    cont_lengths,
    project_in,
    project_out,
    gate_weight,
    up_weight,
    down_weight,
    first_gain,
    first_bias,
    second_gain,
    second_bias,
    grad_output,
):
    rows_dev, width = tokens.shape[1:]
    seq_size = lax.axis_size("seq")
    fsdp_size = lax.axis_size("fsdp")
    chips = seq_size // CORES
    total_rows = rows_dev * seq_size
    me = lax.axis_index("seq")
    shard_rows = project_in.shape[0]
    hidden_units = gate_weight.shape[1]
    own_units = hidden_units // seq_size
    own_pairs = width // LANES // seq_size
    pieces_out = project_out.shape[0] // seq_size
    pieces_down = down_weight.shape[0] // seq_size

    in_cols = lax.dynamic_slice_in_dim(
        project_in.reshape(shard_rows, 3, width), me * own_pairs * LANES, own_pairs * LANES, 2
    )
    in_part = jnp.concatenate(
        [
            in_cols[:, part, pair * LANES : (pair + 1) * LANES]
            for pair in range(own_pairs)
            for part in range(3)
        ],
        axis=1,
    )
    gate_part = lax.dynamic_slice_in_dim(gate_weight, me * own_units, own_units, 1)
    up_part = lax.dynamic_slice_in_dim(up_weight, me * own_units, own_units, 1)
    out_piece = exchange_shards(
        lax.dynamic_slice_in_dim(project_out, me * pieces_out, pieces_out, 0),
        seq_size, fsdp_size, False,
    )
    down_piece = exchange_shards(
        lax.dynamic_slice_in_dim(down_weight, me * pieces_down, pieces_down, 0),
        seq_size, fsdp_size, False,
    )
    vectors = gather_fsdp(
        jnp.stack([first_gain, first_bias, second_gain, second_bias], axis=1)
    ).astype(F32)
    gain_one, bias_one, gain_two, bias_two = [vectors[:, i] for i in range(4)]
    w_in = gather_fsdp(in_part)
    w_out = gather_fsdp(out_piece)
    w_gate = gather_fsdp(gate_part)
    w_up = gather_fsdp(up_part)
    w_down = gather_fsdp(down_piece)

    cosine, sine, ends = rope_tables(cont_lengths[0], total_rows)

    residual = tokens[0].astype(F32)
    all_tokens = gather_rows(tokens[0], chips)
    all_unit, _ = unit_rows(all_tokens.astype(F32))
    normed_first = (all_unit * gain_one + bias_one).astype(BF16)
    qkv = project(normed_first, w_in, cosine, sine)
    attended, qx = attend(ends, qkv)
    hidden = residual + scatter_rows(dot(attended, w_out).astype(BF16), chips)
    unit_two, inverse_two = unit_rows(hidden)
    normed_second = gather_rows((unit_two * gain_two + bias_two).astype(BF16), chips)
    all_upstream = gather_rows(grad_output[0], chips)

    gate_pre = dot(normed_second, w_gate)
    up_pre = dot(normed_second, w_up)
    sigmoid = jax.nn.sigmoid(gate_pre)
    silu = gate_pre * sigmoid
    product = (silu * up_pre).astype(BF16)
    grad_mid = dot_last(all_upstream, w_down)
    grad_gate = (grad_mid * up_pre * sigmoid * (1.0 + gate_pre * (1.0 - sigmoid))).astype(BF16)
    grad_up = (grad_mid * silu).astype(BF16)

    second_gradient = scatter_rows(
        (dot_last(grad_gate, w_gate) + dot_last(grad_up, w_up)).astype(BF16), chips
    )
    upstream = grad_output[0].astype(F32)
    grad_hidden = upstream + norm_backward(second_gradient, unit_two, inverse_two, gain_two)
    low_hidden = gather_rows(grad_hidden.astype(BF16), chips)

    layer_rows = hidden + scatter_rows(dot(product, w_down).astype(BF16), chips)

    grad_gate_piece = scatter_fsdp(dot_first(normed_second, grad_gate).astype(BF16))
    grad_up_piece = scatter_fsdp(dot_first(normed_second, grad_up).astype(BF16))
    grad_down_piece = scatter_fsdp(dot_first(product, all_upstream).astype(BF16))

    grad_attended = dot_last(low_hidden, w_out).astype(BF16)
    grad_out_piece = scatter_fsdp(dot_first(attended, low_hidden).astype(BF16))
    grad_qkv = attend_back(ends, qkv, qx, grad_attended, attended, cosine, sine)
    grad_in_piece = scatter_fsdp(dot_first(normed_first, grad_qkv).astype(BF16))
    first_gradient = scatter_rows(dot_last(grad_qkv, w_in).astype(BF16), chips)
    unit_one, inverse_one = unit_rows(residual)
    input_gradient = grad_hidden + norm_backward(first_gradient, unit_one, inverse_one, gain_one)

    sums = jnp.stack(
        [
            jnp.sum(first_gradient * unit_one, axis=0),
            jnp.sum(first_gradient, axis=0),
            jnp.sum(second_gradient * unit_two, axis=0),
            jnp.sum(second_gradient, axis=0),
        ],
        axis=1,
    )
    sums = lax.psum(scatter_fsdp(sums), "seq")

    def gathered(piece):
        return gather_rows(piece, chips).reshape((seq_size,) + piece.shape)

    grad_in = gathered(grad_in_piece).reshape(seq_size, shard_rows, own_pairs, 3, LANES)
    grad_in = jnp.transpose(grad_in, (1, 3, 0, 2, 4)).reshape(shard_rows, 3 * width).astype(F32)
    grad_gate_w = jnp.transpose(gathered(grad_gate_piece), (1, 0, 2)).reshape(gate_weight.shape)
    grad_up_w = jnp.transpose(gathered(grad_up_piece), (1, 0, 2)).reshape(up_weight.shape)
    grad_out = gather_rows(exchange_shards(grad_out_piece, seq_size, fsdp_size, True), chips)
    grad_down = gather_rows(exchange_shards(grad_down_piece, seq_size, fsdp_size, True), chips)

    return (
        layer_rows.astype(BF16)[None],
        input_gradient[None],
        grad_in,
        grad_out.astype(F32),
        grad_gate_w.astype(F32),
        grad_up_w.astype(F32),
        grad_down.astype(F32),
        sums[:, 0],
        sums[:, 1],
        sums[:, 2],
        sums[:, 3],
    )


def solution(mesh):
    return jax.shard_map(
        local,
        mesh=mesh,
        in_specs=(
            P("fsdp", "seq", None),
            P("fsdp", None),
            P("fsdp", None),
            P("fsdp", None),
            P("fsdp", None),
            P("fsdp", None),
            P("fsdp", None),
            P("fsdp"),
            P("fsdp"),
            P("fsdp"),
            P("fsdp"),
            P("fsdp", "seq", None),
        ),
        out_specs=(
            P("fsdp", "seq", None),
            P("fsdp", "seq", None),
            P("fsdp", None),
            P("fsdp", None),
            P("fsdp", None),
            P("fsdp", None),
            P("fsdp", None),
            P("fsdp"),
            P("fsdp"),
            P("fsdp"),
            P("fsdp"),
        ),
        check_vma=False,
    )
```

```python
import functools

import jax
import jax.numpy as jnp
from jax import lax
from jax.experimental import pallas as pl
from jax.experimental.pallas import tpu as pltpu
from jax.sharding import PartitionSpec as P

HEAD_DIM = 64
ROT = 16
PROMPT = 2048
LANES = 128

epsilon = 1e-05
rope_base = 10000.0

BF16 = jnp.bfloat16
F32 = jnp.float32
CORES = 2
VMEM_LIMIT = 56 * 1024 * 1024


def dot_last(left_side, right_side):
    return lax.dot_general(
        left_side, right_side, (((1,), (1,)), ((), ())), preferred_element_type=F32
    )


def dot_first(left_side, right_side):
    return lax.dot_general(
        left_side, right_side, (((0,), (0,)), ((), ())), preferred_element_type=F32
    )


def dot(left_side, right_side):
    return jnp.dot(left_side, right_side, preferred_element_type=F32)


def cont_ends(lengths):
    count = lengths.shape[0]
    before = jnp.arange(count)[None, :] <= jnp.arange(count)[:, None]
    return jnp.sum(jnp.where(before, lengths[None, :], 0), axis=1)


def rope_tables(lengths, total_rows):
    ends = cont_ends(lengths)
    starts = ends - lengths
    indices = jnp.arange(total_rows, dtype=jnp.int32)
    offset = indices - PROMPT
    inside = (offset[:, None] >= starts[None, :]) & (offset[:, None] < ends[None, :])
    seg_begin = jnp.sum(jnp.where(inside, starts[None, :], 0), axis=1)
    position = jnp.where(indices < PROMPT, indices, PROMPT + offset - seg_begin)
    half = ROT // 2
    within = jnp.arange(LANES, dtype=jnp.int32) % HEAD_DIM
    frequency = rope_base ** (-2.0 * (within % half).astype(F32) / ROT)
    angles = position.astype(F32)[:, None] * frequency[None, :]
    turning = (within < ROT)[None, :]
    sign = jnp.where(within < half, -1.0, 1.0)[None, :]
    cosine = jnp.where(turning, jnp.cos(angles), 1.0)
    sine = jnp.where(turning, sign * jnp.sin(angles), 0.0)
    return cosine, sine, ends


def turn(rows_in, cosine, sine):
    half = ROT // 2
    lane = lax.broadcasted_iota(jnp.int32, rows_in.shape, 1) % HEAD_DIM
    partner = jnp.where(
        lane < half,
        pltpu.roll(rows_in, LANES - half, 1),
        pltpu.roll(rows_in, half, 1),
    )
    return rows_in * cosine + partner * sine


def project_kernel(x_ref, w_ref, gain_ref, bias_ref, cos_ref, sin_ref, out_ref, normed_ref):
    cosine = cos_ref[...]
    sine = sin_ref[...]
    pairs = out_ref.shape[1] // (3 * LANES)
    x = x_ref[...].astype(F32)
    x = x - jnp.mean(x, axis=1, keepdims=True)
    x = x * lax.rsqrt(jnp.mean(x * x, axis=1, keepdims=True) + epsilon)
    x = (x * gain_ref[0:1, :] + bias_ref[0:1, :]).astype(BF16)
    normed_ref[...] = x
    for first in range(0, pairs, 2):
        begin = 3 * LANES * first
        mixed = dot(x, w_ref[:, begin : begin + 6 * LANES])
        for pair in range(2):
            base = 3 * LANES * pair
            query = turn(mixed[:, base : base + LANES], cosine, sine) * HEAD_DIM ** (-0.5)
            key = turn(mixed[:, base + LANES : base + 2 * LANES], cosine, sine)
            value = mixed[:, base + 2 * LANES : base + 3 * LANES]
            base = base + begin
            out_ref[:, base : base + LANES] = query.astype(BF16)
            out_ref[:, base + LANES : base + 2 * LANES] = key.astype(BF16)
            out_ref[:, base + 2 * LANES : base + 3 * LANES] = value.astype(BF16)


def project(x, weight, gain, bias, cosine, sine):
    rows, depth = x.shape
    columns = weight.shape[1]
    block = 512
    vector = pl.BlockSpec((8, depth), lambda i: (0, 0))
    return pl.pallas_call(
        project_kernel,
        grid=(rows // block,),
        in_specs=[
            pl.BlockSpec((block, depth), lambda i: (i, 0)),
            pl.BlockSpec((depth, columns), lambda i: (0, 0), pipeline_mode=pl.Buffered(1)),
            vector,
            vector,
            pl.BlockSpec((block, LANES), lambda i: (i, 0)),
            pl.BlockSpec((block, LANES), lambda i: (i, 0)),
        ],
        out_specs=[
            pl.BlockSpec((block, columns), lambda i: (i, 0)),
            pl.BlockSpec((block, depth), lambda i: (i, 0)),
        ],
        out_shape=[
            jax.ShapeDtypeStruct((rows, columns), BF16),
            jax.ShapeDtypeStruct((rows, depth), BF16),
        ],
        compiler_params=pltpu.CompilerParams(vmem_limit_bytes=VMEM_LIMIT),
        cost_estimate=pl.CostEstimate(
            flops=2 * rows * depth * columns,
            bytes_accessed=2 * (rows * depth + depth * columns + rows * columns),
            transcendentals=0,
        ),
        name="project_in_rope",
    )(
        x,
        weight,
        jnp.broadcast_to(gain[None], (8, depth)),
        jnp.broadcast_to(bias[None], (8, depth)),
        cosine,
        sine,
    )


BLOCK = 512
NEG = -1e30


def segment_of(index, ends_ref):
    count = jnp.zeros_like(index)
    for c in range(ends_ref.shape[0] - 1):
        count = count + (index >= PROMPT + ends_ref[c]).astype(jnp.int32)
    return count


def attend_kernel(ends_ref, *refs):
    held = len(refs) // 3
    q_refs, k_refs, v_refs = refs[:held], refs[held : 2 * held], refs[2 * held : 3 * held]
    o_ref, qx_ref = refs[3 * held :]
    rows = k_refs[0].shape[0]
    lane = lax.broadcasted_iota(jnp.int32, (BLOCK, LANES), 1)
    inside = [lane < HEAD_DIM, lane >= HEAD_DIM]

    def one_block(number):
        start = number * BLOCK
        end = start + BLOCK
        full = min(start, PROMPT)
        row = lax.broadcasted_iota(jnp.int32, (BLOCK, 1), 0) + start
        col = lax.broadcasted_iota(jnp.int32, (1, end - full), 1) + full
        visible = col <= row
        if end > PROMPT:
            visible = visible & (segment_of(row, ends_ref) == segment_of(col, ends_ref))
        for pair in range(held):
            q = q_refs[pair][...]
            outs = []
            for h in range(2):
                q_head = jnp.where(inside[h], q, jnp.zeros_like(q))
                v = v_refs[pair][:end, :]
                lane_v = lax.broadcasted_iota(jnp.int32, v.shape, 1)
                own_v = (lane_v < HEAD_DIM) if h == 0 else (lane_v >= HEAD_DIM)
                v_one = jnp.where(own_v, v, jnp.ones_like(v))
                near = dot_last(q_head, k_refs[pair][full:end, :])
                near = jnp.where(visible, near, NEG)
                peak = jnp.max(near, axis=1, keepdims=True)
                if full:
                    early = dot_last(q_head, k_refs[pair][:full, :])
                    peak = jnp.maximum(peak, jnp.max(early, axis=1, keepdims=True))
                acc = dot(jnp.exp(near - peak).astype(BF16), v_one[full:])
                if full:
                    acc = acc + dot(jnp.exp(early - peak).astype(BF16), v_one[:full])
                outs.append(acc / pltpu.roll(acc, HEAD_DIM, 1))
                minus = -(peak + jnp.log(jnp.where(inside[h], 1.0, acc)))
                high = minus.astype(BF16)
                rest = minus - high.astype(F32)
                mid = rest.astype(BF16)
                low = (rest - mid.astype(F32)).astype(BF16)
                base = HEAD_DIM * (1 - h)
                spare = jnp.where(
                    lane == base, high, jnp.where(lane == base + 1, mid, jnp.zeros_like(high))
                )
                spare = jnp.where(lane == base + 2, low, spare)
                qx_ref[2 * pair + h] = jnp.where(inside[h], q, spare)
            o_ref[:, pair * LANES : (pair + 1) * LANES] = jnp.where(
                inside[0], outs[0], outs[1]
            ).astype(BF16)

    for number in range(rows // BLOCK):
        pl.when(pl.program_id(1) == number)(functools.partial(one_block, number))


def attend(ends, qkv):
    rows, columns = qkv.shape
    pairs = columns // (3 * LANES)
    held = 2
    work = rows * rows // 2 * pairs * 2

    def part(which, height, pair):
        return pl.BlockSpec(
            (height, LANES),
            lambda p, i, e: (i if height == BLOCK else 0, 3 * (p * held + pair) + which),
        )

    return pl.pallas_call(
        attend_kernel,
        grid_spec=pltpu.PrefetchScalarGridSpec(
            num_scalar_prefetch=1,
            grid=(pairs // held, rows // BLOCK),
            in_specs=[
                part(which, BLOCK if which == 0 else rows, pair)
                for which in range(3)
                for pair in range(held)
            ],
            out_specs=[
                pl.BlockSpec((BLOCK, held * LANES), lambda p, i, e: (i, p)),
                pl.BlockSpec((2 * held, BLOCK, LANES), lambda p, i, e: (p, i, 0)),
            ],
        ),
        out_shape=[
            jax.ShapeDtypeStruct((rows, pairs * LANES), BF16),
            jax.ShapeDtypeStruct((2 * pairs, rows, LANES), BF16),
        ],
        compiler_params=pltpu.CompilerParams(vmem_limit_bytes=VMEM_LIMIT),
        cost_estimate=pl.CostEstimate(
            flops=work * 1024, bytes_accessed=2 * rows * columns, transcendentals=0
        ),
        name="attend",
    )(ends, *([qkv] * (3 * held)))


def attend_back_kernel(
    ends_ref, qx_ref, k_ref, v_ref, g_ref, o_ref, cos_ref, sin_ref, out_ref,
    gx_ref, dq_ref, dk_ref, dv_ref,
):
    number = pl.program_id(1)
    blocks = pl.num_programs(1)
    rows = qx_ref.shape[1]
    lane = lax.broadcasted_iota(jnp.int32, (BLOCK, LANES), 1)
    inside = [lane < HEAD_DIM, lane >= HEAD_DIM]

    @pl.when(number == 0)
    def _():
        dq_ref[...] = jnp.zeros_like(dq_ref)

        @pl.loop(0, rows // BLOCK)
        def _(j):
            here = pl.ds(pl.multiple_of(j * BLOCK, BLOCK), BLOCK)
            g = g_ref[here, :]
            both = g.astype(F32) * o_ref[here, :].astype(F32)
            for h in range(2):
                minus = -jnp.sum(jnp.where(inside[h], both, 0.0), axis=1, keepdims=True)
                high = minus.astype(BF16)
                rest = minus - high.astype(F32)
                mid = rest.astype(BF16)
                low = (rest - mid.astype(F32)).astype(BF16)
                base = HEAD_DIM * (1 - h)
                spare = jnp.where(
                    lane == base, high, jnp.where(lane == base + 1, mid, jnp.zeros_like(g))
                )
                spare = jnp.where(lane == base + 2, low, spare)
                gx_ref[h, here, :] = jnp.where(inside[h], g, spare)

    k = k_ref[...]
    v = v_ref[...]
    k_one = [jnp.where(inside[h], k, jnp.ones_like(k)) for h in range(2)]
    v_one = [jnp.where(inside[h], v, jnp.ones_like(v)) for h in range(2)]
    k_turned = [jnp.where(inside[h], k, jnp.zeros_like(k)).T for h in range(2)]
    dk_ref[...] = jnp.zeros_like(dk_ref)
    dv_ref[...] = jnp.zeros_like(dv_ref)

    def step(start, masked):
        here = pl.ds(start, BLOCK)
        if masked:
            row = lax.broadcasted_iota(jnp.int32, (1, BLOCK), 1) + start
            col = lax.broadcasted_iota(jnp.int32, (BLOCK, 1), 0) + start
            visible = (col <= row) & (segment_of(row, ends_ref) == segment_of(col, ends_ref))
        total = None
        for h in range(2):
            qx = qx_ref[h, here, :]
            gx = gx_ref[h, here, :]
            chances = jnp.exp(dot_last(k_one[h], qx))
            if masked:
                chances = jnp.where(visible, chances, 0.0)
            dv_ref[h] += dot(chances.astype(BF16), gx)
            grad_scores = (chances * dot_last(v_one[h], gx)).astype(BF16)
            dk_ref[h] += dot(grad_scores, qx)
            part = dot(k_turned[h], grad_scores)
            total = part if total is None else total + part
        dq_ref[:, here] += total

    step(pl.multiple_of(number * BLOCK, BLOCK), True)

    @pl.loop(number + 1, blocks)
    def _(j):
        step(pl.multiple_of(j * BLOCK, BLOCK), False)

    here = pl.ds(pl.multiple_of(number * BLOCK, BLOCK), BLOCK)
    dk = jnp.where(inside[0], dk_ref[0], dk_ref[1])
    dk = turn(dk, cos_ref[here, :], -sin_ref[here, :])
    out_ref[here, LANES : 2 * LANES] = dk.astype(BF16)
    out_ref[here, 2 * LANES :] = jnp.where(inside[0], dv_ref[0], dv_ref[1]).astype(BF16)

    @pl.when(number == blocks - 1)
    def _():
        for j in range(rows // BLOCK):
            here = slice(j * BLOCK, (j + 1) * BLOCK)
            dq = dq_ref[:, here].T * HEAD_DIM ** (-0.5)
            dq = turn(dq, cos_ref[here, :], -sin_ref[here, :])
            out_ref[here, :LANES] = dq.astype(BF16)


def attend_back(ends, qkv, qx, grad, attended, cosine, sine):
    rows, columns = qkv.shape
    pairs = columns // (3 * LANES)
    blocks = rows // BLOCK
    work = rows * rows // 2 * pairs * 2
    return pl.pallas_call(
        attend_back_kernel,
        grid_spec=pltpu.PrefetchScalarGridSpec(
            num_scalar_prefetch=1,
            grid=(pairs, blocks),
            in_specs=[
                pl.BlockSpec((2, rows, LANES), lambda p, i, e: (p, 0, 0)),
                pl.BlockSpec((BLOCK, LANES), lambda p, i, e: (i, 3 * p + 1)),
                pl.BlockSpec((BLOCK, LANES), lambda p, i, e: (i, 3 * p + 2)),
                pl.BlockSpec((rows, LANES), lambda p, i, e: (0, p)),
                pl.BlockSpec((rows, LANES), lambda p, i, e: (0, p)),
                pl.BlockSpec((rows, LANES), lambda p, i, e: (0, 0)),
                pl.BlockSpec((rows, LANES), lambda p, i, e: (0, 0)),
            ],
            out_specs=pl.BlockSpec((rows, 3 * LANES), lambda p, i, e: (0, p)),
            scratch_shapes=[
                pltpu.VMEM((2, rows, LANES), BF16),
                pltpu.VMEM((LANES, rows), F32),
                pltpu.VMEM((2, BLOCK, LANES), F32),
                pltpu.VMEM((2, BLOCK, LANES), F32),
            ],
        ),
        out_shape=jax.ShapeDtypeStruct((rows, columns), BF16),
        compiler_params=pltpu.CompilerParams(vmem_limit_bytes=VMEM_LIMIT),
        cost_estimate=pl.CostEstimate(
            flops=work * 2560, bytes_accessed=2 * rows * columns, transcendentals=0
        ),
        name="attend_back",
    )(ends, qx, qkv, qkv, grad, attended, cosine, sine)


def params():
    return pltpu.CompilerParams(vmem_limit_bytes=VMEM_LIMIT)


def cost(rows, depth, columns):
    return pl.CostEstimate(
        flops=2 * rows * depth * columns,
        bytes_accessed=2 * (rows * depth + depth * columns + rows * columns),
        transcendentals=0,
    )


def chip_matmul(x, weight, order, rows, turned, name):
    depth = x.shape[1]
    columns = weight.shape[0] if turned else weight.shape[1]
    half = rows // 2
    count = order.shape[0]

    def kernel(order_ref, x_ref, w_ref, *outs):
        multiply = dot_last if turned else dot
        made = multiply(x_ref[...], w_ref[...]).astype(BF16)
        for b in range(count):

            @pl.when(pl.program_id(0) // 2 == b)
            def _(b=b):
                outs[b][...] = made

    made = pl.pallas_call(
        kernel,
        grid_spec=pltpu.PrefetchScalarGridSpec(
            num_scalar_prefetch=1,
            grid=(2 * count,),
            in_specs=[
                pl.BlockSpec((half, depth), lambda i, o: (o[i // 2] * 2 + i % 2, 0)),
                pl.BlockSpec(weight.shape, lambda i, o: (0, 0), pipeline_mode=pl.Buffered(1)),
            ],
            out_specs=[
                pl.BlockSpec((half, columns), lambda i, o, b=b: (jnp.clip(i - 2 * b, 0, 1), 0))
                for b in range(count)
            ],
        ),
        out_shape=[jax.ShapeDtypeStruct((rows, columns), BF16)] * count,
        compiler_params=params(),
        cost_estimate=cost(count * rows, depth, columns),
        name=name,
    )(order, x, weight)
    return [(made[2 * i], made[2 * i + 1]) for i in range(count // 2)]


def buffers(steps):
    return pl.Buffered(1 if steps == 1 else 2)


def weight_grad(x, g, name):
    rows, columns = g.shape
    height = x.shape[1]
    tile = 256 if height % 256 == 0 else height
    part = columns if height % 256 == 0 else 512

    def kernel(x_ref, g_ref, out_ref):
        out_ref[...] = dot_first(x_ref[...], g_ref[...]).astype(BF16)

    return pl.pallas_call(
        kernel,
        grid=(height // tile, columns // part),
        in_specs=[
            pl.BlockSpec((rows, tile), lambda i, j: (0, i), pipeline_mode=buffers(height // tile)),
            pl.BlockSpec((rows, part), lambda i, j: (0, j), pipeline_mode=buffers(columns // part)),
        ],
        out_specs=pl.BlockSpec((tile, part), lambda i, j: (i, j)),
        out_shape=jax.ShapeDtypeStruct((height, columns), BF16),
        compiler_params=params(),
        cost_estimate=cost(height, rows, columns),
        name=name,
    )(x, g)


def own_heads(project_in, me, pairs):
    rows, columns = project_in.shape
    every = columns // 3 // LANES

    def kernel(first_ref, in_ref, out_ref):
        out_ref[...] = in_ref[...]

    return pl.pallas_call(
        kernel,
        grid_spec=pltpu.PrefetchScalarGridSpec(
            num_scalar_prefetch=1,
            grid=(3, pairs),
            in_specs=[
                pl.BlockSpec((rows, LANES), lambda part, p, f: (0, part * every + f[0] + p))
            ],
            out_specs=pl.BlockSpec((rows, LANES), lambda part, p, f: (0, 3 * p + part)),
        ),
        out_shape=jax.ShapeDtypeStruct((rows, 3 * pairs * LANES), BF16),
        compiler_params=params(),
        name="own_heads",
    )(jnp.full((1,), me * pairs, jnp.int32), project_in)


def feed(normed, upstream, w_gate_up, w_down):
    count, rows, width = normed.shape
    units = w_down.shape[0]
    half = rows // 2
    total = rows * count

    def kernel(x_ref, *refs):
        ups, refs = refs[:count], refs[count:]
        wgu_ref, wd_ref, product_ref, grads_ref, normed_ref, upstream_ref = refs
        for b in range(count):

            @pl.when(pl.program_id(0) // 2 == b)
            def _(b=b):
                upstream_ref[...] = ups[b][...]

        x = x_ref[0]
        normed_ref[...] = x
        both = dot(x, wgu_ref[...])
        mid = dot_last(upstream_ref[...], wd_ref[...])
        gate = both[:, :units]
        up = both[:, units:]
        sigmoid = 1.0 / (1.0 + jnp.exp(-gate))
        silu = gate * sigmoid
        product_ref[...] = (silu * up).astype(BF16)
        slope = sigmoid * (1.0 + gate * (1.0 - sigmoid))
        grads_ref[:, :units] = (mid * up * slope).astype(BF16)
        grads_ref[:, units:] = (mid * silu).astype(BF16)

    def here(i):
        return (i, 0)

    def block_spec(b):
        return pl.BlockSpec((half, width), lambda i: (jnp.clip(i - 2 * b, 0, 1), 0))

    return pl.pallas_call(
        kernel,
        grid=(2 * count,),
        in_specs=[pl.BlockSpec((1, half, width), lambda i: (i // 2, i % 2, 0))]
        + [block_spec(b) for b in range(count)]
        + [
            pl.BlockSpec(w_gate_up.shape, lambda i: (0, 0), pipeline_mode=pl.Buffered(1)),
            pl.BlockSpec(w_down.shape, lambda i: (0, 0), pipeline_mode=pl.Buffered(1)),
        ],
        out_specs=[
            pl.BlockSpec((half, units), here),
            pl.BlockSpec((half, 2 * units), here),
            pl.BlockSpec((half, width), here),
            pl.BlockSpec((half, width), here),
        ],
        out_shape=[
            jax.ShapeDtypeStruct((total, units), BF16),
            jax.ShapeDtypeStruct((total, 2 * units), BF16),
            jax.ShapeDtypeStruct((total, width), BF16),
            jax.ShapeDtypeStruct((total, width), BF16),
        ],
        compiler_params=params(),
        cost_estimate=cost(total, 3 * width, units),
        name="feed",
    )(normed, *upstream, w_gate_up, w_down)


def near_and_down(grads, w_gate_up, product, upstream, rows):
    columns = grads.shape[1]
    total, units = product.shape
    width = upstream.shape[1]
    half = rows // 2
    tile = 512

    def kernel(g_ref, w_ref, p_ref, up_ref, own_ref, other_ref, out_ref):
        step = pl.program_id(0)

        @pl.when(step < 4)
        def _():
            made = dot_last(g_ref[...], w_ref[...]).astype(BF16)

            @pl.when(step < 2)
            def _():
                own_ref[...] = made

            @pl.when(step >= 2)
            def _():
                other_ref[...] = made

        @pl.when(step >= 4)
        def _():
            out_ref[...] = dot_first(p_ref[...], up_ref[...]).astype(BF16)

    def late(i):
        return jnp.maximum(i - 4, 0)

    return pl.pallas_call(
        kernel,
        grid=(4 + width // tile,),
        in_specs=[
            pl.BlockSpec((half, columns), lambda i: (jnp.minimum(i, 3), 0)),
            pl.BlockSpec(w_gate_up.shape, lambda i: (0, 0), pipeline_mode=pl.Buffered(1)),
            pl.BlockSpec(product.shape, lambda i: (0, 0), pipeline_mode=pl.Buffered(1)),
            pl.BlockSpec((total, tile), lambda i: (0, late(i))),
        ],
        out_specs=[
            pl.BlockSpec((half, width), lambda i: (jnp.minimum(i, 1), 0)),
            pl.BlockSpec((half, width), lambda i: (jnp.clip(i - 2, 0, 1), 0)),
            pl.BlockSpec((units, tile), lambda i: (0, late(i))),
        ],
        out_shape=[
            jax.ShapeDtypeStruct((rows, width), BF16),
            jax.ShapeDtypeStruct((rows, width), BF16),
            jax.ShapeDtypeStruct((units, width), BF16),
        ],
        compiler_params=params(),
        cost_estimate=cost(total + rows, width, columns),
        name="near_and_down",
    )(grads, w_gate_up, product, upstream)


def blocks_matmul(blocks, weight, order):
    rows, depth = blocks[0].shape
    columns = weight.shape[0]
    half = rows // 2
    count = len(blocks)

    def kernel(order_ref, *refs):
        ins, (w_ref, out_ref, copy_ref) = refs[:count], refs[count:]
        for b in range(count):

            @pl.when(pl.program_id(0) // 2 == b)
            def _(b=b):
                copy_ref[...] = ins[b][...]

        out_ref[...] = dot_last(copy_ref[...], w_ref[...]).astype(BF16)

    def block_spec(b):
        return pl.BlockSpec((half, depth), lambda i, o: (jnp.clip(i - 2 * b, 0, 1), 0))

    return pl.pallas_call(
        kernel,
        grid_spec=pltpu.PrefetchScalarGridSpec(
            num_scalar_prefetch=1,
            grid=(2 * count,),
            in_specs=[block_spec(b) for b in range(count)]
            + [pl.BlockSpec(weight.shape, lambda i, o: (0, 0), pipeline_mode=pl.Buffered(1))],
            out_specs=[
                pl.BlockSpec((half, columns), lambda i, o: (o[i // 2] * 2 + i % 2, 0)),
                pl.BlockSpec((half, depth), lambda i, o: (o[i // 2] * 2 + i % 2, 0)),
            ],
        ),
        out_shape=[
            jax.ShapeDtypeStruct((rows * count, columns), BF16),
            jax.ShapeDtypeStruct((rows * count, depth), BF16),
        ],
        compiler_params=params(),
        cost_estimate=cost(rows * count, depth, columns),
        name="grad_attended",
    )(order, *blocks, weight)


def tie(value, *others):
    return lax.optimization_barrier((value, others))[0]


def from_chip(value, chips, ahead):
    size = chips * CORES
    return lax.ppermute(value, "seq", [(i, (i - ahead * CORES) % size) for i in range(size)])


def to_chip(value, chips, ahead):
    return from_chip(value, chips, chips - ahead)


def core_swap(value, chips):
    return lax.ppermute(value, "seq", [(i, i ^ 1) for i in range(chips * CORES)])


def seq_order(chips):
    me = lax.axis_index("seq")
    core, chip = me % CORES, me // CORES
    found = []
    for ahead in range(chips):
        base = (chip + ahead) % chips * CORES
        found += [base + core, base + 1 - core]
    return jnp.stack(found).astype(jnp.int32)


def planes(size):
    return 4 if size % 4 == 0 else 1


def remote(src, dst, send, recv, **where):
    return pltpu.make_async_remote_copy(
        src_ref=src, dst_ref=dst, send_sem=send, recv_sem=recv, device_id=where,
        device_id_type=pl.DeviceIdType.MESH,
    )


def rows_at(ref, index, rows):
    return ref.at[pl.ds(pl.multiple_of(index * rows, rows), rows)]


class Place:
    def __init__(self, seq_size, fsdp_size):
        self.chips = seq_size // CORES
        self.seq_size, self.fsdp_size = seq_size, fsdp_size
        self.deep = planes(fsdp_size)
        self.across = fsdp_size // self.deep
        self.seq = lax.axis_index("seq")
        self.fsdp = lax.axis_index("fsdp")
        self.core, self.chip = self.seq % CORES, self.seq // CORES
        self.z, self.y = self.fsdp // self.across, self.fsdp % self.across

    def along_x(self, k):
        return (self.chip + k) % self.chips * CORES + self.core

    def other(self):
        return self.chip * CORES + 1 - self.core

    def along_z(self, k):
        return (self.z + k) % self.deep * self.across + self.y

    def along_y(self, k):
        return self.z * self.across + (self.y + k) % self.across

    def shard(self, kz, ky):
        return (self.z + kz) % self.deep * self.across + (self.y + ky) % self.across


def greet_device(**where):
    pl.semaphore_signal(
        pltpu.get_barrier_semaphore(),
        inc=1,
        device_id=where,
        device_id_type=pl.DeviceIdType.MESH,
    )


def greet(place, over_fsdp):
    count = place.chips
    for k in range(1, place.chips):
        greet_device(seq=place.along_x(k))
    greet_device(seq=place.other())
    if over_fsdp:
        count += place.fsdp_size - 1
        for k in range(1, place.fsdp_size):
            greet_device(fsdp=(place.fsdp + k) % place.fsdp_size)
    pl.semaphore_wait(pltpu.get_barrier_semaphore(), count)


def greet_all(place):
    for k in range(1, place.seq_size):
        greet_device(seq=(place.seq + k) % place.seq_size)
    for k in range(1, place.fsdp_size):
        greet_device(fsdp=(place.fsdp + k) % place.fsdp_size)
    count = place.seq_size + place.fsdp_size - 2
    pl.semaphore_wait(pltpu.get_barrier_semaphore(), count)


class FsdpGather:
    def __init__(self, place, own, whole, sems):
        self.place, self.own, self.whole = place, own, whole
        self.rows = own.shape[0]
        self.send_z, self.recv_z, self.send_y, self.recv_y = sems

    def slot(self, index):
        return rows_at(self.whole, index, self.rows)

    def z(self, up, d):
        p = self.place
        sign = 1 if up else -1
        slot = self.slot(p.shard(sign * (1 - d), 0))
        index = (0 if up else p.deep) + d
        return remote(
            self.own if d == 1 else slot, slot,
            self.send_z.at[index], self.recv_z.at[index], fsdp=p.along_z(sign),
        )

    def sends(self, up, d):
        z, deep = self.place.z, self.place.deep
        return (z >= d - 1) & (z + 1 < deep) if up else (z + d - 1 < deep) & (z >= 1)

    def gets(self, up, d):
        z, deep = self.place.z, self.place.deep
        return z >= d if up else z + d < deep

    def y(self, kz, ky):
        p = self.place
        slot = self.slot(p.shard(-kz, 0))
        return remote(
            self.own if kz == 0 else slot, slot,
            self.send_y.at[kz, ky], self.recv_y.at[kz, ky], fsdp=p.along_y(ky),
        )

    def start(self):
        for up in (True, False):
            pl.when(self.sends(up, 1))(lambda up=up: self.z(up, 1).start())
        for ky in range(1, self.place.across):
            self.y(0, ky).start()

    def pass_on(self, d):
        deep = self.place.deep
        for up in (True, False):

            @pl.when(self.gets(up, d))
            def _(up=up):
                self.z(up, d).wait_recv()
                for ky in range(1, self.place.across):
                    self.y(d if up else deep - d, ky).start()

            if d + 1 < deep:
                pl.when(self.sends(up, d + 1))(lambda up=up: self.z(up, d + 1).start())

    def finish(self):
        deep, across = self.place.deep, self.place.across
        for kz in range(deep):
            for ky in range(1, across):
                self.y(kz, ky).wait()
        for d in range(1, deep):
            for up in (True, False):
                pl.when(self.sends(up, d))(lambda up=up, d=d: self.z(up, d).wait_send())


def fsdp_sems(place_deep, place_across):
    return [pltpu.SemaphoreType.DMA((2 * place_deep,))] * 2 + [
        pltpu.SemaphoreType.DMA((place_deep, place_across))
    ] * 2


def opening(tokens, in_part, out_slice, vectors, seq_size, fsdp_size):
    rows, width = tokens.shape
    chips = seq_size // CORES
    deep = planes(fsdp_size)
    across = fsdp_size // deep
    dma = pltpu.SemaphoreType.DMA

    def kernel(
        tok_ref, in_ref, out_ref, vec_ref, tok_all, w_in, w_out, vec_all,
        here, x_send, x_recv, c_send, c_recv, v_send, v_recv, *sems,
    ):
        p = Place(seq_size, fsdp_size)
        greet(p, True)

        def tok_slot(index):
            return rows_at(tok_all, index, rows)

        def tok_x(k):
            return remote(
                tok_ref, tok_slot(p.seq), x_send.at[k], x_recv.at[k], seq=p.along_x(k)
            )

        def tok_core(k):
            slot = tok_slot(p.along_x(-k))
            return remote(
                tok_ref if k == 0 else slot, slot, c_send.at[k], c_recv.at[k], seq=p.other()
            )

        def vec(k):
            return remote(
                vec_ref, vec_all.at[p.fsdp], v_send.at[k], v_recv.at[k],
                fsdp=(p.fsdp + k) % fsdp_size,
            )

        into = FsdpGather(p, in_ref, w_in, sems[:4])
        outof = FsdpGather(p, out_ref, w_out, sems[4:])
        own = [
            pltpu.make_async_copy(tok_ref, tok_slot(p.seq), here.at[0]),
            pltpu.make_async_copy(in_ref, into.slot(p.fsdp), here.at[1]),
            pltpu.make_async_copy(vec_ref, vec_all.at[p.fsdp], here.at[2]),
            pltpu.make_async_copy(out_ref, outof.slot(p.fsdp), here.at[3]),
        ]
        for k in range(1, fsdp_size):
            vec(k).start()
        for k in range(1, chips):
            tok_x(k).start()
        into.start()
        tok_core(0).start()
        for copy in own:
            copy.start()
        into.pass_on(1)
        outof.start()
        for d in range(2, deep):
            into.pass_on(d)
            outof.pass_on(d - 1)
        for d in range(max(deep - 1, 1), deep):
            outof.pass_on(d)
        for k in range(1, chips):
            tok_x(k).wait_recv()
            tok_core(k).start()
        into.finish()
        outof.finish()
        for k in range(chips):
            tok_core(k).wait()
        for k in range(1, chips):
            tok_x(k).wait_send()
        for k in range(1, fsdp_size):
            vec(k).wait()
        for copy in own:
            copy.wait()

    any_space = pl.BlockSpec(memory_space=pl.ANY)
    return pl.pallas_call(
        kernel,
        in_specs=[pl.BlockSpec(memory_space=pltpu.VMEM)] * 4,
        out_specs=[any_space] * 4,
        out_shape=[
            jax.ShapeDtypeStruct((rows * seq_size, width), BF16),
            jax.ShapeDtypeStruct((in_part.shape[0] * fsdp_size, in_part.shape[1]), BF16),
            jax.ShapeDtypeStruct((out_slice.shape[0] * fsdp_size, width), BF16),
            jax.ShapeDtypeStruct((fsdp_size,) + vectors.shape, F32),
        ],
        scratch_shapes=[
            dma((4,)), dma((chips,)), dma((chips,)), dma((chips,)), dma((chips,)),
            dma((fsdp_size,)), dma((fsdp_size,)),
        ]
        + fsdp_sems(deep, across) * 2,
        compiler_params=talking(1),
        name="opening",
    )(tokens, in_part, out_slice, vectors)


def talking(collective_id):
    return pltpu.CompilerParams(
        collective_id=collective_id, has_side_effects=True, vmem_limit_bytes=VMEM_LIMIT
    )


CHUNKS = 4


def hidden_rows(parts, residual, gain, bias, seq_size, fsdp_size):
    rows, width = residual.shape
    chips = seq_size // CORES
    part = rows // CHUNKS
    dma = pltpu.SemaphoreType.DMA

    def kernel(*refs):
        own = refs[0 : 2 * chips : 2]
        other = refs[1 : 2 * chips : 2]
        res_ref, gain_ref, bias_ref, hidden_ref, normed_ref = refs[2 * chips : 2 * chips + 5]
        (
            from_core, total, from_x, mine,
            c_send, c_recv, x_send, x_recv, g_send, g_recv, f_send, f_recv, here,
        ) = refs[2 * chips + 5 :]
        p = Place(seq_size, fsdp_size)
        greet(p, False)

        def span(c):
            return pl.ds(c * part, part)

        def to_core(k, c):
            return remote(
                other[k].at[span(c)], from_core.at[k, span(c)],
                c_send.at[k, c], c_recv.at[k, c], seq=p.other(),
            )

        def along(k, c):
            return remote(
                total.at[k - 1, span(c)], from_x.at[k - 1, span(c)],
                x_send.at[k, c], x_recv.at[k, c], seq=p.along_x(k),
            )

        def share(k, c):
            return remote(
                mine.at[span(c)], normed_ref.at[2 * k, span(c)],
                g_send.at[k, c], g_recv.at[k, c], seq=p.along_x(-k),
            )

        def pass_on(k, c):
            return remote(
                mine.at[span(c)] if k == 0 else normed_ref.at[2 * k, span(c)],
                normed_ref.at[2 * k + 1, span(c)],
                f_send.at[k, c], f_recv.at[k, c], seq=p.other(),
            )

        far = range(1, chips)
        for k in [*far, 0]:
            for c in range(CHUNKS):
                to_core(k, c).start()
        for c in range(CHUNKS):
            for k in far:
                to_core(k, c).wait_recv()
                both = own[k][span(c)].astype(F32) + from_core[k, span(c)].astype(F32)
                total[k - 1, span(c)] = both.astype(BF16)
                along(k, c).start()
        for c in range(CHUNKS):
            to_core(0, c).wait_recv()
            rows_here = own[0][span(c)].astype(F32) + from_core[0, span(c)].astype(F32)
            for k in far:
                along(k, c).wait_recv()
                rows_here = rows_here + from_x[k - 1, span(c)].astype(F32)
            rows_here = rows_here + res_ref[span(c)].astype(F32)
            hidden_ref[span(c)] = rows_here
            unit = rows_here - jnp.mean(rows_here, axis=1, keepdims=True)
            unit = unit * lax.rsqrt(jnp.mean(unit * unit, axis=1, keepdims=True) + epsilon)
            mine[span(c)] = (unit * gain_ref[0:1, :] + bias_ref[0:1, :]).astype(BF16)
            for k in far:
                share(k, c).start()
            pass_on(0, c).start()
        keep = pltpu.make_async_copy(mine, normed_ref.at[0], here)
        keep.start()
        for c in range(CHUNKS):
            for k in far:
                share(k, c).wait_recv()
                pass_on(k, c).start()
        for c in range(CHUNKS):
            for k in range(chips):
                to_core(k, c).wait_send()
                pass_on(k, c).wait()
            for k in far:
                along(k, c).wait_send()
                share(k, c).wait_send()
        keep.wait()

    vmem = pl.BlockSpec(memory_space=pltpu.VMEM)
    block = (rows, width)
    several = (max(chips - 1, 1),) + block
    return pl.pallas_call(
        kernel,
        in_specs=[vmem] * (2 * chips + 3),
        out_specs=[vmem, pl.BlockSpec(memory_space=pl.ANY)],
        out_shape=[
            jax.ShapeDtypeStruct(block, F32),
            jax.ShapeDtypeStruct((2 * chips,) + block, BF16),
        ],
        scratch_shapes=[
            pltpu.VMEM((chips,) + block, BF16),
            pltpu.VMEM(several, BF16),
            pltpu.VMEM(several, BF16),
            pltpu.VMEM(block, BF16),
        ]
        + [dma((chips, CHUNKS))] * 8
        + [dma],
        compiler_params=talking(2),
        name="hidden_rows",
    )(
        *[value for pair in parts for value in pair],
        residual,
        jnp.broadcast_to(gain[None], (8, width)),
        jnp.broadcast_to(bias[None], (8, width)),
    )


def closing_rows(parts, arriving, base, prior, gain, seq_size, fsdp_size, low, collective_id):
    rows, width = base.shape
    chips = seq_size // CORES
    held = len(parts)
    part = rows // CHUNKS
    dma = pltpu.SemaphoreType.DMA
    far = range(1, held)

    def kernel(*refs):
        own, other = refs[0 : 2 * held : 2], refs[1 : 2 * held : 2]
        refs = refs[2 * held :]
        came, refs = refs[: len(arriving)], refs[len(arriving) :]
        base_ref, prior_ref, gain_ref, grad_ref = refs[:4]
        refs = refs[4:]
        if low:
            low_ref, refs = refs[0], refs[1:]
        sums_ref, from_core, total, from_x, c_send, c_recv, x_send, x_recv = refs
        p = Place(seq_size, fsdp_size)
        greet(p, False)

        def span(c):
            return pl.ds(c * part, part)

        def to_core(k, c):
            return remote(
                other[k].at[span(c)], from_core.at[k, span(c)],
                c_send.at[k, c], c_recv.at[k, c], seq=p.other(),
            )

        def along(k, c):
            return remote(
                total.at[k - 1, span(c)], from_x.at[k - 1, span(c)],
                x_send.at[k, c], x_recv.at[k, c], seq=p.along_x(k),
            )

        for k in [*far, 0]:
            for c in range(CHUNKS):
                to_core(k, c).start()
        for c in range(CHUNKS):
            for k in far:
                to_core(k, c).wait_recv()
                both = own[k][span(c)].astype(F32) + from_core[k, span(c)].astype(F32)
                total[k - 1, span(c)] = both.astype(BF16)
                along(k, c).start()
        gained = jnp.zeros((1, width), F32)
        biased = jnp.zeros((1, width), F32)
        for c in range(CHUNKS):
            to_core(0, c).wait_recv()
            gradient = own[0][span(c)].astype(F32) + from_core[0, span(c)].astype(F32)
            for k in far:
                along(k, c).wait_recv()
                gradient = gradient + from_x[k - 1, span(c)].astype(F32)
            for ref in came:
                gradient = gradient + ref[span(c)].astype(F32)
            unit = base_ref[span(c)].astype(F32)
            unit = unit - jnp.mean(unit, axis=1, keepdims=True)
            inverse = lax.rsqrt(jnp.mean(unit * unit, axis=1, keepdims=True) + epsilon)
            unit = unit * inverse
            gained = gained + jnp.sum(gradient * unit, axis=0, keepdims=True)
            biased = biased + jnp.sum(gradient, axis=0, keepdims=True)
            scaled = gradient * gain_ref[0:1, :]
            middle = jnp.mean(scaled, axis=1, keepdims=True)
            tilt = jnp.mean(scaled * unit, axis=1, keepdims=True)
            result = prior_ref[span(c)].astype(F32) + inverse * (scaled - middle - unit * tilt)
            grad_ref[span(c)] = result
            if low:
                low_ref[span(c)] = result.astype(BF16)
        which = lax.broadcasted_iota(jnp.int32, (8, width), 0)
        sums_ref[...] = jnp.where(which == 0, gained, jnp.where(which == 1, biased, 0.0))
        for c in range(CHUNKS):
            for k in range(held):
                to_core(k, c).wait_send()
            for k in far:
                along(k, c).wait_send()

    vmem = pl.BlockSpec(memory_space=pltpu.VMEM)
    block = (rows, width)
    several = (max(held - 1, 1),) + (block if held > 1 else (8, LANES))
    kinds = [(block, F32)] + ([(block, BF16)] if low else []) + [((8, width), F32)]
    operands = [value for pair in parts for value in pair] + list(arriving)
    operands += [base, prior, jnp.broadcast_to(gain[None], (8, width))]
    return pl.pallas_call(
        kernel,
        in_specs=[vmem] * len(operands),
        out_specs=[vmem] * len(kinds),
        out_shape=[jax.ShapeDtypeStruct(*kind) for kind in kinds],
        scratch_shapes=[
            pltpu.VMEM((held,) + block, BF16),
            pltpu.VMEM(several, BF16),
            pltpu.VMEM(several, BF16),
        ]
        + [dma((held, CHUNKS))] * 4,
        compiler_params=talking(collective_id),
        name="closing_rows",
    )(*operands)


class SeqShare:
    def __init__(self, place, piece, whole, sems, number):
        self.place, self.piece, self.whole = place, piece, whole
        self.x_send, self.x_recv, self.c_send, self.c_recv, self.here = (
            [sem.at[number] for sem in sems]
        )

    def x(self, k):
        p = self.place
        return remote(
            self.piece, self.whole.at[p.seq], self.x_send.at[k], self.x_recv.at[k],
            seq=p.along_x(k),
        )

    def core(self, k):
        p = self.place
        slot = self.whole.at[p.along_x(-k)]
        return remote(
            self.piece if k == 0 else slot, slot, self.c_send.at[k], self.c_recv.at[k],
            seq=p.other(),
        )

    def keep(self):
        return pltpu.make_async_copy(self.piece, self.whole.at[self.place.seq], self.here)

    def start(self):
        for k in range(1, self.place.chips):
            self.x(k).start()
        self.core(0).start()
        self.keep().start()

    def finish(self):
        for k in range(1, self.place.chips):
            self.x(k).wait_recv()
            self.core(k).start()
        for k in range(self.place.chips):
            self.core(k).wait()
        for k in range(1, self.place.chips):
            self.x(k).wait_send()
        self.keep().wait()


def share_sems(chips, count):
    dma = pltpu.SemaphoreType.DMA
    return [dma((count, chips))] * 4 + [dma((count,))]


def share_pieces(pieces, seq_size, fsdp_size, collective_id):
    chips = seq_size // CORES
    count = len(pieces)

    def kernel(*refs):
        ins, outs, sems = refs[:count], refs[count : 2 * count], refs[2 * count :]
        p = Place(seq_size, fsdp_size)
        greet(p, False)
        shares = [SeqShare(p, ins[i], outs[i], sems, i) for i in range(count)]
        for share in shares:
            share.start()
        for share in shares:
            share.finish()

    return pl.pallas_call(
        kernel,
        in_specs=[pl.BlockSpec(memory_space=pltpu.VMEM)] * count,
        out_specs=[pl.BlockSpec(memory_space=pl.ANY)] * count,
        out_shape=[jax.ShapeDtypeStruct((seq_size,) + v.shape, v.dtype) for v in pieces],
        scratch_shapes=share_sems(chips, count),
        compiler_params=talking(collective_id),
        name="share_pieces",
    )(*pieces)


def sum_and_share(partial, vectors, pieces, seq_size, fsdp_size, collective_id):
    chips = seq_size // CORES
    deep = planes(fsdp_size)
    across = fsdp_size // deep
    rows, width = partial.shape[0] // fsdp_size, partial.shape[1]
    lanes = vectors.shape[1] // fsdp_size
    count = len(pieces) + 1
    dma = pltpu.SemaphoreType.DMA

    def kernel(part_ref, vec_ref, *refs):
        ins, refs = refs[: count - 1], refs[count - 1 :]
        outs, refs = refs[:count], refs[count:]
        (
            vec_out, from_y, over_y, from_z, piece, vec_cut, vec_f, vec_s, vec_sum,
            y_send, y_recv, z_send, z_recv, f_send, f_recv, s_send, s_recv,
        ) = refs[:17]
        sems = refs[17:]
        p = Place(seq_size, fsdp_size)
        greet_all(p)

        def block(z, y):
            return pl.ds(pl.multiple_of((z * across + y) * rows, rows), rows)

        def to_y(z, k):
            return remote(
                part_ref.at[block(z, (p.y + k) % across)], from_y.at[k, z],
                y_send.at[k, z], y_recv.at[k, z], fsdp=p.along_y(k),
            )

        def to_z(k):
            return remote(
                over_y.at[(p.z + k) % deep], from_z.at[k],
                z_send.at[k], z_recv.at[k], fsdp=p.along_z(k),
            )

        def vec_to(k):
            return remote(
                vec_cut.at[(p.fsdp + k) % fsdp_size], vec_f.at[k],
                f_send.at[k], f_recv.at[k], fsdp=(p.fsdp + k) % fsdp_size,
            )

        def vec_over(k):
            return remote(
                vec_sum, vec_s.at[k], s_send.at[k], s_recv.at[k], seq=(p.seq + k) % seq_size
            )

        for f in range(fsdp_size):
            vec_cut[f] = vec_ref[:, f * lanes : (f + 1) * lanes]
        for k in range(1, fsdp_size):
            vec_to(k).start()
        for z in range(deep):
            for k in range(1, across):
                to_y(z, k).start()
        shares = [SeqShare(p, ins[i], outs[i], sems, i) for i in range(count - 1)]
        for share in shares:
            share.start()
        for z in range(deep):
            total = part_ref[block(z, p.y)].astype(F32)
            for k in range(1, across):
                to_y(z, k).wait_recv()
                total = total + from_y[k, z].astype(F32)
            over_y[z] = total.astype(BF16)
        for k in range(1, deep):
            to_z(k).start()
        vec_total = vec_cut[p.fsdp]
        for k in range(1, fsdp_size):
            vec_to(k).wait_recv()
            vec_total = vec_total + vec_f[k]
        vec_sum[...] = vec_total
        for k in range(1, seq_size):
            vec_over(k).start()
        total = over_y[p.z].astype(F32)
        for k in range(1, deep):
            to_z(k).wait_recv()
            total = total + from_z[k].astype(F32)
        piece[...] = total.astype(BF16)
        shares.append(SeqShare(p, piece, outs[-1], sems, count - 1))
        shares[-1].start()
        for k in range(1, seq_size):
            vec_over(k).wait_recv()
            vec_total = vec_total + vec_s[k]
        vec_out[...] = vec_total
        for share in shares:
            share.finish()
        for z in range(deep):
            for k in range(1, across):
                to_y(z, k).wait_send()
        for k in range(1, deep):
            to_z(k).wait_send()
        for k in range(1, fsdp_size):
            vec_to(k).wait_send()
        for k in range(1, seq_size):
            vec_over(k).wait_send()

    vmem = pl.BlockSpec(memory_space=pltpu.VMEM)
    shapes = [v.shape for v in pieces] + [(rows, width)]
    cut = (8, lanes)
    return pl.pallas_call(
        kernel,
        in_specs=[vmem] * (count + 1),
        out_specs=[pl.BlockSpec(memory_space=pl.ANY)] * count + [vmem],
        out_shape=[jax.ShapeDtypeStruct((seq_size,) + shape, BF16) for shape in shapes]
        + [jax.ShapeDtypeStruct(cut, F32)],
        scratch_shapes=[
            pltpu.VMEM((across, deep, rows, width), BF16),
            pltpu.VMEM((deep, rows, width), BF16),
            pltpu.VMEM((deep, rows, width), BF16),
            pltpu.VMEM((rows, width), BF16),
            pltpu.VMEM((fsdp_size,) + cut, F32),
            pltpu.VMEM((fsdp_size,) + cut, F32),
            pltpu.VMEM((seq_size,) + cut, F32),
            pltpu.VMEM(cut, F32),
        ]
        + [dma((across, deep))] * 2
        + [dma((deep,))] * 2
        + [dma((fsdp_size,))] * 2
        + [dma((seq_size,))] * 2
        + share_sems(chips, count),
        compiler_params=talking(collective_id),
        name="sum_and_share",
    )(partial, vectors, *pieces)


def own_columns(gate, up, me, seq_size, fsdp_size):
    rows, columns = gate.shape
    shard = columns // fsdp_size
    chunk = shard // seq_size

    def kernel(me_ref, gate_ref, up_ref, out_ref):
        for s in range(seq_size):

            @pl.when(me_ref[0] == s)
            def _(s=s):
                for which, ref in enumerate((gate_ref, up_ref)):
                    taken = [
                        ref[:, f * shard + s * chunk : f * shard + (s + 1) * chunk]
                        for f in range(fsdp_size)
                    ]
                    at = which * chunk * fsdp_size
                    out_ref[:, at : at + chunk * fsdp_size] = jnp.concatenate(taken, axis=1)

    return pl.pallas_call(
        kernel,
        grid_spec=pltpu.PrefetchScalarGridSpec(
            num_scalar_prefetch=1,
            grid=(1,),
            in_specs=[pl.BlockSpec((rows, columns), lambda i, m: (0, 0))] * 2,
            out_specs=pl.BlockSpec((rows, 2 * chunk * fsdp_size), lambda i, m: (0, 0)),
        ),
        out_shape=jax.ShapeDtypeStruct((rows, 2 * chunk * fsdp_size), BF16),
        compiler_params=params(),
        cost_estimate=cost(rows, 1, 2 * columns),
        name="own_columns",
    )(jnp.full((1,), me, jnp.int32), gate, up)


def whole_columns(pieces, fsdp_size):
    seq_size, rows, columns = pieces.shape
    units = columns // 2
    chunk = units // fsdp_size

    def kernel(in_ref, gate_ref, up_ref):
        for which, ref in enumerate((gate_ref, up_ref)):
            for f in range(fsdp_size):
                at = which * units + f * chunk
                taken = [in_ref[s, :, at : at + chunk].astype(F32) for s in range(seq_size)]
                whole = jnp.concatenate(taken, axis=1)
                ref[:, f * chunk * seq_size : (f + 1) * chunk * seq_size] = whole

    tile = rows // 4
    out = pl.BlockSpec((tile, units * seq_size), lambda i: (i, 0))
    return pl.pallas_call(
        kernel,
        grid=(4,),
        in_specs=[pl.BlockSpec((seq_size, tile, columns), lambda i: (0, i, 0))],
        out_specs=[out, out],
        out_shape=[jax.ShapeDtypeStruct((rows, units * seq_size), F32)] * 2,
        compiler_params=params(),
        cost_estimate=cost(rows, 1, 2 * columns * seq_size),
        name="whole_columns",
    )(pieces)


def own_heads_spread(project_in, me, pairs, seq_size):
    rows, columns = project_in.shape
    every = columns // 3 // LANES
    step = seq_size // 2

    def kernel(me_ref, low_ref, high_ref, out_ref):
        lane = lax.broadcasted_iota(jnp.int32, (rows, LANES), 1)
        odd = me_ref[0] % 2 == 1
        first = low_ref[...].astype(F32)
        second = high_ref[...].astype(F32)
        first = jnp.where(odd, pltpu.roll(first, HEAD_DIM, 1), first)
        second = jnp.where(odd, second, pltpu.roll(second, HEAD_DIM, 1))
        out_ref[...] = jnp.where(lane < HEAD_DIM, first, second).astype(BF16)

    def source(ahead):
        return pl.BlockSpec(
            (rows, LANES),
            lambda part, p, m: (0, part * every + (2 * p + ahead) * step + m[0] // 2),
        )

    return pl.pallas_call(
        kernel,
        grid_spec=pltpu.PrefetchScalarGridSpec(
            num_scalar_prefetch=1,
            grid=(3, pairs),
            in_specs=[source(0), source(1)],
            out_specs=pl.BlockSpec((rows, LANES), lambda part, p, m: (0, 3 * p + part)),
        ),
        out_shape=jax.ShapeDtypeStruct((rows, 3 * pairs * LANES), BF16),
        compiler_params=params(),
        name="own_heads",
    )(jnp.full((1,), me, jnp.int32), project_in, project_in)


def whole_heads_spread(pieces):
    seq_size, rows, columns = pieces.shape
    each = columns * seq_size // 3
    step = seq_size // 2

    def kernel(in_ref, out_ref):
        lane = lax.broadcasted_iota(jnp.int32, (rows // 4, LANES), 1)
        for part in range(3):
            for b in range(each // LANES):
                shard, seq = b // step, 2 * (b % step)
                at = (3 * (shard // 2) + part) * LANES
                first = in_ref[seq, :, at : at + LANES].astype(F32)
                second = in_ref[seq + 1, :, at : at + LANES].astype(F32)
                if shard % 2:
                    first = pltpu.roll(first, HEAD_DIM, 1)
                else:
                    second = pltpu.roll(second, HEAD_DIM, 1)
                start = part * each + b * LANES
                out_ref[:, start : start + LANES] = jnp.where(lane < HEAD_DIM, first, second)

    return pl.pallas_call(
        kernel,
        grid=(4,),
        in_specs=[pl.BlockSpec((seq_size, rows // 4, columns), lambda i: (0, i, 0))],
        out_specs=pl.BlockSpec((rows // 4, 3 * each), lambda i: (i, 0)),
        out_shape=jax.ShapeDtypeStruct((rows, 3 * each), F32),
        compiler_params=params(),
        cost_estimate=cost(rows, 1, 3 * each),
        name="whole_heads",
    )(pieces)


def gather_fsdp(value):
    return lax.all_gather(value, "fsdp", axis=0, tiled=True)


def scatter_fsdp(value):
    return lax.psum_scatter(value, "fsdp", scatter_dimension=0, tiled=True)


def local(
    tokens,
    cont_lengths,
    project_in,
    project_out,
    gate_weight,
    up_weight,
    down_weight,
    first_gain,
    first_bias,
    second_gain,
    second_bias,
    grad_output,
):
    rows_dev, width = tokens.shape[1:]
    seq_size = lax.axis_size("seq")
    fsdp_size = lax.axis_size("fsdp")
    chips = seq_size // CORES
    total_rows = rows_dev * seq_size
    me = lax.axis_index("seq")
    order = seq_order(chips)
    shard_rows = project_in.shape[0]
    own_pairs = width // LANES // seq_size
    pieces_out = project_out.shape[0] // seq_size
    pieces_down = down_weight.shape[0] // seq_size
    far = range(1, chips)

    spread = pieces_out == HEAD_DIM
    if spread:
        in_part = own_heads_spread(project_in, me, own_pairs, seq_size)
    else:
        in_part = own_heads(project_in, me, own_pairs)
    vectors = jnp.stack([first_gain, first_bias, second_gain, second_bias]).astype(F32)
    all_tokens, w_in, w_out, vectors = opening(
        tokens[0],
        in_part,
        lax.dynamic_slice_in_dim(project_out, me * pieces_out, pieces_out, 0),
        jnp.concatenate([vectors, vectors]),
        seq_size,
        fsdp_size,
    )
    if not spread:
        own_rows = width // seq_size
        w_out = lax.dynamic_slice_in_dim(gather_fsdp(project_out), me * own_rows, own_rows, 0)
    vectors = jnp.transpose(vectors[:, :4], (1, 0, 2)).reshape(4, width)
    gain_one, bias_one, gain_two, bias_two = [vectors[i] for i in range(4)]
    upstream_own = tie(grad_output[0], all_tokens)
    upstream_far = [from_chip(upstream_own, chips, ahead) for ahead in far]
    gate_late, up_late, down_late = tie((gate_weight, up_weight, down_weight), w_in)
    w_down = gather_fsdp(lax.dynamic_slice_in_dim(down_late, me * pieces_down, pieces_down, 0))
    w_gate_up = gather_fsdp(own_columns(gate_late, up_late, me, seq_size, fsdp_size))

    cosine, sine, ends = rope_tables(cont_lengths[0], total_rows)

    qkv, normed_first = project(all_tokens, w_in, gain_one, bias_one, cosine, sine)
    attended, qx = attend(ends, qkv)
    upstream_blocks = [grad_output[0], core_swap(grad_output[0], chips)]
    for block in upstream_far:
        block = tie(block, attended)
        upstream_blocks += [block, core_swap(block, chips)]

    def scatter_end(started):
        arriving, own, other, _ = started
        total = own.astype(F32) + other.astype(F32)
        for part in arriving:
            total = total + part.astype(F32)
        return total

    attended = tie(attended, upstream_blocks)
    parts = chip_matmul(attended, w_out, order, rows_dev, False, "attention_out")
    hidden, normed_blocks = hidden_rows(parts, tokens[0], gain_two, bias_two, seq_size, fsdp_size)
    product, grads, normed_second, upstream_all = feed(
        normed_blocks, upstream_blocks, w_gate_up, w_down
    )

    far_order = jnp.arange(CORES, chips * CORES, dtype=jnp.int32)
    sent = [
        (own.astype(F32) + core_swap(other, chips).astype(F32)).astype(BF16)
        for own, other in chip_matmul(grads, w_gate_up, far_order, rows_dev, True, "feed_back")
    ]
    arriving = [to_chip(value, chips, ahead) for value, ahead in zip(sent, far)]
    own, other, grad_down = near_and_down(
        tie(grads, *sent), w_gate_up, product, upstream_all, rows_dev
    )
    grad_hidden, low_own, sums_two = closing_rows(
        [(own, other)], tie(arriving, grad_down), hidden, grad_output[0], gain_two,
        seq_size, fsdp_size, True, 3,
    )
    low_far = [from_chip(low_own, chips, ahead) for ahead in far]
    low_near = [low_own, core_swap(low_own, chips)]

    normed_late, product_late = tie((normed_second, product), low_own)
    grad_gate_up = weight_grad(normed_late, grads, "grad_gate_up")
    product_late = tie(product_late, grad_gate_up)

    near_order = jnp.arange(chips * CORES, dtype=jnp.int32)
    layer_parts = chip_matmul(product_late, w_down, near_order, rows_dev, False, "feed_down")
    (layer_own, layer_other), layer_far = layer_parts[0], layer_parts[1:]
    low_far = tie(low_far, layer_own)
    layer_far = tie(layer_far, low_far)
    grad_down_piece = scatter_fsdp(tie(grad_down, low_own))
    grad_gate_up_piece = scatter_fsdp(tie(grad_gate_up, low_far))
    low_blocks = low_near
    for block in low_far:
        low_blocks = low_blocks + [block, core_swap(block, chips)]
    layer_sent = [
        (own.astype(F32) + core_swap(other, chips).astype(F32)).astype(BF16)
        for own, other in layer_far
    ]
    layer_arriving = [to_chip(s, chips, ahead) for s, ahead in zip(layer_sent, far)]
    grad_attended, low_hidden = blocks_matmul(tie(low_blocks, layer_sent), w_out, order)
    grad_out = dot_first(attended, low_hidden).astype(BF16)
    grad_attended = tie(grad_attended, grad_out)

    grad_qkv = attend_back(ends, qkv, qx, grad_attended, attended, cosine, sine)
    grad_in = weight_grad(normed_first, grad_qkv, "grad_project_in")
    grad_in_piece = scatter_fsdp(grad_in)
    grad_late = tie(grad_qkv, grad_in)
    parts = chip_matmul(grad_late, w_in, order, rows_dev, True, "project_back")
    input_gradient, sums_one = closing_rows(
        parts, [], tokens[0], grad_hidden, gain_one, seq_size, fsdp_size, False, 4
    )
    layer_rows = hidden + scatter_end(
        (layer_arriving, layer_own, core_swap(layer_other, chips), None)
    )

    sums = jnp.concatenate([sums_one[:2], sums_two[:2], sums_one[2:6]])
    all_gate_up, all_down, all_out, sums = sum_and_share(
        grad_out, sums, [grad_gate_up_piece, grad_down_piece], seq_size, fsdp_size, 5
    )
    (all_in,) = share_pieces([tie(grad_in_piece, all_out)], seq_size, fsdp_size, 6)
    if spread:
        grad_in = whole_heads_spread(all_in)
        grad_out = all_out.reshape(project_out.shape).astype(F32)
    else:
        grad_in = all_in.reshape(seq_size, shard_rows, own_pairs, 3, LANES)
        grad_in = jnp.transpose(grad_in, (1, 3, 0, 2, 4)).reshape(shard_rows, 3 * width)
        grad_in = grad_in.astype(F32)
        whole = jnp.zeros((width, width), F32)
        whole = lax.dynamic_update_slice_in_dim(
            whole, grad_out.astype(F32), me * (width // seq_size), 0
        )
        grad_out = lax.psum(scatter_fsdp(whole), "seq")
    grad_gate, grad_up = whole_columns(all_gate_up, fsdp_size)
    return (
        layer_rows.astype(BF16)[None],
        input_gradient[None],
        grad_in,
        grad_out,
        grad_gate,
        grad_up,
        all_down.reshape(down_weight.shape).astype(F32),
        sums[0],
        sums[1],
        sums[2],
        sums[3],
    )


def solution(mesh):
    return jax.shard_map(
        local,
        mesh=mesh,
        in_specs=(
            P("fsdp", "seq", None),
            P("fsdp", None),
            P("fsdp", None),
            P("fsdp", None),
            P("fsdp", None),
            P("fsdp", None),
            P("fsdp", None),
            P("fsdp"),
            P("fsdp"),
            P("fsdp"),
            P("fsdp"),
            P("fsdp", "seq", None),
        ),
        out_specs=(
            P("fsdp", "seq", None),
            P("fsdp", "seq", None),
            P("fsdp", None),
            P("fsdp", None),
            P("fsdp", None),
            P("fsdp", None),
            P("fsdp", None),
            P("fsdp"),
            P("fsdp"),
            P("fsdp"),
            P("fsdp"),
        ),
        check_vma=False,
    )
```

```python
import functools

import jax
import jax.numpy as jnp
from jax import lax
from jax.experimental import pallas as pl
from jax.experimental.pallas import tpu as pltpu
from jax.sharding import PartitionSpec as P

HEAD_DIM = 64
ROT = 16
PROMPT = 2048
LANES = 128

epsilon = 1e-05
rope_base = 10000.0

BF16 = jnp.bfloat16
F32 = jnp.float32
CORES = 2
VMEM_LIMIT = 56 * 1024 * 1024


def dot_last(left_side, right_side):
    return lax.dot_general(
        left_side, right_side, (((1,), (1,)), ((), ())), preferred_element_type=F32
    )


def dot_first(left_side, right_side):
    return lax.dot_general(
        left_side, right_side, (((0,), (0,)), ((), ())), preferred_element_type=F32
    )


def dot(left_side, right_side):
    return jnp.dot(left_side, right_side, preferred_element_type=F32)


def cont_ends(lengths):
    count = lengths.shape[0]
    before = jnp.arange(count)[None, :] <= jnp.arange(count)[:, None]
    return jnp.sum(jnp.where(before, lengths[None, :], 0), axis=1)


def rope_tables(lengths, total_rows):
    ends = cont_ends(lengths)
    starts = ends - lengths
    indices = jnp.arange(total_rows, dtype=jnp.int32)
    offset = indices - PROMPT
    inside = (offset[:, None] >= starts[None, :]) & (offset[:, None] < ends[None, :])
    seg_begin = jnp.sum(jnp.where(inside, starts[None, :], 0), axis=1)
    position = jnp.where(indices < PROMPT, indices, PROMPT + offset - seg_begin)
    half = ROT // 2
    within = jnp.arange(LANES, dtype=jnp.int32) % HEAD_DIM
    frequency = rope_base ** (-2.0 * (within % half).astype(F32) / ROT)
    angles = position.astype(F32)[:, None] * frequency[None, :]
    turning = (within < ROT)[None, :]
    sign = jnp.where(within < half, -1.0, 1.0)[None, :]
    cosine = jnp.where(turning, jnp.cos(angles), 1.0)
    sine = jnp.where(turning, sign * jnp.sin(angles), 0.0)
    return cosine, sine, ends


def turn(rows_in, cosine, sine):
    half = ROT // 2
    lane = lax.broadcasted_iota(jnp.int32, rows_in.shape, 1) % HEAD_DIM
    partner = jnp.where(
        lane < half,
        pltpu.roll(rows_in, LANES - half, 1),
        pltpu.roll(rows_in, half, 1),
    )
    return rows_in * cosine + partner * sine


def project_kernel(x_ref, w_ref, gain_ref, bias_ref, cos_ref, sin_ref, out_ref, normed_ref):
    cosine = cos_ref[...]
    sine = sin_ref[...]
    pairs = out_ref.shape[1] // (3 * LANES)
    x = x_ref[...].astype(F32)
    x = x - jnp.mean(x, axis=1, keepdims=True)
    x = x * lax.rsqrt(jnp.mean(x * x, axis=1, keepdims=True) + epsilon)
    x = (x * gain_ref[0:1, :] + bias_ref[0:1, :]).astype(BF16)
    normed_ref[...] = x
    for first in range(0, pairs, 2):
        begin = 3 * LANES * first
        mixed = dot(x, w_ref[:, begin : begin + 6 * LANES])
        for pair in range(2):
            base = 3 * LANES * pair
            query = turn(mixed[:, base : base + LANES], cosine, sine) * HEAD_DIM ** (-0.5)
            key = turn(mixed[:, base + LANES : base + 2 * LANES], cosine, sine)
            value = mixed[:, base + 2 * LANES : base + 3 * LANES]
            base = base + begin
            out_ref[:, base : base + LANES] = query.astype(BF16)
            out_ref[:, base + LANES : base + 2 * LANES] = key.astype(BF16)
            out_ref[:, base + 2 * LANES : base + 3 * LANES] = value.astype(BF16)


def project(x, weight, gain, bias, cosine, sine):
    rows, depth = x.shape
    columns = weight.shape[1]
    block = 512
    vector = pl.BlockSpec((8, depth), lambda i: (0, 0))
    return pl.pallas_call(
        project_kernel,
        grid=(rows // block,),
        in_specs=[
            pl.BlockSpec((block, depth), lambda i: (i, 0)),
            pl.BlockSpec((depth, columns), lambda i: (0, 0), pipeline_mode=pl.Buffered(1)),
            vector,
            vector,
            pl.BlockSpec((block, LANES), lambda i: (i, 0)),
            pl.BlockSpec((block, LANES), lambda i: (i, 0)),
        ],
        out_specs=[
            pl.BlockSpec((block, columns), lambda i: (i, 0)),
            pl.BlockSpec((block, depth), lambda i: (i, 0)),
        ],
        out_shape=[
            jax.ShapeDtypeStruct((rows, columns), BF16),
            jax.ShapeDtypeStruct((rows, depth), BF16),
        ],
        compiler_params=pltpu.CompilerParams(vmem_limit_bytes=VMEM_LIMIT),
        cost_estimate=pl.CostEstimate(
            flops=2 * rows * depth * columns,
            bytes_accessed=2 * (rows * depth + depth * columns + rows * columns),
            transcendentals=0,
        ),
        name="project_in_rope",
    )(
        x,
        weight,
        jnp.broadcast_to(gain[None], (8, depth)),
        jnp.broadcast_to(bias[None], (8, depth)),
        cosine,
        sine,
    )


BLOCK = 512
NEG = -1e30


def segment_of(index, ends_ref):
    count = jnp.zeros_like(index)
    for c in range(ends_ref.shape[0] - 1):
        count = count + (index >= PROMPT + ends_ref[c]).astype(jnp.int32)
    return count


def attend_kernel(ends_ref, *refs):
    held = len(refs) // 3
    q_refs, k_refs, v_refs = refs[:held], refs[held : 2 * held], refs[2 * held : 3 * held]
    o_ref, qx_ref = refs[3 * held :]
    rows = k_refs[0].shape[0]
    lane = lax.broadcasted_iota(jnp.int32, (BLOCK, LANES), 1)
    inside = [lane < HEAD_DIM, lane >= HEAD_DIM]

    def one_block(number):
        start = number * BLOCK
        end = start + BLOCK
        full = min(start, PROMPT)
        row = lax.broadcasted_iota(jnp.int32, (BLOCK, 1), 0) + start
        col = lax.broadcasted_iota(jnp.int32, (1, end - full), 1) + full
        visible = col <= row
        if end > PROMPT:
            visible = visible & (segment_of(row, ends_ref) == segment_of(col, ends_ref))
        for pair in range(held):
            q = q_refs[pair][...]
            outs = []
            for h in range(2):
                q_head = jnp.where(inside[h], q, jnp.zeros_like(q))
                v = v_refs[pair][:end, :]
                lane_v = lax.broadcasted_iota(jnp.int32, v.shape, 1)
                own_v = (lane_v < HEAD_DIM) if h == 0 else (lane_v >= HEAD_DIM)
                v_one = jnp.where(own_v, v, jnp.ones_like(v))
                near = dot_last(q_head, k_refs[pair][full:end, :])
                near = jnp.where(visible, near, NEG)
                peak = jnp.max(near, axis=1, keepdims=True)
                if full:
                    early = dot_last(q_head, k_refs[pair][:full, :])
                    peak = jnp.maximum(peak, jnp.max(early, axis=1, keepdims=True))
                acc = dot(jnp.exp(near - peak).astype(BF16), v_one[full:])
                if full:
                    acc = acc + dot(jnp.exp(early - peak).astype(BF16), v_one[:full])
                outs.append(acc / pltpu.roll(acc, HEAD_DIM, 1))
                minus = -(peak + jnp.log(jnp.where(inside[h], 1.0, acc)))
                high = minus.astype(BF16)
                rest = minus - high.astype(F32)
                mid = rest.astype(BF16)
                low = (rest - mid.astype(F32)).astype(BF16)
                base = HEAD_DIM * (1 - h)
                spare = jnp.where(
                    lane == base, high, jnp.where(lane == base + 1, mid, jnp.zeros_like(high))
                )
                spare = jnp.where(lane == base + 2, low, spare)
                qx_ref[2 * pair + h] = jnp.where(inside[h], q, spare)
            o_ref[:, pair * LANES : (pair + 1) * LANES] = jnp.where(
                inside[0], outs[0], outs[1]
            ).astype(BF16)

    for number in range(rows // BLOCK):
        pl.when(pl.program_id(1) == number)(functools.partial(one_block, number))


def attend(ends, qkv):
    rows, columns = qkv.shape
    pairs = columns // (3 * LANES)
    held = 2
    work = rows * rows // 2 * pairs * 2

    def part(which, height, pair):
        return pl.BlockSpec(
            (height, LANES),
            lambda p, i, e: (i if height == BLOCK else 0, 3 * (p * held + pair) + which),
        )

    return pl.pallas_call(
        attend_kernel,
        grid_spec=pltpu.PrefetchScalarGridSpec(
            num_scalar_prefetch=1,
            grid=(pairs // held, rows // BLOCK),
            in_specs=[
                part(which, BLOCK if which == 0 else rows, pair)
                for which in range(3)
                for pair in range(held)
            ],
            out_specs=[
                pl.BlockSpec((BLOCK, held * LANES), lambda p, i, e: (i, p)),
                pl.BlockSpec((2 * held, BLOCK, LANES), lambda p, i, e: (p, i, 0)),
            ],
        ),
        out_shape=[
            jax.ShapeDtypeStruct((rows, pairs * LANES), BF16),
            jax.ShapeDtypeStruct((2 * pairs, rows, LANES), BF16),
        ],
        compiler_params=pltpu.CompilerParams(vmem_limit_bytes=VMEM_LIMIT),
        cost_estimate=pl.CostEstimate(
            flops=work * 1024, bytes_accessed=2 * rows * columns, transcendentals=0
        ),
        name="attend",
    )(ends, *([qkv] * (3 * held)))


def attend_back_kernel(
    ends_ref, qx_ref, k_ref, v_ref, g_ref, o_ref, cos_ref, sin_ref, out_ref,
    gx_ref, dq_ref, dk_ref, dv_ref,
):
    number = pl.program_id(1)
    blocks = pl.num_programs(1)
    rows = qx_ref.shape[1]
    lane = lax.broadcasted_iota(jnp.int32, (BLOCK, LANES), 1)
    inside = [lane < HEAD_DIM, lane >= HEAD_DIM]

    @pl.when(number == 0)
    def _():
        dq_ref[...] = jnp.zeros_like(dq_ref)

        @pl.loop(0, rows // BLOCK)
        def _(j):
            here = pl.ds(pl.multiple_of(j * BLOCK, BLOCK), BLOCK)
            g = g_ref[here, :]
            both = g.astype(F32) * o_ref[here, :].astype(F32)
            for h in range(2):
                minus = -jnp.sum(jnp.where(inside[h], both, 0.0), axis=1, keepdims=True)
                high = minus.astype(BF16)
                rest = minus - high.astype(F32)
                mid = rest.astype(BF16)
                low = (rest - mid.astype(F32)).astype(BF16)
                base = HEAD_DIM * (1 - h)
                spare = jnp.where(
                    lane == base, high, jnp.where(lane == base + 1, mid, jnp.zeros_like(g))
                )
                spare = jnp.where(lane == base + 2, low, spare)
                gx_ref[h, here, :] = jnp.where(inside[h], g, spare)

    k = k_ref[...]
    v = v_ref[...]
    k_one = [jnp.where(inside[h], k, jnp.ones_like(k)) for h in range(2)]
    v_one = [jnp.where(inside[h], v, jnp.ones_like(v)) for h in range(2)]
    k_turned = [jnp.where(inside[h], k, jnp.zeros_like(k)).T for h in range(2)]
    dk_ref[...] = jnp.zeros_like(dk_ref)
    dv_ref[...] = jnp.zeros_like(dv_ref)

    def step(start, masked, keys=(0, BLOCK), size=BLOCK):
        here = pl.ds(start, size)
        first, end = keys
        if masked:
            row = lax.broadcasted_iota(jnp.int32, (1, size), 1) + start
            col = lax.broadcasted_iota(jnp.int32, (end - first, 1), 0) + number * BLOCK + first
            visible = (col <= row) & (segment_of(row, ends_ref) == segment_of(col, ends_ref))
        total = None
        for h in range(2):
            qx = qx_ref[h, here, :]
            gx = gx_ref[h, here, :]
            chances = jnp.exp(dot_last(k_one[h][first:end], qx))
            if masked:
                chances = jnp.where(visible, chances, 0.0)
            dv_ref[h, first:end] += dot(chances.astype(BF16), gx)
            grad_scores = (chances * dot_last(v_one[h][first:end], gx)).astype(BF16)
            dk_ref[h, first:end] += dot(grad_scores, qx)
            part = dot(k_turned[h][:, first:end], grad_scores)
            total = part if total is None else total + part
        dq_ref[:, here] += total

    half = BLOCK // 2
    step(pl.multiple_of(number * BLOCK, BLOCK), True, (0, half))
    step(pl.multiple_of(number * BLOCK + half, half), True, (half, BLOCK), half)

    @pl.loop(number + 1, blocks)
    def _(j):
        step(pl.multiple_of(j * BLOCK, BLOCK), False)

    here = pl.ds(pl.multiple_of(number * BLOCK, BLOCK), BLOCK)
    dk = jnp.where(inside[0], dk_ref[0], dk_ref[1])
    dk = turn(dk, cos_ref[here, :], -sin_ref[here, :])
    out_ref[here, LANES : 2 * LANES] = dk.astype(BF16)
    out_ref[here, 2 * LANES :] = jnp.where(inside[0], dv_ref[0], dv_ref[1]).astype(BF16)

    @pl.when(number == blocks - 1)
    def _():
        for j in range(rows // BLOCK):
            here = slice(j * BLOCK, (j + 1) * BLOCK)
            dq = dq_ref[:, here].T * HEAD_DIM ** (-0.5)
            dq = turn(dq, cos_ref[here, :], -sin_ref[here, :])
            out_ref[here, :LANES] = dq.astype(BF16)


def attend_back(ends, qkv, qx, grad, attended, cosine, sine):
    rows, columns = qkv.shape
    pairs = columns // (3 * LANES)
    blocks = rows // BLOCK
    work = rows * rows // 2 * pairs * 2
    return pl.pallas_call(
        attend_back_kernel,
        grid_spec=pltpu.PrefetchScalarGridSpec(
            num_scalar_prefetch=1,
            grid=(pairs, blocks),
            in_specs=[
                pl.BlockSpec((2, rows, LANES), lambda p, i, e: (p, 0, 0)),
                pl.BlockSpec((BLOCK, LANES), lambda p, i, e: (i, 3 * p + 1)),
                pl.BlockSpec((BLOCK, LANES), lambda p, i, e: (i, 3 * p + 2)),
                pl.BlockSpec((rows, LANES), lambda p, i, e: (0, p)),
                pl.BlockSpec((rows, LANES), lambda p, i, e: (0, p)),
                pl.BlockSpec((rows, LANES), lambda p, i, e: (0, 0)),
                pl.BlockSpec((rows, LANES), lambda p, i, e: (0, 0)),
            ],
            out_specs=pl.BlockSpec((rows, 3 * LANES), lambda p, i, e: (0, p)),
            scratch_shapes=[
                pltpu.VMEM((2, rows, LANES), BF16),
                pltpu.VMEM((LANES, rows), F32),
                pltpu.VMEM((2, BLOCK, LANES), F32),
                pltpu.VMEM((2, BLOCK, LANES), F32),
            ],
        ),
        out_shape=jax.ShapeDtypeStruct((rows, columns), BF16),
        compiler_params=pltpu.CompilerParams(vmem_limit_bytes=VMEM_LIMIT),
        cost_estimate=pl.CostEstimate(
            flops=work * 2560, bytes_accessed=2 * rows * columns, transcendentals=0
        ),
        name="attend_back",
    )(ends, qx, qkv, qkv, grad, attended, cosine, sine)


def params():
    return pltpu.CompilerParams(vmem_limit_bytes=VMEM_LIMIT)


def cost(rows, depth, columns):
    return pl.CostEstimate(
        flops=2 * rows * depth * columns,
        bytes_accessed=2 * (rows * depth + depth * columns + rows * columns),
        transcendentals=0,
    )


def chip_matmul(x, weight, order, rows, turned, name):
    depth = x.shape[1]
    columns = weight.shape[0] if turned else weight.shape[1]
    half = rows // 2
    count = order.shape[0]

    def kernel(order_ref, x_ref, w_ref, *outs):
        multiply = dot_last if turned else dot
        made = multiply(x_ref[...], w_ref[...]).astype(BF16)
        for b in range(count):

            @pl.when(pl.program_id(0) // 2 == b)
            def _(b=b):
                outs[b][...] = made

    made = pl.pallas_call(
        kernel,
        grid_spec=pltpu.PrefetchScalarGridSpec(
            num_scalar_prefetch=1,
            grid=(2 * count,),
            in_specs=[
                pl.BlockSpec((half, depth), lambda i, o: (o[i // 2] * 2 + i % 2, 0)),
                pl.BlockSpec(weight.shape, lambda i, o: (0, 0), pipeline_mode=pl.Buffered(1)),
            ],
            out_specs=[
                pl.BlockSpec((half, columns), lambda i, o, b=b: (jnp.clip(i - 2 * b, 0, 1), 0))
                for b in range(count)
            ],
        ),
        out_shape=[jax.ShapeDtypeStruct((rows, columns), BF16)] * count,
        compiler_params=params(),
        cost_estimate=cost(count * rows, depth, columns),
        name=name,
    )(order, x, weight)
    return [(made[2 * i], made[2 * i + 1]) for i in range(count // 2)]


def buffers(steps):
    return pl.Buffered(1 if steps == 1 else 2)


def weight_grad(x, g, name):
    rows, columns = g.shape
    height = x.shape[1]
    tile = 256 if height % 256 == 0 else height
    part = columns if height % 256 == 0 else 512

    def kernel(x_ref, g_ref, out_ref):
        out_ref[...] = dot_first(x_ref[...], g_ref[...]).astype(BF16)

    return pl.pallas_call(
        kernel,
        grid=(height // tile, columns // part),
        in_specs=[
            pl.BlockSpec((rows, tile), lambda i, j: (0, i), pipeline_mode=buffers(height // tile)),
            pl.BlockSpec((rows, part), lambda i, j: (0, j), pipeline_mode=buffers(columns // part)),
        ],
        out_specs=pl.BlockSpec((tile, part), lambda i, j: (i, j)),
        out_shape=jax.ShapeDtypeStruct((height, columns), BF16),
        compiler_params=params(),
        cost_estimate=cost(height, rows, columns),
        name=name,
    )(x, g)


def own_heads(project_in, me, pairs):
    rows, columns = project_in.shape
    every = columns // 3 // LANES

    def kernel(first_ref, in_ref, out_ref):
        out_ref[...] = in_ref[...]

    return pl.pallas_call(
        kernel,
        grid_spec=pltpu.PrefetchScalarGridSpec(
            num_scalar_prefetch=1,
            grid=(3, pairs),
            in_specs=[
                pl.BlockSpec((rows, LANES), lambda part, p, f: (0, part * every + f[0] + p))
            ],
            out_specs=pl.BlockSpec((rows, LANES), lambda part, p, f: (0, 3 * p + part)),
        ),
        out_shape=jax.ShapeDtypeStruct((rows, 3 * pairs * LANES), BF16),
        compiler_params=params(),
        name="own_heads",
    )(jnp.full((1,), me * pairs, jnp.int32), project_in)


def feed(normed, upstream, w_gate_up, w_down):
    count, rows, width = normed.shape
    units = w_down.shape[0]
    half = rows // 2
    total = rows * count

    def kernel(x_ref, *refs):
        ups, refs = refs[:count], refs[count:]
        wgu_ref, wd_ref, product_ref, grads_ref, normed_ref, upstream_ref = refs
        for b in range(count):

            @pl.when(pl.program_id(0) // 2 == b)
            def _(b=b):
                upstream_ref[...] = ups[b][...]

        x = x_ref[0]
        normed_ref[...] = x
        both = dot(x, wgu_ref[...])
        mid = dot_last(upstream_ref[...], wd_ref[...])
        gate = both[:, :units]
        up = both[:, units:]
        sigmoid = 1.0 / (1.0 + jnp.exp(-gate))
        silu = gate * sigmoid
        product_ref[...] = (silu * up).astype(BF16)
        slope = sigmoid * (1.0 + gate * (1.0 - sigmoid))
        grads_ref[:, :units] = (mid * up * slope).astype(BF16)
        grads_ref[:, units:] = (mid * silu).astype(BF16)

    def here(i):
        return (i, 0)

    def block_spec(b):
        return pl.BlockSpec((half, width), lambda i: (jnp.clip(i - 2 * b, 0, 1), 0))

    return pl.pallas_call(
        kernel,
        grid=(2 * count,),
        in_specs=[pl.BlockSpec((1, half, width), lambda i: (i // 2, i % 2, 0))]
        + [block_spec(b) for b in range(count)]
        + [
            pl.BlockSpec(w_gate_up.shape, lambda i: (0, 0), pipeline_mode=pl.Buffered(1)),
            pl.BlockSpec(w_down.shape, lambda i: (0, 0), pipeline_mode=pl.Buffered(1)),
        ],
        out_specs=[
            pl.BlockSpec((half, units), here),
            pl.BlockSpec((half, 2 * units), here),
            pl.BlockSpec((half, width), here),
            pl.BlockSpec((half, width), here),
        ],
        out_shape=[
            jax.ShapeDtypeStruct((total, units), BF16),
            jax.ShapeDtypeStruct((total, 2 * units), BF16),
            jax.ShapeDtypeStruct((total, width), BF16),
            jax.ShapeDtypeStruct((total, width), BF16),
        ],
        compiler_params=params(),
        cost_estimate=cost(total, 3 * width, units),
        name="feed",
    )(normed, *upstream, w_gate_up, w_down)


def near_and_grad(x, weight, order, left, right, rows, name):
    columns = x.shape[1]
    total, height = left.shape
    width = weight.shape[0]
    breadth = right.shape[1]
    half = rows // 2
    tile = 512 if breadth % 512 == 0 else 256

    def kernel(order_ref, x_ref, w_ref, left_ref, right_ref, own_ref, other_ref, out_ref):
        step = pl.program_id(0)

        @pl.when(step < 4)
        def _():
            made = dot_last(x_ref[...], w_ref[...]).astype(BF16)

            @pl.when(step < 2)
            def _():
                own_ref[...] = made

            @pl.when(step >= 2)
            def _():
                other_ref[...] = made

        @pl.when(step >= 4)
        def _():
            out_ref[...] = dot_first(left_ref[...], right_ref[...]).astype(BF16)

    def late(i):
        return jnp.maximum(i - 4, 0)

    def near(i, o):
        step = jnp.minimum(i, 3)
        return (o[step // 2] * 2 + step % 2, 0)

    return pl.pallas_call(
        kernel,
        grid_spec=pltpu.PrefetchScalarGridSpec(
            num_scalar_prefetch=1,
            grid=(4 + breadth // tile,),
            in_specs=[
                pl.BlockSpec((half, columns), near),
                pl.BlockSpec(weight.shape, lambda i, o: (0, 0), pipeline_mode=pl.Buffered(1)),
                pl.BlockSpec(left.shape, lambda i, o: (0, 0), pipeline_mode=pl.Buffered(1)),
                pl.BlockSpec((total, tile), lambda i, o: (0, late(i))),
            ],
            out_specs=[
                pl.BlockSpec((half, width), lambda i, o: (jnp.minimum(i, 1), 0)),
                pl.BlockSpec((half, width), lambda i, o: (jnp.clip(i - 2, 0, 1), 0)),
                pl.BlockSpec((height, tile), lambda i, o: (0, late(i))),
            ],
        ),
        out_shape=[
            jax.ShapeDtypeStruct((rows, width), BF16),
            jax.ShapeDtypeStruct((rows, width), BF16),
            jax.ShapeDtypeStruct((height, breadth), BF16),
        ],
        compiler_params=params(),
        cost_estimate=cost(total + rows, width, columns),
        name=name,
    )(order, x, weight, left, right)


def blocks_matmul(blocks, weight, order):
    rows, depth = blocks[0].shape
    columns = weight.shape[0]
    half = rows // 2
    count = len(blocks)

    def kernel(order_ref, *refs):
        ins, (w_ref, out_ref, copy_ref) = refs[:count], refs[count:]
        for b in range(count):

            @pl.when(pl.program_id(0) // 2 == b)
            def _(b=b):
                copy_ref[...] = ins[b][...]

        out_ref[...] = dot_last(copy_ref[...], w_ref[...]).astype(BF16)

    def block_spec(b):
        return pl.BlockSpec((half, depth), lambda i, o: (jnp.clip(i - 2 * b, 0, 1), 0))

    return pl.pallas_call(
        kernel,
        grid_spec=pltpu.PrefetchScalarGridSpec(
            num_scalar_prefetch=1,
            grid=(2 * count,),
            in_specs=[block_spec(b) for b in range(count)]
            + [pl.BlockSpec(weight.shape, lambda i, o: (0, 0), pipeline_mode=pl.Buffered(1))],
            out_specs=[
                pl.BlockSpec((half, columns), lambda i, o: (o[i // 2] * 2 + i % 2, 0)),
                pl.BlockSpec((half, depth), lambda i, o: (o[i // 2] * 2 + i % 2, 0)),
            ],
        ),
        out_shape=[
            jax.ShapeDtypeStruct((rows * count, columns), BF16),
            jax.ShapeDtypeStruct((rows * count, depth), BF16),
        ],
        compiler_params=params(),
        cost_estimate=cost(rows * count, depth, columns),
        name="grad_attended",
    )(order, *blocks, weight)


def tie(value, *others):
    return lax.optimization_barrier((value, others))[0]


def from_chip(value, chips, ahead):
    size = chips * CORES
    return lax.ppermute(value, "seq", [(i, (i - ahead * CORES) % size) for i in range(size)])


def to_chip(value, chips, ahead):
    return from_chip(value, chips, chips - ahead)


def core_swap(value, chips):
    return lax.ppermute(value, "seq", [(i, i ^ 1) for i in range(chips * CORES)])


def seq_order(chips):
    me = lax.axis_index("seq")
    core, chip = me % CORES, me // CORES
    found = []
    for ahead in range(chips):
        base = (chip + ahead) % chips * CORES
        found += [base + core, base + 1 - core]
    return jnp.stack(found).astype(jnp.int32)


def planes(size):
    return 4 if size % 4 == 0 else 1


def remote(src, dst, send, recv, **where):
    return pltpu.make_async_remote_copy(
        src_ref=src, dst_ref=dst, send_sem=send, recv_sem=recv, device_id=where,
        device_id_type=pl.DeviceIdType.MESH,
    )


def rows_at(ref, index, rows):
    return ref.at[pl.ds(pl.multiple_of(index * rows, rows), rows)]


class Place:
    def __init__(self, seq_size, fsdp_size):
        self.chips = seq_size // CORES
        self.seq_size, self.fsdp_size = seq_size, fsdp_size
        self.deep = planes(fsdp_size)
        self.across = fsdp_size // self.deep
        self.seq = lax.axis_index("seq")
        self.fsdp = lax.axis_index("fsdp")
        self.core, self.chip = self.seq % CORES, self.seq // CORES
        self.z, self.y = self.fsdp // self.across, self.fsdp % self.across

    def along_x(self, k):
        return (self.chip + k) % self.chips * CORES + self.core

    def other(self):
        return self.chip * CORES + 1 - self.core

    def along_z(self, k):
        return (self.z + k) % self.deep * self.across + self.y

    def along_y(self, k):
        return self.z * self.across + (self.y + k) % self.across

    def shard(self, kz, ky):
        return (self.z + kz) % self.deep * self.across + (self.y + ky) % self.across


def greet_device(**where):
    pl.semaphore_signal(
        pltpu.get_barrier_semaphore(),
        inc=1,
        device_id=where,
        device_id_type=pl.DeviceIdType.MESH,
    )


def greet(place, over_fsdp):
    count = place.chips
    for k in range(1, place.chips):
        greet_device(seq=place.along_x(k))
    greet_device(seq=place.other())
    if over_fsdp:
        count += place.fsdp_size - 1
        for k in range(1, place.fsdp_size):
            greet_device(fsdp=(place.fsdp + k) % place.fsdp_size)
    pl.semaphore_wait(pltpu.get_barrier_semaphore(), count)


def greet_all(place):
    for k in range(1, place.seq_size):
        greet_device(seq=(place.seq + k) % place.seq_size)
    for k in range(1, place.fsdp_size):
        greet_device(fsdp=(place.fsdp + k) % place.fsdp_size)
    count = place.seq_size + place.fsdp_size - 2
    pl.semaphore_wait(pltpu.get_barrier_semaphore(), count)


class FsdpGather:
    def __init__(self, place, own, whole, sems):
        self.place, self.own, self.whole = place, own, whole
        self.rows = own.shape[0]
        self.send_z, self.recv_z, self.send_y, self.recv_y = sems

    def slot(self, index):
        return rows_at(self.whole, index, self.rows)

    def z(self, up, d):
        p = self.place
        sign = 1 if up else -1
        slot = self.slot(p.shard(sign * (1 - d), 0))
        index = (0 if up else p.deep) + d
        return remote(
            self.own if d == 1 else slot, slot,
            self.send_z.at[index], self.recv_z.at[index], fsdp=p.along_z(sign),
        )

    def sends(self, up, d):
        z, deep = self.place.z, self.place.deep
        return (z >= d - 1) & (z + 1 < deep) if up else (z + d - 1 < deep) & (z >= 1)

    def gets(self, up, d):
        z, deep = self.place.z, self.place.deep
        return z >= d if up else z + d < deep

    def y(self, kz, ky):
        p = self.place
        slot = self.slot(p.shard(-kz, 0))
        return remote(
            self.own if kz == 0 else slot, slot,
            self.send_y.at[kz, ky], self.recv_y.at[kz, ky], fsdp=p.along_y(ky),
        )

    def start(self):
        for up in (True, False):
            pl.when(self.sends(up, 1))(lambda up=up: self.z(up, 1).start())
        for ky in range(1, self.place.across):
            self.y(0, ky).start()

    def pass_on(self, d):
        deep = self.place.deep
        for up in (True, False):

            @pl.when(self.gets(up, d))
            def _(up=up):
                self.z(up, d).wait_recv()
                for ky in range(1, self.place.across):
                    self.y(d if up else deep - d, ky).start()

            if d + 1 < deep:
                pl.when(self.sends(up, d + 1))(lambda up=up: self.z(up, d + 1).start())

    def finish(self):
        deep, across = self.place.deep, self.place.across
        for kz in range(deep):
            for ky in range(1, across):
                self.y(kz, ky).wait()
        for d in range(1, deep):
            for up in (True, False):
                pl.when(self.sends(up, d))(lambda up=up, d=d: self.z(up, d).wait_send())


def fsdp_sems(place_deep, place_across):
    return [pltpu.SemaphoreType.DMA((2 * place_deep,))] * 2 + [
        pltpu.SemaphoreType.DMA((place_deep, place_across))
    ] * 2


def opening(tokens, in_part, vectors, seq_size, fsdp_size):
    rows, width = tokens.shape
    chips = seq_size // CORES
    deep = planes(fsdp_size)
    across = fsdp_size // deep
    dma = pltpu.SemaphoreType.DMA

    def kernel(
        tok_ref, in_ref, vec_ref, tok_all, w_in, vec_all,
        here, x_send, x_recv, c_send, c_recv, v_send, v_recv, *sems,
    ):
        p = Place(seq_size, fsdp_size)
        greet(p, True)

        def tok_slot(index):
            return rows_at(tok_all, index, rows)

        def tok_x(k):
            return remote(
                tok_ref, tok_slot(p.seq), x_send.at[k], x_recv.at[k], seq=p.along_x(k)
            )

        def tok_core(k):
            slot = tok_slot(p.along_x(-k))
            return remote(
                tok_ref if k == 0 else slot, slot, c_send.at[k], c_recv.at[k], seq=p.other()
            )

        def vec(k):
            return remote(
                vec_ref, vec_all.at[p.fsdp], v_send.at[k], v_recv.at[k],
                fsdp=(p.fsdp + k) % fsdp_size,
            )

        into = FsdpGather(p, in_ref, w_in, sems)
        own = [
            pltpu.make_async_copy(tok_ref, tok_slot(p.seq), here.at[0]),
            pltpu.make_async_copy(in_ref, into.slot(p.fsdp), here.at[1]),
            pltpu.make_async_copy(vec_ref, vec_all.at[p.fsdp], here.at[2]),
        ]
        for k in range(1, fsdp_size):
            vec(k).start()
        for k in range(1, chips):
            tok_x(k).start()
        into.start()
        tok_core(0).start()
        for copy in own:
            copy.start()
        for d in range(1, deep):
            into.pass_on(d)
        for k in range(1, chips):
            tok_x(k).wait_recv()
            tok_core(k).start()
        into.finish()
        for k in range(chips):
            tok_core(k).wait()
        for k in range(1, chips):
            tok_x(k).wait_send()
        for k in range(1, fsdp_size):
            vec(k).wait()
        for copy in own:
            copy.wait()

    any_space = pl.BlockSpec(memory_space=pl.ANY)
    return pl.pallas_call(
        kernel,
        in_specs=[pl.BlockSpec(memory_space=pltpu.VMEM)] * 3,
        out_specs=[any_space] * 3,
        out_shape=[
            jax.ShapeDtypeStruct((rows * seq_size, width), BF16),
            jax.ShapeDtypeStruct((in_part.shape[0] * fsdp_size, in_part.shape[1]), BF16),
            jax.ShapeDtypeStruct((fsdp_size,) + vectors.shape, F32),
        ],
        scratch_shapes=[
            dma((3,)), dma((chips,)), dma((chips,)), dma((chips,)), dma((chips,)),
            dma((fsdp_size,)), dma((fsdp_size,)),
        ]
        + fsdp_sems(deep, across),
        compiler_params=talking(1),
        name="opening",
    )(tokens, in_part, vectors)


def talking(collective_id):
    return pltpu.CompilerParams(
        collective_id=collective_id, has_side_effects=True, vmem_limit_bytes=VMEM_LIMIT
    )


CHUNKS = 4


def hidden_rows(parts, residual, gain, bias, down_slice, seq_size, fsdp_size):
    rows, width = residual.shape
    chips = seq_size // CORES
    deep = planes(fsdp_size)
    part = rows // CHUNKS
    dma = pltpu.SemaphoreType.DMA

    def kernel(*refs):
        own = refs[0 : 2 * chips : 2]
        other = refs[1 : 2 * chips : 2]
        refs = refs[2 * chips :]
        res_ref, gain_ref, bias_ref, down_ref, hidden_ref, normed_ref, w_down = refs[:7]
        (
            from_core, total, from_x, mine,
            c_send, c_recv, x_send, x_recv, g_send, g_recv, f_send, f_recv, here,
        ) = refs[7:20]
        p = Place(seq_size, fsdp_size)
        greet(p, True)
        down = FsdpGather(p, down_ref, w_down, refs[20:])

        def span(c):
            return pl.ds(c * part, part)

        def to_core(k, c):
            return remote(
                other[k].at[span(c)], from_core.at[k, span(c)],
                c_send.at[k, c], c_recv.at[k, c], seq=p.other(),
            )

        def along(k, c):
            return remote(
                total.at[k - 1, span(c)], from_x.at[k - 1, span(c)],
                x_send.at[k, c], x_recv.at[k, c], seq=p.along_x(k),
            )

        def share(k, c):
            return remote(
                mine.at[span(c)], normed_ref.at[2 * k, span(c)],
                g_send.at[k, c], g_recv.at[k, c], seq=p.along_x(-k),
            )

        def pass_on(k, c):
            return remote(
                mine.at[span(c)] if k == 0 else normed_ref.at[2 * k, span(c)],
                normed_ref.at[2 * k + 1, span(c)],
                f_send.at[k, c], f_recv.at[k, c], seq=p.other(),
            )

        far = range(1, chips)
        for k in [*far, 0]:
            for c in range(CHUNKS):
                to_core(k, c).start()
        for c in range(CHUNKS):
            for k in far:
                to_core(k, c).wait_recv()
                both = own[k][span(c)].astype(F32) + from_core[k, span(c)].astype(F32)
                total[k - 1, span(c)] = both.astype(BF16)
                along(k, c).start()
        down.start()
        down_here = pltpu.make_async_copy(down_ref, down.slot(p.fsdp), here.at[1])
        down_here.start()
        for c in range(CHUNKS):
            to_core(0, c).wait_recv()
            rows_here = own[0][span(c)].astype(F32) + from_core[0, span(c)].astype(F32)
            for k in far:
                along(k, c).wait_recv()
                rows_here = rows_here + from_x[k - 1, span(c)].astype(F32)
            rows_here = rows_here + res_ref[span(c)].astype(F32)
            hidden_ref[span(c)] = rows_here
            unit = rows_here - jnp.mean(rows_here, axis=1, keepdims=True)
            unit = unit * lax.rsqrt(jnp.mean(unit * unit, axis=1, keepdims=True) + epsilon)
            mine[span(c)] = (unit * gain_ref[0:1, :] + bias_ref[0:1, :]).astype(BF16)
            for k in far:
                share(k, c).start()
            pass_on(0, c).start()
            if c + 1 < deep:
                down.pass_on(c + 1)
        keep = pltpu.make_async_copy(mine, normed_ref.at[0], here.at[0])
        keep.start()
        for d in range(CHUNKS + 1, deep):
            down.pass_on(d)
        for c in range(CHUNKS):
            for k in far:
                share(k, c).wait_recv()
                pass_on(k, c).start()
        for c in range(CHUNKS):
            for k in range(chips):
                to_core(k, c).wait_send()
                pass_on(k, c).wait()
            for k in far:
                along(k, c).wait_send()
                share(k, c).wait_send()
        keep.wait()
        down.finish()
        down_here.wait()

    vmem = pl.BlockSpec(memory_space=pltpu.VMEM)
    any_space = pl.BlockSpec(memory_space=pl.ANY)
    block = (rows, width)
    several = (max(chips - 1, 1),) + block
    return pl.pallas_call(
        kernel,
        in_specs=[vmem] * (2 * chips + 4),
        out_specs=[vmem, any_space, any_space],
        out_shape=[
            jax.ShapeDtypeStruct(block, F32),
            jax.ShapeDtypeStruct((2 * chips,) + block, BF16),
            jax.ShapeDtypeStruct((down_slice.shape[0] * fsdp_size, width), BF16),
        ],
        scratch_shapes=[
            pltpu.VMEM((chips,) + block, BF16),
            pltpu.VMEM(several, BF16),
            pltpu.VMEM(several, BF16),
            pltpu.VMEM(block, BF16),
        ]
        + [dma((chips, CHUNKS))] * 8
        + [dma((2,))]
        + fsdp_sems(deep, fsdp_size // deep),
        compiler_params=talking(2),
        name="hidden_rows",
    )(
        *[value for pair in parts for value in pair],
        residual,
        jnp.broadcast_to(gain[None], (8, width)),
        jnp.broadcast_to(bias[None], (8, width)),
        down_slice,
    )


def closing_rows(parts, arriving, base, prior, gain, seq_size, fsdp_size, low, collective_id):
    rows, width = base.shape
    chips = seq_size // CORES
    held = len(parts)
    part = rows // CHUNKS
    dma = pltpu.SemaphoreType.DMA
    far = range(1, held)

    def kernel(*refs):
        own, other = refs[0 : 2 * held : 2], refs[1 : 2 * held : 2]
        refs = refs[2 * held :]
        came, refs = refs[: len(arriving)], refs[len(arriving) :]
        base_ref, prior_ref, gain_ref, grad_ref = refs[:4]
        refs = refs[4:]
        if low:
            low_ref, refs = refs[0], refs[1:]
        sums_ref, from_core, total, from_x, c_send, c_recv, x_send, x_recv = refs
        p = Place(seq_size, fsdp_size)
        greet(p, False)

        def span(c):
            return pl.ds(c * part, part)

        def to_core(k, c):
            return remote(
                other[k].at[span(c)], from_core.at[k, span(c)],
                c_send.at[k, c], c_recv.at[k, c], seq=p.other(),
            )

        def along(k, c):
            return remote(
                total.at[k - 1, span(c)], from_x.at[k - 1, span(c)],
                x_send.at[k, c], x_recv.at[k, c], seq=p.along_x(k),
            )

        for k in [*far, 0]:
            for c in range(CHUNKS):
                to_core(k, c).start()
        for c in range(CHUNKS):
            for k in far:
                to_core(k, c).wait_recv()
                both = own[k][span(c)].astype(F32) + from_core[k, span(c)].astype(F32)
                total[k - 1, span(c)] = both.astype(BF16)
                along(k, c).start()
        gained = jnp.zeros((1, width), F32)
        biased = jnp.zeros((1, width), F32)
        for c in range(CHUNKS):
            to_core(0, c).wait_recv()
            gradient = own[0][span(c)].astype(F32) + from_core[0, span(c)].astype(F32)
            for k in far:
                along(k, c).wait_recv()
                gradient = gradient + from_x[k - 1, span(c)].astype(F32)
            for ref in came:
                gradient = gradient + ref[span(c)].astype(F32)
            unit = base_ref[span(c)].astype(F32)
            unit = unit - jnp.mean(unit, axis=1, keepdims=True)
            inverse = lax.rsqrt(jnp.mean(unit * unit, axis=1, keepdims=True) + epsilon)
            unit = unit * inverse
            gained = gained + jnp.sum(gradient * unit, axis=0, keepdims=True)
            biased = biased + jnp.sum(gradient, axis=0, keepdims=True)
            scaled = gradient * gain_ref[0:1, :]
            middle = jnp.mean(scaled, axis=1, keepdims=True)
            tilt = jnp.mean(scaled * unit, axis=1, keepdims=True)
            result = prior_ref[span(c)].astype(F32) + inverse * (scaled - middle - unit * tilt)
            grad_ref[span(c)] = result
            if low:
                low_ref[span(c)] = result.astype(BF16)
        which = lax.broadcasted_iota(jnp.int32, (8, width), 0)
        sums_ref[...] = jnp.where(which == 0, gained, jnp.where(which == 1, biased, 0.0))
        for c in range(CHUNKS):
            for k in range(held):
                to_core(k, c).wait_send()
            for k in far:
                along(k, c).wait_send()

    vmem = pl.BlockSpec(memory_space=pltpu.VMEM)
    block = (rows, width)
    several = (max(held - 1, 1),) + (block if held > 1 else (8, LANES))
    kinds = [(block, F32)] + ([(block, BF16)] if low else []) + [((8, width), F32)]
    operands = [value for pair in parts for value in pair] + list(arriving)
    operands += [base, prior, jnp.broadcast_to(gain[None], (8, width))]
    return pl.pallas_call(
        kernel,
        in_specs=[vmem] * len(operands),
        out_specs=[vmem] * len(kinds),
        out_shape=[jax.ShapeDtypeStruct(*kind) for kind in kinds],
        scratch_shapes=[
            pltpu.VMEM((held,) + block, BF16),
            pltpu.VMEM(several, BF16),
            pltpu.VMEM(several, BF16),
        ]
        + [dma((held, CHUNKS))] * 4,
        compiler_params=talking(collective_id),
        name="closing_rows",
    )(*operands)


class SeqShare:
    def __init__(self, place, piece, whole, sems, number):
        self.place, self.piece, self.whole = place, piece, whole
        self.x_send, self.x_recv, self.c_send, self.c_recv, self.here = (
            [sem.at[number] for sem in sems]
        )

    def x(self, k):
        p = self.place
        return remote(
            self.piece, self.whole.at[p.seq], self.x_send.at[k], self.x_recv.at[k],
            seq=p.along_x(k),
        )

    def core(self, k):
        p = self.place
        slot = self.whole.at[p.along_x(-k)]
        return remote(
            self.piece if k == 0 else slot, slot, self.c_send.at[k], self.c_recv.at[k],
            seq=p.other(),
        )

    def keep(self):
        return pltpu.make_async_copy(self.piece, self.whole.at[self.place.seq], self.here)

    def start(self):
        for k in range(1, self.place.chips):
            self.x(k).start()
        self.core(0).start()
        self.keep().start()

    def finish(self):
        for k in range(1, self.place.chips):
            self.x(k).wait_recv()
            self.core(k).start()
        for k in range(self.place.chips):
            self.core(k).wait()
        for k in range(1, self.place.chips):
            self.x(k).wait_send()
        self.keep().wait()


def share_sems(chips, count):
    dma = pltpu.SemaphoreType.DMA
    return [dma((count, chips))] * 4 + [dma((count,))]


def share_pieces(pieces, seq_size, fsdp_size, collective_id):
    chips = seq_size // CORES
    count = len(pieces)

    def kernel(*refs):
        ins, outs, sems = refs[:count], refs[count : 2 * count], refs[2 * count :]
        p = Place(seq_size, fsdp_size)
        greet(p, False)
        shares = [SeqShare(p, ins[i], outs[i], sems, i) for i in range(count)]
        for share in shares:
            share.start()
        for share in shares:
            share.finish()

    return pl.pallas_call(
        kernel,
        in_specs=[pl.BlockSpec(memory_space=pltpu.VMEM)] * count,
        out_specs=[pl.BlockSpec(memory_space=pl.ANY)] * count,
        out_shape=[jax.ShapeDtypeStruct((seq_size,) + v.shape, v.dtype) for v in pieces],
        scratch_shapes=share_sems(chips, count),
        compiler_params=talking(collective_id),
        name="share_pieces",
    )(*pieces)


def sum_and_share(partial, vectors, pieces, seq_size, fsdp_size, collective_id):
    chips = seq_size // CORES
    deep = planes(fsdp_size)
    across = fsdp_size // deep
    rows, width = partial.shape[0] // fsdp_size, partial.shape[1]
    lanes = vectors.shape[1] // fsdp_size
    count = len(pieces) + 1
    dma = pltpu.SemaphoreType.DMA

    def kernel(part_ref, vec_ref, *refs):
        ins, refs = refs[: count - 1], refs[count - 1 :]
        outs, refs = refs[:count], refs[count:]
        (
            vec_out, from_y, over_y, from_z, piece, vec_cut, vec_f, vec_s, vec_sum,
            y_send, y_recv, z_send, z_recv, f_send, f_recv, s_send, s_recv,
        ) = refs[:17]
        sems = refs[17:]
        p = Place(seq_size, fsdp_size)
        greet_all(p)

        def block(z, y):
            return pl.ds(pl.multiple_of((z * across + y) * rows, rows), rows)

        def to_y(z, k):
            return remote(
                part_ref.at[block(z, (p.y + k) % across)], from_y.at[k, z],
                y_send.at[k, z], y_recv.at[k, z], fsdp=p.along_y(k),
            )

        def to_z(k):
            return remote(
                over_y.at[(p.z + k) % deep], from_z.at[k],
                z_send.at[k], z_recv.at[k], fsdp=p.along_z(k),
            )

        def vec_to(k):
            return remote(
                vec_cut.at[(p.fsdp + k) % fsdp_size], vec_f.at[k],
                f_send.at[k], f_recv.at[k], fsdp=(p.fsdp + k) % fsdp_size,
            )

        def vec_over(k):
            return remote(
                vec_sum, vec_s.at[k], s_send.at[k], s_recv.at[k], seq=(p.seq + k) % seq_size
            )

        for f in range(fsdp_size):
            vec_cut[f] = vec_ref[:, f * lanes : (f + 1) * lanes]
        for k in range(1, fsdp_size):
            vec_to(k).start()
        for z in range(deep):
            for k in range(1, across):
                to_y(z, k).start()
        shares = [SeqShare(p, ins[i], outs[i], sems, i) for i in range(count - 1)]
        for share in shares:
            share.start()
        for z in range(deep):
            total = part_ref[block(z, p.y)].astype(F32)
            for k in range(1, across):
                to_y(z, k).wait_recv()
                total = total + from_y[k, z].astype(F32)
            over_y[z] = total.astype(BF16)
        for k in range(1, deep):
            to_z(k).start()
        vec_total = vec_cut[p.fsdp]
        for k in range(1, fsdp_size):
            vec_to(k).wait_recv()
            vec_total = vec_total + vec_f[k]
        vec_sum[...] = vec_total
        for k in range(1, seq_size):
            vec_over(k).start()
        total = over_y[p.z].astype(F32)
        for k in range(1, deep):
            to_z(k).wait_recv()
            total = total + from_z[k].astype(F32)
        piece[...] = total.astype(BF16)
        shares.append(SeqShare(p, piece, outs[-1], sems, count - 1))
        shares[-1].start()
        for k in range(1, seq_size):
            vec_over(k).wait_recv()
            vec_total = vec_total + vec_s[k]
        vec_out[...] = vec_total
        for share in shares:
            share.finish()
        for z in range(deep):
            for k in range(1, across):
                to_y(z, k).wait_send()
        for k in range(1, deep):
            to_z(k).wait_send()
        for k in range(1, fsdp_size):
            vec_to(k).wait_send()
        for k in range(1, seq_size):
            vec_over(k).wait_send()

    vmem = pl.BlockSpec(memory_space=pltpu.VMEM)
    shapes = [v.shape for v in pieces] + [(rows, width)]
    cut = (8, lanes)
    return pl.pallas_call(
        kernel,
        in_specs=[vmem] * (count + 1),
        out_specs=[pl.BlockSpec(memory_space=pl.ANY)] * count + [vmem],
        out_shape=[jax.ShapeDtypeStruct((seq_size,) + shape, BF16) for shape in shapes]
        + [jax.ShapeDtypeStruct(cut, F32)],
        scratch_shapes=[
            pltpu.VMEM((across, deep, rows, width), BF16),
            pltpu.VMEM((deep, rows, width), BF16),
            pltpu.VMEM((deep, rows, width), BF16),
            pltpu.VMEM((rows, width), BF16),
            pltpu.VMEM((fsdp_size,) + cut, F32),
            pltpu.VMEM((fsdp_size,) + cut, F32),
            pltpu.VMEM((seq_size,) + cut, F32),
            pltpu.VMEM(cut, F32),
        ]
        + [dma((across, deep))] * 2
        + [dma((deep,))] * 2
        + [dma((fsdp_size,))] * 2
        + [dma((seq_size,))] * 2
        + share_sems(chips, count),
        compiler_params=talking(collective_id),
        name="sum_and_share",
    )(partial, vectors, *pieces)


def own_columns(gate, up, me, seq_size, fsdp_size):
    rows, columns = gate.shape
    shard = columns // fsdp_size
    chunk = shard // seq_size

    def kernel(me_ref, gate_ref, up_ref, out_ref):
        for s in range(seq_size):

            @pl.when(me_ref[0] == s)
            def _(s=s):
                for which, ref in enumerate((gate_ref, up_ref)):
                    taken = [
                        ref[:, f * shard + s * chunk : f * shard + (s + 1) * chunk]
                        for f in range(fsdp_size)
                    ]
                    at = which * chunk * fsdp_size
                    out_ref[:, at : at + chunk * fsdp_size] = jnp.concatenate(taken, axis=1)

    return pl.pallas_call(
        kernel,
        grid_spec=pltpu.PrefetchScalarGridSpec(
            num_scalar_prefetch=1,
            grid=(1,),
            in_specs=[pl.BlockSpec((rows, columns), lambda i, m: (0, 0))] * 2,
            out_specs=pl.BlockSpec((rows, 2 * chunk * fsdp_size), lambda i, m: (0, 0)),
        ),
        out_shape=jax.ShapeDtypeStruct((rows, 2 * chunk * fsdp_size), BF16),
        compiler_params=params(),
        cost_estimate=cost(rows, 1, 2 * columns),
        name="own_columns",
    )(jnp.full((1,), me, jnp.int32), gate, up)


def whole_columns(pieces, fsdp_size):
    seq_size, rows, columns = pieces.shape
    units = columns // 2
    chunk = units // fsdp_size

    def kernel(in_ref, gate_ref, up_ref):
        for which, ref in enumerate((gate_ref, up_ref)):
            for f in range(fsdp_size):
                at = which * units + f * chunk
                taken = [in_ref[s, :, at : at + chunk].astype(F32) for s in range(seq_size)]
                whole = jnp.concatenate(taken, axis=1)
                ref[:, f * chunk * seq_size : (f + 1) * chunk * seq_size] = whole

    tile = rows // 4
    out = pl.BlockSpec((tile, units * seq_size), lambda i: (i, 0))
    return pl.pallas_call(
        kernel,
        grid=(4,),
        in_specs=[pl.BlockSpec((seq_size, tile, columns), lambda i: (0, i, 0))],
        out_specs=[out, out],
        out_shape=[jax.ShapeDtypeStruct((rows, units * seq_size), F32)] * 2,
        compiler_params=params(),
        cost_estimate=cost(rows, 1, 2 * columns * seq_size),
        name="whole_columns",
    )(pieces)


def own_heads_spread(project_in, me, pairs, seq_size):
    rows, columns = project_in.shape
    every = columns // 3 // LANES
    step = seq_size // 2

    def kernel(me_ref, low_ref, high_ref, out_ref):
        lane = lax.broadcasted_iota(jnp.int32, (rows, LANES), 1)
        odd = me_ref[0] % 2 == 1
        first = low_ref[...].astype(F32)
        second = high_ref[...].astype(F32)
        first = jnp.where(odd, pltpu.roll(first, HEAD_DIM, 1), first)
        second = jnp.where(odd, second, pltpu.roll(second, HEAD_DIM, 1))
        out_ref[...] = jnp.where(lane < HEAD_DIM, first, second).astype(BF16)

    def source(ahead):
        return pl.BlockSpec(
            (rows, LANES),
            lambda part, p, m: (0, part * every + (2 * p + ahead) * step + m[0] // 2),
        )

    return pl.pallas_call(
        kernel,
        grid_spec=pltpu.PrefetchScalarGridSpec(
            num_scalar_prefetch=1,
            grid=(3, pairs),
            in_specs=[source(0), source(1)],
            out_specs=pl.BlockSpec((rows, LANES), lambda part, p, m: (0, 3 * p + part)),
        ),
        out_shape=jax.ShapeDtypeStruct((rows, 3 * pairs * LANES), BF16),
        compiler_params=params(),
        name="own_heads",
    )(jnp.full((1,), me, jnp.int32), project_in, project_in)


def whole_heads_spread(pieces):
    seq_size, rows, columns = pieces.shape
    each = columns * seq_size // 3
    step = seq_size // 2

    def kernel(in_ref, out_ref):
        lane = lax.broadcasted_iota(jnp.int32, (rows // 4, LANES), 1)
        for part in range(3):
            for b in range(each // LANES):
                shard, seq = b // step, 2 * (b % step)
                at = (3 * (shard // 2) + part) * LANES
                first = in_ref[seq, :, at : at + LANES].astype(F32)
                second = in_ref[seq + 1, :, at : at + LANES].astype(F32)
                if shard % 2:
                    first = pltpu.roll(first, HEAD_DIM, 1)
                else:
                    second = pltpu.roll(second, HEAD_DIM, 1)
                start = part * each + b * LANES
                out_ref[:, start : start + LANES] = jnp.where(lane < HEAD_DIM, first, second)

    return pl.pallas_call(
        kernel,
        grid=(4,),
        in_specs=[pl.BlockSpec((seq_size, rows // 4, columns), lambda i: (0, i, 0))],
        out_specs=pl.BlockSpec((rows // 4, 3 * each), lambda i: (i, 0)),
        out_shape=jax.ShapeDtypeStruct((rows, 3 * each), F32),
        compiler_params=params(),
        cost_estimate=cost(rows, 1, 3 * each),
        name="whole_heads",
    )(pieces)


def gather_fsdp(value):
    return lax.all_gather(value, "fsdp", axis=0, tiled=True)


def scatter_fsdp(value):
    return lax.psum_scatter(value, "fsdp", scatter_dimension=0, tiled=True)


def local(
    tokens,
    cont_lengths,
    project_in,
    project_out,
    gate_weight,
    up_weight,
    down_weight,
    first_gain,
    first_bias,
    second_gain,
    second_bias,
    grad_output,
):
    rows_dev, width = tokens.shape[1:]
    seq_size = lax.axis_size("seq")
    fsdp_size = lax.axis_size("fsdp")
    chips = seq_size // CORES
    total_rows = rows_dev * seq_size
    me = lax.axis_index("seq")
    order = seq_order(chips)
    shard_rows = project_in.shape[0]
    own_pairs = width // LANES // seq_size
    pieces_out = project_out.shape[0] // seq_size
    pieces_down = down_weight.shape[0] // seq_size
    far = range(1, chips)

    spread = pieces_out == HEAD_DIM
    if spread:
        in_part = own_heads_spread(project_in, me, own_pairs, seq_size)
    else:
        in_part = own_heads(project_in, me, own_pairs)
    vectors = jnp.stack([first_gain, first_bias, second_gain, second_bias]).astype(F32)
    all_tokens, w_in, vectors = opening(
        tokens[0],
        in_part,
        jnp.concatenate([vectors, vectors]),
        seq_size,
        fsdp_size,
    )
    gate_late, up_late, out_late = tie((gate_weight, up_weight, project_out), w_in)
    if spread:
        w_out = gather_fsdp(lax.dynamic_slice_in_dim(out_late, me * pieces_out, pieces_out, 0))
    else:
        own_rows = width // seq_size
        w_out = lax.dynamic_slice_in_dim(gather_fsdp(project_out), me * own_rows, own_rows, 0)
    vectors = jnp.transpose(vectors[:, :4], (1, 0, 2)).reshape(4, width)
    gain_one, bias_one, gain_two, bias_two = [vectors[i] for i in range(4)]
    upstream_own = tie(grad_output[0], all_tokens)
    upstream_far = [from_chip(upstream_own, chips, ahead) for ahead in far]
    down_slice = lax.dynamic_slice_in_dim(down_weight, me * pieces_down, pieces_down, 0)
    whole_tiles = pieces_down % 16 == 0
    w_gate_up = gather_fsdp(own_columns(gate_late, up_late, me, seq_size, fsdp_size))

    cosine, sine, ends = rope_tables(cont_lengths[0], total_rows)

    qkv, normed_first = project(all_tokens, w_in, gain_one, bias_one, cosine, sine)
    attended, qx = attend(ends, qkv)
    upstream_blocks = [grad_output[0], core_swap(grad_output[0], chips)]
    for block in upstream_far:
        block = tie(block, attended)
        upstream_blocks += [block, core_swap(block, chips)]

    def scatter_end(started):
        arriving, own, other, _ = started
        total = own.astype(F32) + other.astype(F32)
        for part in arriving:
            total = total + part.astype(F32)
        return total

    attended = tie(attended, upstream_blocks)
    parts = chip_matmul(attended, w_out, order, rows_dev, False, "attention_out")
    hidden, normed_blocks, w_down = hidden_rows(
        parts, tokens[0], gain_two, bias_two,
        down_slice if whole_tiles else down_slice[: pieces_down // 16 * 16],
        seq_size, fsdp_size,
    )
    if not whole_tiles:
        w_down = gather_fsdp(down_slice)
    product, grads, normed_second, upstream_all = feed(
        normed_blocks, upstream_blocks, w_gate_up, w_down
    )

    near_order = jnp.arange(chips * CORES, dtype=jnp.int32)

    def send_far(x, weight, x_order, name):
        sent = [
            (own.astype(F32) + core_swap(other, chips).astype(F32)).astype(BF16)
            for own, other in chip_matmul(x, weight, x_order[CORES:], rows_dev, True, name)
        ]
        return sent, [to_chip(value, chips, ahead) for value, ahead in zip(sent, far)]

    sent, arriving = send_far(grads, w_gate_up, near_order, "feed_back")
    own, other, grad_down = near_and_grad(
        tie(grads, *sent), w_gate_up, near_order[:CORES], product, upstream_all, rows_dev,
        "near_and_down",
    )
    grad_hidden, low_own, sums_two = closing_rows(
        [(own, other)], tie(arriving, grad_down), hidden, grad_output[0], gain_two,
        seq_size, fsdp_size, True, 3,
    )
    low_far = [from_chip(low_own, chips, ahead) for ahead in far]
    low_near = [low_own, core_swap(low_own, chips)]

    normed_late, product_late = tie((normed_second, product), low_own)
    grad_gate_up = weight_grad(normed_late, grads, "grad_gate_up")
    product_late = tie(product_late, grad_gate_up)

    layer_parts = chip_matmul(product_late, w_down, near_order, rows_dev, False, "feed_down")
    (layer_own, layer_other), layer_far = layer_parts[0], layer_parts[1:]
    low_far = tie(low_far, layer_own)
    layer_far = tie(layer_far, low_far)
    grad_down_piece = scatter_fsdp(tie(grad_down, arriving))
    grad_gate_up_piece = scatter_fsdp(tie(grad_gate_up, low_far))
    low_blocks = low_near
    for block in low_far:
        low_blocks = low_blocks + [block, core_swap(block, chips)]
    layer_sent = [
        (own.astype(F32) + core_swap(other, chips).astype(F32)).astype(BF16)
        for own, other in layer_far
    ]
    layer_arriving = [to_chip(s, chips, ahead) for s, ahead in zip(layer_sent, far)]
    grad_attended, low_hidden = blocks_matmul(tie(low_blocks, layer_sent), w_out, order)
    grad_out = dot_first(attended, low_hidden).astype(BF16)
    grad_attended = tie(grad_attended, grad_out)

    grad_qkv = attend_back(ends, qkv, qx, grad_attended, attended, cosine, sine)
    grad_qkv = tie(grad_qkv, layer_arriving)
    sent, arriving = send_far(grad_qkv, w_in, order, "project_back")
    grad_late = tie(grad_qkv, *sent)
    own, other, grad_in = near_and_grad(
        grad_late, w_in, order[:CORES], normed_first, grad_late, rows_dev, "near_and_project_in"
    )
    arriving = tie(arriving, grad_in)
    grad_in_piece = scatter_fsdp(tie(grad_in, arriving))
    input_gradient, sums_one = closing_rows(
        [(own, other)], arriving, tokens[0], grad_hidden, gain_one,
        seq_size, fsdp_size, False, 4,
    )
    layer_rows = hidden + scatter_end(
        (layer_arriving, layer_own, core_swap(layer_other, chips), None)
    )

    sums = jnp.concatenate([sums_one[:2], sums_two[:2], sums_one[2:6]])
    all_gate_up, all_down, all_out, sums = sum_and_share(
        grad_out, sums, [grad_gate_up_piece, grad_down_piece], seq_size, fsdp_size, 5
    )
    (all_in,) = share_pieces([tie(grad_in_piece, all_out)], seq_size, fsdp_size, 6)
    if spread:
        grad_in = whole_heads_spread(all_in)
        grad_out = all_out.reshape(project_out.shape).astype(F32)
    else:
        grad_in = all_in.reshape(seq_size, shard_rows, own_pairs, 3, LANES)
        grad_in = jnp.transpose(grad_in, (1, 3, 0, 2, 4)).reshape(shard_rows, 3 * width)
        grad_in = grad_in.astype(F32)
        whole = jnp.zeros((width, width), F32)
        whole = lax.dynamic_update_slice_in_dim(
            whole, grad_out.astype(F32), me * (width // seq_size), 0
        )
        grad_out = lax.psum(scatter_fsdp(whole), "seq")
    grad_gate, grad_up = whole_columns(all_gate_up, fsdp_size)
    return (
        layer_rows.astype(BF16)[None],
        input_gradient[None],
        grad_in,
        grad_out,
        grad_gate,
        grad_up,
        all_down.reshape(down_weight.shape).astype(F32),
        sums[0],
        sums[1],
        sums[2],
        sums[3],
    )


def solution(mesh):
    return jax.shard_map(
        local,
        mesh=mesh,
        in_specs=(
            P("fsdp", "seq", None),
            P("fsdp", None),
            P("fsdp", None),
            P("fsdp", None),
            P("fsdp", None),
            P("fsdp", None),
            P("fsdp", None),
            P("fsdp"),
            P("fsdp"),
            P("fsdp"),
            P("fsdp"),
            P("fsdp", "seq", None),
        ),
        out_specs=(
            P("fsdp", "seq", None),
            P("fsdp", "seq", None),
            P("fsdp", None),
            P("fsdp", None),
            P("fsdp", None),
            P("fsdp", None),
            P("fsdp", None),
            P("fsdp"),
            P("fsdp"),
            P("fsdp"),
            P("fsdp"),
        ),
        check_vma=False,
    )
```

```python
import functools

import jax
import jax.numpy as jnp
from jax import lax
from jax.experimental import pallas as pl
from jax.experimental.pallas import tpu as pltpu
from jax.sharding import PartitionSpec as P

HEAD_DIM = 64
ROT = 16
PROMPT = 2048
LANES = 128

epsilon = 1e-05
rope_base = 10000.0

BF16 = jnp.bfloat16
F32 = jnp.float32
CORES = 2
VMEM_LIMIT = 56 * 1024 * 1024


def dot_last(left_side, right_side):
    return lax.dot_general(
        left_side, right_side, (((1,), (1,)), ((), ())), preferred_element_type=F32
    )


def dot_first(left_side, right_side):
    return lax.dot_general(
        left_side, right_side, (((0,), (0,)), ((), ())), preferred_element_type=F32
    )


def dot(left_side, right_side):
    return jnp.dot(left_side, right_side, preferred_element_type=F32)


def cont_ends(lengths):
    count = lengths.shape[0]
    before = jnp.arange(count)[None, :] <= jnp.arange(count)[:, None]
    return jnp.sum(jnp.where(before, lengths[None, :], 0), axis=1)


def rope_tables(lengths, total_rows):
    ends = cont_ends(lengths)
    starts = ends - lengths
    indices = jnp.arange(total_rows, dtype=jnp.int32)
    offset = indices - PROMPT
    inside = (offset[:, None] >= starts[None, :]) & (offset[:, None] < ends[None, :])
    seg_begin = jnp.sum(jnp.where(inside, starts[None, :], 0), axis=1)
    position = jnp.where(indices < PROMPT, indices, PROMPT + offset - seg_begin)
    half = ROT // 2
    within = jnp.arange(LANES, dtype=jnp.int32) % HEAD_DIM
    frequency = rope_base ** (-2.0 * (within % half).astype(F32) / ROT)
    angles = position.astype(F32)[:, None] * frequency[None, :]
    turning = (within < ROT)[None, :]
    sign = jnp.where(within < half, -1.0, 1.0)[None, :]
    cosine = jnp.where(turning, jnp.cos(angles), 1.0)
    sine = jnp.where(turning, sign * jnp.sin(angles), 0.0)
    return cosine, sine, ends


def turn(rows_in, cosine, sine):
    half = ROT // 2
    lane = lax.broadcasted_iota(jnp.int32, rows_in.shape, 1) % HEAD_DIM
    partner = jnp.where(
        lane < half,
        pltpu.roll(rows_in, LANES - half, 1),
        pltpu.roll(rows_in, half, 1),
    )
    return rows_in * cosine + partner * sine


def project_kernel(x_ref, w_ref, gain_ref, bias_ref, cos_ref, sin_ref, out_ref, normed_ref):
    cosine = cos_ref[...]
    sine = sin_ref[...]
    pairs = out_ref.shape[1] // (3 * LANES)
    x = x_ref[...].astype(F32)
    x = x - jnp.mean(x, axis=1, keepdims=True)
    x = x * lax.rsqrt(jnp.mean(x * x, axis=1, keepdims=True) + epsilon)
    x = (x * gain_ref[0:1, :] + bias_ref[0:1, :]).astype(BF16)
    normed_ref[...] = x
    for first in range(0, pairs, 2):
        begin = 3 * LANES * first
        mixed = dot(x, w_ref[:, begin : begin + 6 * LANES])
        for pair in range(2):
            base = 3 * LANES * pair
            query = turn(mixed[:, base : base + LANES], cosine, sine) * HEAD_DIM ** (-0.5)
            key = turn(mixed[:, base + LANES : base + 2 * LANES], cosine, sine)
            value = mixed[:, base + 2 * LANES : base + 3 * LANES]
            base = base + begin
            out_ref[:, base : base + LANES] = query.astype(BF16)
            out_ref[:, base + LANES : base + 2 * LANES] = key.astype(BF16)
            out_ref[:, base + 2 * LANES : base + 3 * LANES] = value.astype(BF16)


def project(x, weight, gain, bias, cosine, sine):
    rows, depth = x.shape
    columns = weight.shape[1]
    block = 512
    vector = pl.BlockSpec((8, depth), lambda i: (0, 0))
    return pl.pallas_call(
        project_kernel,
        grid=(rows // block,),
        in_specs=[
            pl.BlockSpec((block, depth), lambda i: (i, 0)),
            pl.BlockSpec((depth, columns), lambda i: (0, 0), pipeline_mode=pl.Buffered(1)),
            vector,
            vector,
            pl.BlockSpec((block, LANES), lambda i: (i, 0)),
            pl.BlockSpec((block, LANES), lambda i: (i, 0)),
        ],
        out_specs=[
            pl.BlockSpec((block, columns), lambda i: (i, 0)),
            pl.BlockSpec((block, depth), lambda i: (i, 0)),
        ],
        out_shape=[
            jax.ShapeDtypeStruct((rows, columns), BF16),
            jax.ShapeDtypeStruct((rows, depth), BF16),
        ],
        compiler_params=pltpu.CompilerParams(vmem_limit_bytes=VMEM_LIMIT),
        cost_estimate=pl.CostEstimate(
            flops=2 * rows * depth * columns,
            bytes_accessed=2 * (rows * depth + depth * columns + rows * columns),
            transcendentals=0,
        ),
        name="project_in_rope",
    )(
        x,
        weight,
        jnp.broadcast_to(gain[None], (8, depth)),
        jnp.broadcast_to(bias[None], (8, depth)),
        cosine,
        sine,
    )


BLOCK = 512
NEG = -1e30


def segment_of(index, ends_ref):
    count = jnp.zeros_like(index)
    for c in range(ends_ref.shape[0] - 1):
        count = count + (index >= PROMPT + ends_ref[c]).astype(jnp.int32)
    return count


def attend_kernel(ends_ref, *refs):
    held = len(refs) // 3
    q_refs, k_refs, v_refs = refs[:held], refs[held : 2 * held], refs[2 * held : 3 * held]
    o_ref, qx_ref = refs[3 * held :]
    rows = k_refs[0].shape[0]
    lane = lax.broadcasted_iota(jnp.int32, (BLOCK, LANES), 1)
    inside = [lane < HEAD_DIM, lane >= HEAD_DIM]

    def one_block(number):
        start = number * BLOCK
        end = start + BLOCK
        full = min(start, PROMPT)
        row = lax.broadcasted_iota(jnp.int32, (BLOCK, 1), 0) + start
        col = lax.broadcasted_iota(jnp.int32, (1, end - full), 1) + full
        visible = col <= row
        if end > PROMPT:
            visible = visible & (segment_of(row, ends_ref) == segment_of(col, ends_ref))
        for pair in range(held):
            q = q_refs[pair][...]
            outs = []
            for h in range(2):
                q_head = jnp.where(inside[h], q, jnp.zeros_like(q))
                v = v_refs[pair][:end, :]
                lane_v = lax.broadcasted_iota(jnp.int32, v.shape, 1)
                own_v = (lane_v < HEAD_DIM) if h == 0 else (lane_v >= HEAD_DIM)
                v_one = jnp.where(own_v, v, jnp.ones_like(v))
                near = dot_last(q_head, k_refs[pair][full:end, :])
                near = jnp.where(visible, near, NEG)
                peak = jnp.max(near, axis=1, keepdims=True)
                if full:
                    early = dot_last(q_head, k_refs[pair][:full, :])
                    peak = jnp.maximum(peak, jnp.max(early, axis=1, keepdims=True))
                acc = dot(jnp.exp(near - peak).astype(BF16), v_one[full:])
                if full:
                    acc = acc + dot(jnp.exp(early - peak).astype(BF16), v_one[:full])
                outs.append(acc / pltpu.roll(acc, HEAD_DIM, 1))
                minus = -(peak + jnp.log(jnp.where(inside[h], 1.0, acc)))
                high = minus.astype(BF16)
                rest = minus - high.astype(F32)
                mid = rest.astype(BF16)
                low = (rest - mid.astype(F32)).astype(BF16)
                base = HEAD_DIM * (1 - h)
                spare = jnp.where(
                    lane == base, high, jnp.where(lane == base + 1, mid, jnp.zeros_like(high))
                )
                spare = jnp.where(lane == base + 2, low, spare)
                qx_ref[2 * pair + h] = jnp.where(inside[h], q, spare)
            o_ref[:, pair * LANES : (pair + 1) * LANES] = jnp.where(
                inside[0], outs[0], outs[1]
            ).astype(BF16)

    for number in range(rows // BLOCK):
        pl.when(pl.program_id(1) == number)(functools.partial(one_block, number))


def attend(ends, qkv):
    rows, columns = qkv.shape
    pairs = columns // (3 * LANES)
    held = 2
    work = rows * rows // 2 * pairs * 2

    def part(which, height, pair):
        return pl.BlockSpec(
            (height, LANES),
            lambda p, i, e: (i if height == BLOCK else 0, 3 * (p * held + pair) + which),
        )

    return pl.pallas_call(
        attend_kernel,
        grid_spec=pltpu.PrefetchScalarGridSpec(
            num_scalar_prefetch=1,
            grid=(pairs // held, rows // BLOCK),
            in_specs=[
                part(which, BLOCK if which == 0 else rows, pair)
                for which in range(3)
                for pair in range(held)
            ],
            out_specs=[
                pl.BlockSpec((BLOCK, held * LANES), lambda p, i, e: (i, p)),
                pl.BlockSpec((2 * held, BLOCK, LANES), lambda p, i, e: (p, i, 0)),
            ],
        ),
        out_shape=[
            jax.ShapeDtypeStruct((rows, pairs * LANES), BF16),
            jax.ShapeDtypeStruct((2 * pairs, rows, LANES), BF16),
        ],
        compiler_params=pltpu.CompilerParams(vmem_limit_bytes=VMEM_LIMIT),
        cost_estimate=pl.CostEstimate(
            flops=work * 1024, bytes_accessed=2 * rows * columns, transcendentals=0
        ),
        name="attend",
    )(ends, *([qkv] * (3 * held)))


def attend_back_kernel(
    ends_ref, qx_ref, k_ref, v_ref, g_ref, o_ref, cos_ref, sin_ref, out_ref,
    gx_ref, dq_ref, dk_ref, dv_ref,
):
    number = pl.program_id(1)
    blocks = pl.num_programs(1)
    rows = qx_ref.shape[1]
    lane = lax.broadcasted_iota(jnp.int32, (BLOCK, LANES), 1)
    inside = [lane < HEAD_DIM, lane >= HEAD_DIM]

    @pl.when(number == 0)
    def _():
        dq_ref[...] = jnp.zeros_like(dq_ref)

        @pl.loop(0, rows // BLOCK)
        def _(j):
            here = pl.ds(pl.multiple_of(j * BLOCK, BLOCK), BLOCK)
            g = g_ref[here, :]
            both = g.astype(F32) * o_ref[here, :].astype(F32)
            for h in range(2):
                minus = -jnp.sum(jnp.where(inside[h], both, 0.0), axis=1, keepdims=True)
                high = minus.astype(BF16)
                rest = minus - high.astype(F32)
                mid = rest.astype(BF16)
                low = (rest - mid.astype(F32)).astype(BF16)
                base = HEAD_DIM * (1 - h)
                spare = jnp.where(
                    lane == base, high, jnp.where(lane == base + 1, mid, jnp.zeros_like(g))
                )
                spare = jnp.where(lane == base + 2, low, spare)
                gx_ref[h, here, :] = jnp.where(inside[h], g, spare)

    k = k_ref[...]
    v = v_ref[...]
    k_one = [jnp.where(inside[h], k, jnp.ones_like(k)) for h in range(2)]
    v_one = [jnp.where(inside[h], v, jnp.ones_like(v)) for h in range(2)]
    k_turned = [jnp.where(inside[h], k, jnp.zeros_like(k)).T for h in range(2)]
    dk_ref[...] = jnp.zeros_like(dk_ref)
    dv_ref[...] = jnp.zeros_like(dv_ref)

    def step(start, masked, keys=(0, BLOCK), size=BLOCK):
        here = pl.ds(start, size)
        first, end = keys
        if masked:
            row = lax.broadcasted_iota(jnp.int32, (1, size), 1) + start
            col = lax.broadcasted_iota(jnp.int32, (end - first, 1), 0) + number * BLOCK + first
            visible = (col <= row) & (segment_of(row, ends_ref) == segment_of(col, ends_ref))
        total = None
        for h in range(2):
            qx = qx_ref[h, here, :]
            gx = gx_ref[h, here, :]
            chances = jnp.exp(dot_last(k_one[h][first:end], qx))
            if masked:
                chances = jnp.where(visible, chances, 0.0)
            dv_ref[h, first:end] += dot(chances.astype(BF16), gx)
            grad_scores = (chances * dot_last(v_one[h][first:end], gx)).astype(BF16)
            dk_ref[h, first:end] += dot(grad_scores, qx)
            part = dot(k_turned[h][:, first:end], grad_scores)
            total = part if total is None else total + part
        dq_ref[:, here] += total

    half = BLOCK // 2
    step(pl.multiple_of(number * BLOCK, BLOCK), True, (0, half))
    step(pl.multiple_of(number * BLOCK + half, half), True, (half, BLOCK), half)

    @pl.loop(number + 1, blocks)
    def _(j):
        step(pl.multiple_of(j * BLOCK, BLOCK), False)

    here = pl.ds(pl.multiple_of(number * BLOCK, BLOCK), BLOCK)
    dk = jnp.where(inside[0], dk_ref[0], dk_ref[1])
    dk = turn(dk, cos_ref[here, :], -sin_ref[here, :])
    out_ref[here, LANES : 2 * LANES] = dk.astype(BF16)
    out_ref[here, 2 * LANES :] = jnp.where(inside[0], dv_ref[0], dv_ref[1]).astype(BF16)

    @pl.when(number == blocks - 1)
    def _():
        for j in range(rows // BLOCK):
            here = slice(j * BLOCK, (j + 1) * BLOCK)
            dq = dq_ref[:, here].T * HEAD_DIM ** (-0.5)
            dq = turn(dq, cos_ref[here, :], -sin_ref[here, :])
            out_ref[here, :LANES] = dq.astype(BF16)


def attend_back(ends, qkv, qx, grad, attended, cosine, sine):
    rows, columns = qkv.shape
    pairs = columns // (3 * LANES)
    blocks = rows // BLOCK
    work = rows * rows // 2 * pairs * 2
    return pl.pallas_call(
        attend_back_kernel,
        grid_spec=pltpu.PrefetchScalarGridSpec(
            num_scalar_prefetch=1,
            grid=(pairs, blocks),
            in_specs=[
                pl.BlockSpec((2, rows, LANES), lambda p, i, e: (p, 0, 0)),
                pl.BlockSpec((BLOCK, LANES), lambda p, i, e: (i, 3 * p + 1)),
                pl.BlockSpec((BLOCK, LANES), lambda p, i, e: (i, 3 * p + 2)),
                pl.BlockSpec((rows, LANES), lambda p, i, e: (0, p)),
                pl.BlockSpec((rows, LANES), lambda p, i, e: (0, p)),
                pl.BlockSpec((rows, LANES), lambda p, i, e: (0, 0)),
                pl.BlockSpec((rows, LANES), lambda p, i, e: (0, 0)),
            ],
            out_specs=pl.BlockSpec((rows, 3 * LANES), lambda p, i, e: (0, p)),
            scratch_shapes=[
                pltpu.VMEM((2, rows, LANES), BF16),
                pltpu.VMEM((LANES, rows), F32),
                pltpu.VMEM((2, BLOCK, LANES), F32),
                pltpu.VMEM((2, BLOCK, LANES), F32),
            ],
        ),
        out_shape=jax.ShapeDtypeStruct((rows, columns), BF16),
        compiler_params=pltpu.CompilerParams(vmem_limit_bytes=VMEM_LIMIT),
        cost_estimate=pl.CostEstimate(
            flops=work * 2560, bytes_accessed=2 * rows * columns, transcendentals=0
        ),
        name="attend_back",
    )(ends, qx, qkv, qkv, grad, attended, cosine, sine)


def params():
    return pltpu.CompilerParams(vmem_limit_bytes=VMEM_LIMIT)


def cost(rows, depth, columns):
    return pl.CostEstimate(
        flops=2 * rows * depth * columns,
        bytes_accessed=2 * (rows * depth + depth * columns + rows * columns),
        transcendentals=0,
    )


def chip_matmul(x, weight, order, rows, turned, name):
    depth = x.shape[1]
    columns = weight.shape[0] if turned else weight.shape[1]
    half = rows // 2
    count = order.shape[0]

    def kernel(order_ref, x_ref, w_ref, *outs):
        multiply = dot_last if turned else dot
        made = multiply(x_ref[...], w_ref[...]).astype(BF16)
        for b in range(count):

            @pl.when(pl.program_id(0) // 2 == b)
            def _(b=b):
                outs[b][...] = made

    made = pl.pallas_call(
        kernel,
        grid_spec=pltpu.PrefetchScalarGridSpec(
            num_scalar_prefetch=1,
            grid=(2 * count,),
            in_specs=[
                pl.BlockSpec((half, depth), lambda i, o: (o[i // 2] * 2 + i % 2, 0)),
                pl.BlockSpec(weight.shape, lambda i, o: (0, 0), pipeline_mode=pl.Buffered(1)),
            ],
            out_specs=[
                pl.BlockSpec((half, columns), lambda i, o, b=b: (jnp.clip(i - 2 * b, 0, 1), 0))
                for b in range(count)
            ],
        ),
        out_shape=[jax.ShapeDtypeStruct((rows, columns), BF16)] * count,
        compiler_params=params(),
        cost_estimate=cost(count * rows, depth, columns),
        name=name,
    )(order, x, weight)
    return [(made[2 * i], made[2 * i + 1]) for i in range(count // 2)]


def buffers(steps):
    return pl.Buffered(1 if steps == 1 else 2)


def weight_grad(x, g, name):
    rows, columns = g.shape
    height = x.shape[1]
    tile = 256 if height % 256 == 0 else height
    part = columns if height % 256 == 0 else 512

    def kernel(x_ref, g_ref, out_ref):
        out_ref[...] = dot_first(x_ref[...], g_ref[...]).astype(BF16)

    return pl.pallas_call(
        kernel,
        grid=(height // tile, columns // part),
        in_specs=[
            pl.BlockSpec((rows, tile), lambda i, j: (0, i), pipeline_mode=buffers(height // tile)),
            pl.BlockSpec((rows, part), lambda i, j: (0, j), pipeline_mode=buffers(columns // part)),
        ],
        out_specs=pl.BlockSpec((tile, part), lambda i, j: (i, j)),
        out_shape=jax.ShapeDtypeStruct((height, columns), BF16),
        compiler_params=params(),
        cost_estimate=cost(height, rows, columns),
        name=name,
    )(x, g)


def own_heads(project_in, me, pairs):
    rows, columns = project_in.shape
    every = columns // 3 // LANES

    def kernel(first_ref, in_ref, out_ref):
        out_ref[...] = in_ref[...]

    return pl.pallas_call(
        kernel,
        grid_spec=pltpu.PrefetchScalarGridSpec(
            num_scalar_prefetch=1,
            grid=(3, pairs),
            in_specs=[
                pl.BlockSpec((rows, LANES), lambda part, p, f: (0, part * every + f[0] + p))
            ],
            out_specs=pl.BlockSpec((rows, LANES), lambda part, p, f: (0, 3 * p + part)),
        ),
        out_shape=jax.ShapeDtypeStruct((rows, 3 * pairs * LANES), BF16),
        compiler_params=params(),
        name="own_heads",
    )(jnp.full((1,), me * pairs, jnp.int32), project_in)


def feed(normed, upstream, w_gate_up, w_down):
    count, rows, width = normed.shape
    units = w_down.shape[0]
    half = rows // 2
    total = rows * count

    def kernel(x_ref, *refs):
        ups, refs = refs[:count], refs[count:]
        wgu_ref, wd_ref, product_ref, grads_ref, normed_ref, upstream_ref = refs
        for b in range(count):

            @pl.when(pl.program_id(0) // 2 == b)
            def _(b=b):
                upstream_ref[...] = ups[b][...]

        x = x_ref[0]
        normed_ref[...] = x
        both = dot(x, wgu_ref[...])
        mid = dot_last(upstream_ref[...], wd_ref[...])
        gate = both[:, :units]
        up = both[:, units:]
        sigmoid = 1.0 / (1.0 + jnp.exp(-gate))
        silu = gate * sigmoid
        product_ref[...] = (silu * up).astype(BF16)
        slope = sigmoid * (1.0 + gate * (1.0 - sigmoid))
        grads_ref[:, :units] = (mid * up * slope).astype(BF16)
        grads_ref[:, units:] = (mid * silu).astype(BF16)

    def here(i):
        return (i, 0)

    def block_spec(b):
        return pl.BlockSpec((half, width), lambda i: (jnp.clip(i - 2 * b, 0, 1), 0))

    return pl.pallas_call(
        kernel,
        grid=(2 * count,),
        in_specs=[pl.BlockSpec((1, half, width), lambda i: (i // 2, i % 2, 0))]
        + [block_spec(b) for b in range(count)]
        + [
            pl.BlockSpec(w_gate_up.shape, lambda i: (0, 0), pipeline_mode=pl.Buffered(1)),
            pl.BlockSpec(w_down.shape, lambda i: (0, 0), pipeline_mode=pl.Buffered(1)),
        ],
        out_specs=[
            pl.BlockSpec((half, units), here),
            pl.BlockSpec((half, 2 * units), here),
            pl.BlockSpec((half, width), here),
            pl.BlockSpec((half, width), here),
        ],
        out_shape=[
            jax.ShapeDtypeStruct((total, units), BF16),
            jax.ShapeDtypeStruct((total, 2 * units), BF16),
            jax.ShapeDtypeStruct((total, width), BF16),
            jax.ShapeDtypeStruct((total, width), BF16),
        ],
        compiler_params=params(),
        cost_estimate=cost(total, 3 * width, units),
        name="feed",
    )(normed, *upstream, w_gate_up, w_down)


def near_and_grad(x, weight, order, left, right, rows, name):
    columns = x.shape[1]
    total, height = left.shape
    width = weight.shape[0]
    breadth = right.shape[1]
    half = rows // 2
    tile = 512 if breadth % 512 == 0 else 256

    def kernel(order_ref, x_ref, w_ref, left_ref, right_ref, own_ref, other_ref, out_ref):
        step = pl.program_id(0)

        @pl.when(step < 4)
        def _():
            made = dot_last(x_ref[...], w_ref[...]).astype(BF16)

            @pl.when(step < 2)
            def _():
                own_ref[...] = made

            @pl.when(step >= 2)
            def _():
                other_ref[...] = made

        @pl.when(step >= 4)
        def _():
            out_ref[...] = dot_first(left_ref[...], right_ref[...]).astype(BF16)

    def late(i):
        return jnp.maximum(i - 4, 0)

    def near(i, o):
        step = jnp.minimum(i, 3)
        return (o[step // 2] * 2 + step % 2, 0)

    return pl.pallas_call(
        kernel,
        grid_spec=pltpu.PrefetchScalarGridSpec(
            num_scalar_prefetch=1,
            grid=(4 + breadth // tile,),
            in_specs=[
                pl.BlockSpec((half, columns), near),
                pl.BlockSpec(weight.shape, lambda i, o: (0, 0), pipeline_mode=pl.Buffered(1)),
                pl.BlockSpec(left.shape, lambda i, o: (0, 0), pipeline_mode=pl.Buffered(1)),
                pl.BlockSpec((total, tile), lambda i, o: (0, late(i))),
            ],
            out_specs=[
                pl.BlockSpec((half, width), lambda i, o: (jnp.minimum(i, 1), 0)),
                pl.BlockSpec((half, width), lambda i, o: (jnp.clip(i - 2, 0, 1), 0)),
                pl.BlockSpec((height, tile), lambda i, o: (0, late(i))),
            ],
        ),
        out_shape=[
            jax.ShapeDtypeStruct((rows, width), BF16),
            jax.ShapeDtypeStruct((rows, width), BF16),
            jax.ShapeDtypeStruct((height, breadth), BF16),
        ],
        compiler_params=params(),
        cost_estimate=cost(total + rows, width, columns),
        name=name,
    )(order, x, weight, left, right)


def blocks_matmul(blocks, weight, order):
    rows, depth = blocks[0].shape
    columns = weight.shape[0]
    half = rows // 2
    count = len(blocks)

    def kernel(order_ref, *refs):
        ins, (w_ref, out_ref, copy_ref) = refs[:count], refs[count:]
        for b in range(count):

            @pl.when(pl.program_id(0) // 2 == b)
            def _(b=b):
                copy_ref[...] = ins[b][...]

        out_ref[...] = dot_last(copy_ref[...], w_ref[...]).astype(BF16)

    def block_spec(b):
        return pl.BlockSpec((half, depth), lambda i, o: (jnp.clip(i - 2 * b, 0, 1), 0))

    return pl.pallas_call(
        kernel,
        grid_spec=pltpu.PrefetchScalarGridSpec(
            num_scalar_prefetch=1,
            grid=(2 * count,),
            in_specs=[block_spec(b) for b in range(count)]
            + [pl.BlockSpec(weight.shape, lambda i, o: (0, 0), pipeline_mode=pl.Buffered(1))],
            out_specs=[
                pl.BlockSpec((half, columns), lambda i, o: (o[i // 2] * 2 + i % 2, 0)),
                pl.BlockSpec((half, depth), lambda i, o: (o[i // 2] * 2 + i % 2, 0)),
            ],
        ),
        out_shape=[
            jax.ShapeDtypeStruct((rows * count, columns), BF16),
            jax.ShapeDtypeStruct((rows * count, depth), BF16),
        ],
        compiler_params=params(),
        cost_estimate=cost(rows * count, depth, columns),
        name="grad_attended",
    )(order, *blocks, weight)


def tie(value, *others):
    return lax.optimization_barrier((value, others))[0]


def from_chip(value, chips, ahead):
    size = chips * CORES
    return lax.ppermute(value, "seq", [(i, (i - ahead * CORES) % size) for i in range(size)])


def to_chip(value, chips, ahead):
    return from_chip(value, chips, chips - ahead)


def core_swap(value, chips):
    return lax.ppermute(value, "seq", [(i, i ^ 1) for i in range(chips * CORES)])


def seq_order(chips):
    me = lax.axis_index("seq")
    core, chip = me % CORES, me // CORES
    found = []
    for ahead in range(chips):
        base = (chip + ahead) % chips * CORES
        found += [base + core, base + 1 - core]
    return jnp.stack(found).astype(jnp.int32)


def planes(size):
    return 4 if size % 4 == 0 else 1


def remote(src, dst, send, recv, **where):
    return pltpu.make_async_remote_copy(
        src_ref=src, dst_ref=dst, send_sem=send, recv_sem=recv, device_id=where,
        device_id_type=pl.DeviceIdType.MESH,
    )


def rows_at(ref, index, rows):
    return ref.at[pl.ds(pl.multiple_of(index * rows, rows), rows)]


class Place:
    def __init__(self, seq_size, fsdp_size):
        self.chips = seq_size // CORES
        self.seq_size, self.fsdp_size = seq_size, fsdp_size
        self.deep = planes(fsdp_size)
        self.across = fsdp_size // self.deep
        self.seq = lax.axis_index("seq")
        self.fsdp = lax.axis_index("fsdp")
        self.core, self.chip = self.seq % CORES, self.seq // CORES
        self.z, self.y = self.fsdp // self.across, self.fsdp % self.across

    def along_x(self, k):
        return (self.chip + k) % self.chips * CORES + self.core

    def other(self):
        return self.chip * CORES + 1 - self.core

    def along_z(self, k):
        return (self.z + k) % self.deep * self.across + self.y

    def along_y(self, k):
        return self.z * self.across + (self.y + k) % self.across

    def shard(self, kz, ky):
        return (self.z + kz) % self.deep * self.across + (self.y + ky) % self.across


def greet_device(**where):
    pl.semaphore_signal(
        pltpu.get_barrier_semaphore(),
        inc=1,
        device_id=where,
        device_id_type=pl.DeviceIdType.MESH,
    )


def greet(place, over_fsdp):
    count = place.chips
    for k in range(1, place.chips):
        greet_device(seq=place.along_x(k))
    greet_device(seq=place.other())
    if over_fsdp:
        count += place.fsdp_size - 1
        for k in range(1, place.fsdp_size):
            greet_device(fsdp=(place.fsdp + k) % place.fsdp_size)
    pl.semaphore_wait(pltpu.get_barrier_semaphore(), count)


def greet_all(place):
    for k in range(1, place.seq_size):
        greet_device(seq=(place.seq + k) % place.seq_size)
    for k in range(1, place.fsdp_size):
        greet_device(fsdp=(place.fsdp + k) % place.fsdp_size)
    count = place.seq_size + place.fsdp_size - 2
    pl.semaphore_wait(pltpu.get_barrier_semaphore(), count)


class FsdpGather:
    def __init__(self, place, own, whole, sems):
        self.place, self.own, self.whole = place, own, whole
        self.rows = own.shape[0]
        self.send_z, self.recv_z, self.send_y, self.recv_y = sems

    def slot(self, index):
        return rows_at(self.whole, index, self.rows)

    def z(self, up, d):
        p = self.place
        sign = 1 if up else -1
        slot = self.slot(p.shard(sign * (1 - d), 0))
        index = (0 if up else p.deep) + d
        return remote(
            self.own if d == 1 else slot, slot,
            self.send_z.at[index], self.recv_z.at[index], fsdp=p.along_z(sign),
        )

    def sends(self, up, d):
        z, deep = self.place.z, self.place.deep
        return (z >= d - 1) & (z + 1 < deep) if up else (z + d - 1 < deep) & (z >= 1)

    def gets(self, up, d):
        z, deep = self.place.z, self.place.deep
        return z >= d if up else z + d < deep

    def y(self, kz, ky):
        p = self.place
        slot = self.slot(p.shard(-kz, 0))
        return remote(
            self.own if kz == 0 else slot, slot,
            self.send_y.at[kz, ky], self.recv_y.at[kz, ky], fsdp=p.along_y(ky),
        )

    def start(self):
        for up in (True, False):
            pl.when(self.sends(up, 1))(lambda up=up: self.z(up, 1).start())
        for ky in range(1, self.place.across):
            self.y(0, ky).start()

    def pass_on(self, d):
        deep = self.place.deep
        for up in (True, False):

            @pl.when(self.gets(up, d))
            def _(up=up):
                self.z(up, d).wait_recv()
                for ky in range(1, self.place.across):
                    self.y(d if up else deep - d, ky).start()

            if d + 1 < deep:
                pl.when(self.sends(up, d + 1))(lambda up=up: self.z(up, d + 1).start())

    def finish(self):
        deep, across = self.place.deep, self.place.across
        for kz in range(deep):
            for ky in range(1, across):
                self.y(kz, ky).wait()
        for d in range(1, deep):
            for up in (True, False):
                pl.when(self.sends(up, d))(lambda up=up, d=d: self.z(up, d).wait_send())


def fsdp_sems(place_deep, place_across):
    return [pltpu.SemaphoreType.DMA((2 * place_deep,))] * 2 + [
        pltpu.SemaphoreType.DMA((place_deep, place_across))
    ] * 2


def opening(tokens, in_part, vectors, seq_size, fsdp_size):
    rows, width = tokens.shape
    chips = seq_size // CORES
    deep = planes(fsdp_size)
    across = fsdp_size // deep
    dma = pltpu.SemaphoreType.DMA

    def kernel(
        tok_ref, in_ref, vec_ref, tok_all, w_in, vec_all,
        here, x_send, x_recv, c_send, c_recv, v_send, v_recv, *sems,
    ):
        p = Place(seq_size, fsdp_size)
        greet(p, True)

        def tok_slot(index):
            return rows_at(tok_all, index, rows)

        def tok_x(k):
            return remote(
                tok_ref, tok_slot(p.seq), x_send.at[k], x_recv.at[k], seq=p.along_x(k)
            )

        def tok_core(k):
            slot = tok_slot(p.along_x(-k))
            return remote(
                tok_ref if k == 0 else slot, slot, c_send.at[k], c_recv.at[k], seq=p.other()
            )

        def vec(k):
            return remote(
                vec_ref, vec_all.at[p.fsdp], v_send.at[k], v_recv.at[k],
                fsdp=(p.fsdp + k) % fsdp_size,
            )

        into = FsdpGather(p, in_ref, w_in, sems)
        own = [
            pltpu.make_async_copy(tok_ref, tok_slot(p.seq), here.at[0]),
            pltpu.make_async_copy(in_ref, into.slot(p.fsdp), here.at[1]),
            pltpu.make_async_copy(vec_ref, vec_all.at[p.fsdp], here.at[2]),
        ]
        for k in range(1, fsdp_size):
            vec(k).start()
        for k in range(1, chips):
            tok_x(k).start()
        into.start()
        tok_core(0).start()
        for copy in own:
            copy.start()
        for d in range(1, deep):
            into.pass_on(d)
        for k in range(1, chips):
            tok_x(k).wait_recv()
            tok_core(k).start()
        into.finish()
        for k in range(chips):
            tok_core(k).wait()
        for k in range(1, chips):
            tok_x(k).wait_send()
        for k in range(1, fsdp_size):
            vec(k).wait()
        for copy in own:
            copy.wait()

    any_space = pl.BlockSpec(memory_space=pl.ANY)
    return pl.pallas_call(
        kernel,
        in_specs=[pl.BlockSpec(memory_space=pltpu.VMEM)] * 3,
        out_specs=[any_space] * 3,
        out_shape=[
            jax.ShapeDtypeStruct((rows * seq_size, width), BF16),
            jax.ShapeDtypeStruct((in_part.shape[0] * fsdp_size, in_part.shape[1]), BF16),
            jax.ShapeDtypeStruct((fsdp_size,) + vectors.shape, F32),
        ],
        scratch_shapes=[
            dma((3,)), dma((chips,)), dma((chips,)), dma((chips,)), dma((chips,)),
            dma((fsdp_size,)), dma((fsdp_size,)),
        ]
        + fsdp_sems(deep, across),
        compiler_params=talking(1),
        name="opening",
    )(tokens, in_part, vectors)


def talking(collective_id):
    return pltpu.CompilerParams(
        collective_id=collective_id, has_side_effects=True, vmem_limit_bytes=VMEM_LIMIT
    )


CHUNKS = 4


def hidden_rows(parts, residual, gain, bias, carry, seq_size, fsdp_size):
    rows, width = residual.shape
    chips = seq_size // CORES
    deep = planes(fsdp_size)
    part = rows // CHUNKS
    dma = pltpu.SemaphoreType.DMA

    def kernel(*refs):
        own = refs[0 : 2 * chips : 2]
        other = refs[1 : 2 * chips : 2]
        refs = refs[2 * chips :]
        res_ref, gain_ref, bias_ref, carry_ref, hidden_ref, normed_ref, carried_all = refs[:7]
        (
            from_core, total, from_x, mine,
            c_send, c_recv, x_send, x_recv, g_send, g_recv, f_send, f_recv, here,
        ) = refs[7:20]
        p = Place(seq_size, fsdp_size)
        greet(p, True)
        carried = FsdpGather(p, carry_ref, carried_all, refs[20:])

        def span(c):
            return pl.ds(c * part, part)

        def to_core(k, c):
            return remote(
                other[k].at[span(c)], from_core.at[k, span(c)],
                c_send.at[k, c], c_recv.at[k, c], seq=p.other(),
            )

        def along(k, c):
            return remote(
                total.at[k - 1, span(c)], from_x.at[k - 1, span(c)],
                x_send.at[k, c], x_recv.at[k, c], seq=p.along_x(k),
            )

        def share(k, c):
            return remote(
                mine.at[span(c)], normed_ref.at[2 * k, span(c)],
                g_send.at[k, c], g_recv.at[k, c], seq=p.along_x(-k),
            )

        def pass_on(k, c):
            return remote(
                mine.at[span(c)] if k == 0 else normed_ref.at[2 * k, span(c)],
                normed_ref.at[2 * k + 1, span(c)],
                f_send.at[k, c], f_recv.at[k, c], seq=p.other(),
            )

        far = range(1, chips)
        for k in [*far, 0]:
            for c in range(CHUNKS):
                to_core(k, c).start()
        for c in range(CHUNKS):
            for k in far:
                to_core(k, c).wait_recv()
                both = own[k][span(c)].astype(F32) + from_core[k, span(c)].astype(F32)
                total[k - 1, span(c)] = both.astype(BF16)
                along(k, c).start()
        carried.start()
        carry_here = pltpu.make_async_copy(carry_ref, carried.slot(p.fsdp), here.at[1])
        carry_here.start()
        for c in range(CHUNKS):
            to_core(0, c).wait_recv()
            rows_here = own[0][span(c)].astype(F32) + from_core[0, span(c)].astype(F32)
            for k in far:
                along(k, c).wait_recv()
                rows_here = rows_here + from_x[k - 1, span(c)].astype(F32)
            rows_here = rows_here + res_ref[span(c)].astype(F32)
            hidden_ref[span(c)] = rows_here
            unit = rows_here - jnp.mean(rows_here, axis=1, keepdims=True)
            unit = unit * lax.rsqrt(jnp.mean(unit * unit, axis=1, keepdims=True) + epsilon)
            mine[span(c)] = (unit * gain_ref[0:1, :] + bias_ref[0:1, :]).astype(BF16)
            for k in far:
                share(k, c).start()
            pass_on(0, c).start()
            if c % 2 == 1 and c // 2 + 1 < deep:
                carried.pass_on(c // 2 + 1)
        keep = pltpu.make_async_copy(mine, normed_ref.at[0], here.at[0])
        keep.start()
        for c in range(CHUNKS):
            for k in far:
                share(k, c).wait_recv()
                pass_on(k, c).start()
            if c == 1:
                for d in range(CHUNKS // 2 + 1, deep):
                    carried.pass_on(d)
        for c in range(CHUNKS):
            for k in range(chips):
                to_core(k, c).wait_send()
                pass_on(k, c).wait()
            for k in far:
                along(k, c).wait_send()
                share(k, c).wait_send()
        keep.wait()
        carried.finish()
        carry_here.wait()

    vmem = pl.BlockSpec(memory_space=pltpu.VMEM)
    any_space = pl.BlockSpec(memory_space=pl.ANY)
    block = (rows, width)
    several = (max(chips - 1, 1),) + block
    return pl.pallas_call(
        kernel,
        in_specs=[vmem] * (2 * chips + 4),
        out_specs=[vmem, any_space, any_space],
        out_shape=[
            jax.ShapeDtypeStruct(block, F32),
            jax.ShapeDtypeStruct((2 * chips,) + block, BF16),
            jax.ShapeDtypeStruct((carry.shape[0] * fsdp_size, carry.shape[1]), BF16),
        ],
        scratch_shapes=[
            pltpu.VMEM((chips,) + block, BF16),
            pltpu.VMEM(several, BF16),
            pltpu.VMEM(several, BF16),
            pltpu.VMEM(block, BF16),
        ]
        + [dma((chips, CHUNKS))] * 8
        + [dma((2,))]
        + fsdp_sems(deep, fsdp_size // deep),
        compiler_params=talking(2),
        name="hidden_rows",
    )(
        *[value for pair in parts for value in pair],
        residual,
        jnp.broadcast_to(gain[None], (8, width)),
        jnp.broadcast_to(bias[None], (8, width)),
        carry,
    )


def closing_rows(parts, arriving, base, prior, gain, seq_size, fsdp_size, low, collective_id):
    rows, width = base.shape
    chips = seq_size // CORES
    held = len(parts)
    part = rows // CHUNKS
    dma = pltpu.SemaphoreType.DMA
    far = range(1, held)

    def kernel(*refs):
        own, other = refs[0 : 2 * held : 2], refs[1 : 2 * held : 2]
        refs = refs[2 * held :]
        came, refs = refs[: len(arriving)], refs[len(arriving) :]
        base_ref, prior_ref, gain_ref, grad_ref = refs[:4]
        refs = refs[4:]
        if low:
            low_ref, refs = refs[0], refs[1:]
        sums_ref, from_core, total, from_x, c_send, c_recv, x_send, x_recv = refs
        p = Place(seq_size, fsdp_size)
        greet(p, False)

        def span(c):
            return pl.ds(c * part, part)

        def to_core(k, c):
            return remote(
                other[k].at[span(c)], from_core.at[k, span(c)],
                c_send.at[k, c], c_recv.at[k, c], seq=p.other(),
            )

        def along(k, c):
            return remote(
                total.at[k - 1, span(c)], from_x.at[k - 1, span(c)],
                x_send.at[k, c], x_recv.at[k, c], seq=p.along_x(k),
            )

        for k in [*far, 0]:
            for c in range(CHUNKS):
                to_core(k, c).start()
        for c in range(CHUNKS):
            for k in far:
                to_core(k, c).wait_recv()
                both = own[k][span(c)].astype(F32) + from_core[k, span(c)].astype(F32)
                total[k - 1, span(c)] = both.astype(BF16)
                along(k, c).start()
        gained = jnp.zeros((1, width), F32)
        biased = jnp.zeros((1, width), F32)
        for c in range(CHUNKS):
            to_core(0, c).wait_recv()
            gradient = own[0][span(c)].astype(F32) + from_core[0, span(c)].astype(F32)
            for k in far:
                along(k, c).wait_recv()
                gradient = gradient + from_x[k - 1, span(c)].astype(F32)
            for ref in came:
                gradient = gradient + ref[span(c)].astype(F32)
            unit = base_ref[span(c)].astype(F32)
            unit = unit - jnp.mean(unit, axis=1, keepdims=True)
            inverse = lax.rsqrt(jnp.mean(unit * unit, axis=1, keepdims=True) + epsilon)
            unit = unit * inverse
            gained = gained + jnp.sum(gradient * unit, axis=0, keepdims=True)
            biased = biased + jnp.sum(gradient, axis=0, keepdims=True)
            scaled = gradient * gain_ref[0:1, :]
            middle = jnp.mean(scaled, axis=1, keepdims=True)
            tilt = jnp.mean(scaled * unit, axis=1, keepdims=True)
            result = prior_ref[span(c)].astype(F32) + inverse * (scaled - middle - unit * tilt)
            grad_ref[span(c)] = result
            if low:
                low_ref[span(c)] = result.astype(BF16)
        which = lax.broadcasted_iota(jnp.int32, (8, width), 0)
        sums_ref[...] = jnp.where(which == 0, gained, jnp.where(which == 1, biased, 0.0))
        for c in range(CHUNKS):
            for k in range(held):
                to_core(k, c).wait_send()
            for k in far:
                along(k, c).wait_send()

    vmem = pl.BlockSpec(memory_space=pltpu.VMEM)
    block = (rows, width)
    several = (max(held - 1, 1),) + (block if held > 1 else (8, LANES))
    kinds = [(block, F32)] + ([(block, BF16)] if low else []) + [((8, width), F32)]
    operands = [value for pair in parts for value in pair] + list(arriving)
    operands += [base, prior, jnp.broadcast_to(gain[None], (8, width))]
    return pl.pallas_call(
        kernel,
        in_specs=[vmem] * len(operands),
        out_specs=[vmem] * len(kinds),
        out_shape=[jax.ShapeDtypeStruct(*kind) for kind in kinds],
        scratch_shapes=[
            pltpu.VMEM((held,) + block, BF16),
            pltpu.VMEM(several, BF16),
            pltpu.VMEM(several, BF16),
        ]
        + [dma((held, CHUNKS))] * 4,
        compiler_params=talking(collective_id),
        name="closing_rows",
    )(*operands)


class SeqShare:
    def __init__(self, place, piece, whole, sems, number):
        self.place, self.piece, self.whole = place, piece, whole
        self.x_send, self.x_recv, self.c_send, self.c_recv, self.here = (
            [sem.at[number] for sem in sems]
        )

    def x(self, k):
        p = self.place
        return remote(
            self.piece, self.whole.at[p.seq], self.x_send.at[k], self.x_recv.at[k],
            seq=p.along_x(k),
        )

    def core(self, k):
        p = self.place
        slot = self.whole.at[p.along_x(-k)]
        return remote(
            self.piece if k == 0 else slot, slot, self.c_send.at[k], self.c_recv.at[k],
            seq=p.other(),
        )

    def keep(self):
        return pltpu.make_async_copy(self.piece, self.whole.at[self.place.seq], self.here)

    def start(self):
        for k in range(1, self.place.chips):
            self.x(k).start()
        self.core(0).start()
        self.keep().start()

    def finish(self):
        for k in range(1, self.place.chips):
            self.x(k).wait_recv()
            self.core(k).start()
        for k in range(self.place.chips):
            self.core(k).wait()
        for k in range(1, self.place.chips):
            self.x(k).wait_send()
        self.keep().wait()


def share_sems(chips, count):
    dma = pltpu.SemaphoreType.DMA
    return [dma((count, chips))] * 4 + [dma((count,))]


def share_pieces(pieces, seq_size, fsdp_size, collective_id):
    chips = seq_size // CORES
    count = len(pieces)

    def kernel(*refs):
        ins, outs, sems = refs[:count], refs[count : 2 * count], refs[2 * count :]
        p = Place(seq_size, fsdp_size)
        greet(p, False)
        shares = [SeqShare(p, ins[i], outs[i], sems, i) for i in range(count)]
        for share in shares:
            share.start()
        for share in shares:
            share.finish()

    return pl.pallas_call(
        kernel,
        in_specs=[pl.BlockSpec(memory_space=pltpu.VMEM)] * count,
        out_specs=[pl.BlockSpec(memory_space=pl.ANY)] * count,
        out_shape=[jax.ShapeDtypeStruct((seq_size,) + v.shape, v.dtype) for v in pieces],
        scratch_shapes=share_sems(chips, count),
        compiler_params=talking(collective_id),
        name="share_pieces",
    )(*pieces)


def sum_and_share(partial, vectors, pieces, seq_size, fsdp_size, collective_id):
    chips = seq_size // CORES
    deep = planes(fsdp_size)
    across = fsdp_size // deep
    rows, width = partial.shape[0] // fsdp_size, partial.shape[1]
    lanes = vectors.shape[1] // fsdp_size
    count = len(pieces) + 1
    dma = pltpu.SemaphoreType.DMA

    def kernel(part_ref, vec_ref, *refs):
        ins, refs = refs[: count - 1], refs[count - 1 :]
        outs, refs = refs[:count], refs[count:]
        (
            vec_out, from_y, over_y, from_z, piece, vec_cut, vec_f, vec_s, vec_sum,
            y_send, y_recv, z_send, z_recv, f_send, f_recv, s_send, s_recv,
        ) = refs[:17]
        sems = refs[17:]
        p = Place(seq_size, fsdp_size)
        greet_all(p)

        def block(z, y):
            return pl.ds(pl.multiple_of((z * across + y) * rows, rows), rows)

        def to_y(z, k):
            return remote(
                part_ref.at[block(z, (p.y + k) % across)], from_y.at[k, z],
                y_send.at[k, z], y_recv.at[k, z], fsdp=p.along_y(k),
            )

        def to_z(k):
            return remote(
                over_y.at[(p.z + k) % deep], from_z.at[k],
                z_send.at[k], z_recv.at[k], fsdp=p.along_z(k),
            )

        def vec_to(k):
            return remote(
                vec_cut.at[(p.fsdp + k) % fsdp_size], vec_f.at[k],
                f_send.at[k], f_recv.at[k], fsdp=(p.fsdp + k) % fsdp_size,
            )

        def vec_over(k):
            return remote(
                vec_sum, vec_s.at[k], s_send.at[k], s_recv.at[k], seq=(p.seq + k) % seq_size
            )

        for f in range(fsdp_size):
            vec_cut[f] = vec_ref[:, f * lanes : (f + 1) * lanes]
        for k in range(1, fsdp_size):
            vec_to(k).start()
        for z in range(deep):
            for k in range(1, across):
                to_y(z, k).start()
        shares = [SeqShare(p, ins[i], outs[i], sems, i) for i in range(count - 1)]
        for share in shares:
            share.start()
        for z in range(deep):
            total = part_ref[block(z, p.y)].astype(F32)
            for k in range(1, across):
                to_y(z, k).wait_recv()
                total = total + from_y[k, z].astype(F32)
            over_y[z] = total.astype(BF16)
        for k in range(1, deep):
            to_z(k).start()
        vec_total = vec_cut[p.fsdp]
        for k in range(1, fsdp_size):
            vec_to(k).wait_recv()
            vec_total = vec_total + vec_f[k]
        vec_sum[...] = vec_total
        for k in range(1, seq_size):
            vec_over(k).start()
        total = over_y[p.z].astype(F32)
        for k in range(1, deep):
            to_z(k).wait_recv()
            total = total + from_z[k].astype(F32)
        piece[...] = total.astype(BF16)
        shares.append(SeqShare(p, piece, outs[-1], sems, count - 1))
        shares[-1].start()
        for k in range(1, seq_size):
            vec_over(k).wait_recv()
            vec_total = vec_total + vec_s[k]
        vec_out[...] = vec_total
        for share in shares:
            share.finish()
        for z in range(deep):
            for k in range(1, across):
                to_y(z, k).wait_send()
        for k in range(1, deep):
            to_z(k).wait_send()
        for k in range(1, fsdp_size):
            vec_to(k).wait_send()
        for k in range(1, seq_size):
            vec_over(k).wait_send()

    vmem = pl.BlockSpec(memory_space=pltpu.VMEM)
    shapes = [v.shape for v in pieces] + [(rows, width)]
    cut = (8, lanes)
    return pl.pallas_call(
        kernel,
        in_specs=[vmem] * (count + 1),
        out_specs=[pl.BlockSpec(memory_space=pl.ANY)] * count + [vmem],
        out_shape=[jax.ShapeDtypeStruct((seq_size,) + shape, BF16) for shape in shapes]
        + [jax.ShapeDtypeStruct(cut, F32)],
        scratch_shapes=[
            pltpu.VMEM((across, deep, rows, width), BF16),
            pltpu.VMEM((deep, rows, width), BF16),
            pltpu.VMEM((deep, rows, width), BF16),
            pltpu.VMEM((rows, width), BF16),
            pltpu.VMEM((fsdp_size,) + cut, F32),
            pltpu.VMEM((fsdp_size,) + cut, F32),
            pltpu.VMEM((seq_size,) + cut, F32),
            pltpu.VMEM(cut, F32),
        ]
        + [dma((across, deep))] * 2
        + [dma((deep,))] * 2
        + [dma((fsdp_size,))] * 2
        + [dma((seq_size,))] * 2
        + share_sems(chips, count),
        compiler_params=talking(collective_id),
        name="sum_and_share",
    )(partial, vectors, *pieces)


def own_columns(gate, up, me, seq_size, fsdp_size):
    rows, columns = gate.shape
    shard = columns // fsdp_size
    chunk = shard // seq_size

    def kernel(me_ref, gate_ref, up_ref, out_ref):
        for s in range(seq_size):

            @pl.when(me_ref[0] == s)
            def _(s=s):
                for which, ref in enumerate((gate_ref, up_ref)):
                    taken = [
                        ref[:, f * shard + s * chunk : f * shard + (s + 1) * chunk]
                        for f in range(fsdp_size)
                    ]
                    at = which * chunk * fsdp_size
                    out_ref[:, at : at + chunk * fsdp_size] = jnp.concatenate(taken, axis=1)

    return pl.pallas_call(
        kernel,
        grid_spec=pltpu.PrefetchScalarGridSpec(
            num_scalar_prefetch=1,
            grid=(1,),
            in_specs=[pl.BlockSpec((rows, columns), lambda i, m: (0, 0))] * 2,
            out_specs=pl.BlockSpec((rows, 2 * chunk * fsdp_size), lambda i, m: (0, 0)),
        ),
        out_shape=jax.ShapeDtypeStruct((rows, 2 * chunk * fsdp_size), BF16),
        compiler_params=params(),
        cost_estimate=cost(rows, 1, 2 * columns),
        name="own_columns",
    )(jnp.full((1,), me, jnp.int32), gate, up)


def whole_columns(pieces, fsdp_size):
    seq_size, rows, columns = pieces.shape
    units = columns // 2
    chunk = units // fsdp_size

    def kernel(in_ref, gate_ref, up_ref):
        for which, ref in enumerate((gate_ref, up_ref)):
            for f in range(fsdp_size):
                at = which * units + f * chunk
                taken = [in_ref[s, :, at : at + chunk].astype(F32) for s in range(seq_size)]
                whole = jnp.concatenate(taken, axis=1)
                ref[:, f * chunk * seq_size : (f + 1) * chunk * seq_size] = whole

    tile = rows // 4
    out = pl.BlockSpec((tile, units * seq_size), lambda i: (i, 0))
    return pl.pallas_call(
        kernel,
        grid=(4,),
        in_specs=[pl.BlockSpec((seq_size, tile, columns), lambda i: (0, i, 0))],
        out_specs=[out, out],
        out_shape=[jax.ShapeDtypeStruct((rows, units * seq_size), F32)] * 2,
        compiler_params=params(),
        cost_estimate=cost(rows, 1, 2 * columns * seq_size),
        name="whole_columns",
    )(pieces)


def own_heads_spread(project_in, me, pairs, seq_size):
    rows, columns = project_in.shape
    every = columns // 3 // LANES
    step = seq_size // 2

    def kernel(me_ref, low_ref, high_ref, out_ref):
        lane = lax.broadcasted_iota(jnp.int32, (rows, LANES), 1)
        odd = me_ref[0] % 2 == 1
        first = low_ref[...].astype(F32)
        second = high_ref[...].astype(F32)
        first = jnp.where(odd, pltpu.roll(first, HEAD_DIM, 1), first)
        second = jnp.where(odd, second, pltpu.roll(second, HEAD_DIM, 1))
        out_ref[...] = jnp.where(lane < HEAD_DIM, first, second).astype(BF16)

    def source(ahead):
        return pl.BlockSpec(
            (rows, LANES),
            lambda part, p, m: (0, part * every + (2 * p + ahead) * step + m[0] // 2),
        )

    return pl.pallas_call(
        kernel,
        grid_spec=pltpu.PrefetchScalarGridSpec(
            num_scalar_prefetch=1,
            grid=(3, pairs),
            in_specs=[source(0), source(1)],
            out_specs=pl.BlockSpec((rows, LANES), lambda part, p, m: (0, 3 * p + part)),
        ),
        out_shape=jax.ShapeDtypeStruct((rows, 3 * pairs * LANES), BF16),
        compiler_params=params(),
        name="own_heads",
    )(jnp.full((1,), me, jnp.int32), project_in, project_in)


def whole_heads_spread(pieces):
    seq_size, rows, columns = pieces.shape
    each = columns * seq_size // 3
    step = seq_size // 2

    def kernel(in_ref, out_ref):
        lane = lax.broadcasted_iota(jnp.int32, (rows // 4, LANES), 1)
        for part in range(3):
            for b in range(each // LANES):
                shard, seq = b // step, 2 * (b % step)
                at = (3 * (shard // 2) + part) * LANES
                first = in_ref[seq, :, at : at + LANES].astype(F32)
                second = in_ref[seq + 1, :, at : at + LANES].astype(F32)
                if shard % 2:
                    first = pltpu.roll(first, HEAD_DIM, 1)
                else:
                    second = pltpu.roll(second, HEAD_DIM, 1)
                start = part * each + b * LANES
                out_ref[:, start : start + LANES] = jnp.where(lane < HEAD_DIM, first, second)

    return pl.pallas_call(
        kernel,
        grid=(4,),
        in_specs=[pl.BlockSpec((seq_size, rows // 4, columns), lambda i: (0, i, 0))],
        out_specs=pl.BlockSpec((rows // 4, 3 * each), lambda i: (i, 0)),
        out_shape=jax.ShapeDtypeStruct((rows, 3 * each), F32),
        compiler_params=params(),
        cost_estimate=cost(rows, 1, 3 * each),
        name="whole_heads",
    )(pieces)


def gather_fsdp(value):
    return lax.all_gather(value, "fsdp", axis=0, tiled=True)


def scatter_fsdp(value):
    return lax.psum_scatter(value, "fsdp", scatter_dimension=0, tiled=True)


def local(
    tokens,
    cont_lengths,
    project_in,
    project_out,
    gate_weight,
    up_weight,
    down_weight,
    first_gain,
    first_bias,
    second_gain,
    second_bias,
    grad_output,
):
    rows_dev, width = tokens.shape[1:]
    seq_size = lax.axis_size("seq")
    fsdp_size = lax.axis_size("fsdp")
    chips = seq_size // CORES
    total_rows = rows_dev * seq_size
    me = lax.axis_index("seq")
    order = seq_order(chips)
    shard_rows = project_in.shape[0]
    own_pairs = width // LANES // seq_size
    pieces_out = project_out.shape[0] // seq_size
    pieces_down = down_weight.shape[0] // seq_size
    far = range(1, chips)

    spread = pieces_out == HEAD_DIM
    if spread:
        in_part = own_heads_spread(project_in, me, own_pairs, seq_size)
    else:
        in_part = own_heads(project_in, me, own_pairs)
    vectors = jnp.stack([first_gain, first_bias, second_gain, second_bias]).astype(F32)
    all_tokens, w_in, vectors = opening(
        tokens[0],
        in_part,
        jnp.concatenate([vectors, vectors]),
        seq_size,
        fsdp_size,
    )
    down_late, out_late = tie((down_weight, project_out), w_in)
    if spread:
        w_out = gather_fsdp(lax.dynamic_slice_in_dim(out_late, me * pieces_out, pieces_out, 0))
    else:
        own_rows = width // seq_size
        w_out = lax.dynamic_slice_in_dim(gather_fsdp(project_out), me * own_rows, own_rows, 0)
    vectors = jnp.transpose(vectors[:, :4], (1, 0, 2)).reshape(4, width)
    gain_one, bias_one, gain_two, bias_two = [vectors[i] for i in range(4)]
    upstream_own = tie(grad_output[0], all_tokens)
    upstream_far = [from_chip(upstream_own, chips, ahead) for ahead in far]
    w_down = gather_fsdp(lax.dynamic_slice_in_dim(down_late, me * pieces_down, pieces_down, 0))
    gate_up_part = own_columns(gate_weight, up_weight, me, seq_size, fsdp_size)

    cosine, sine, ends = rope_tables(cont_lengths[0], total_rows)

    qkv, normed_first = project(all_tokens, w_in, gain_one, bias_one, cosine, sine)
    attended, qx = attend(ends, qkv)
    upstream_blocks = [grad_output[0], core_swap(grad_output[0], chips)]
    for block in upstream_far:
        block = tie(block, attended)
        upstream_blocks += [block, core_swap(block, chips)]

    def scatter_end(started):
        arriving, own, other, _ = started
        total = own.astype(F32) + other.astype(F32)
        for part in arriving:
            total = total + part.astype(F32)
        return total

    attended = tie(attended, upstream_blocks)
    parts = chip_matmul(attended, w_out, order, rows_dev, False, "attention_out")
    hidden, normed_blocks, w_gate_up = hidden_rows(
        parts, tokens[0], gain_two, bias_two, gate_up_part, seq_size, fsdp_size
    )
    product, grads, normed_second, upstream_all = feed(
        normed_blocks, upstream_blocks, w_gate_up, w_down
    )

    near_order = jnp.arange(chips * CORES, dtype=jnp.int32)

    def send_far(x, weight, x_order, name):
        sent = [
            (own.astype(F32) + core_swap(other, chips).astype(F32)).astype(BF16)
            for own, other in chip_matmul(x, weight, x_order[CORES:], rows_dev, True, name)
        ]
        return sent, [to_chip(value, chips, ahead) for value, ahead in zip(sent, far)]

    sent, arriving = send_far(grads, w_gate_up, near_order, "feed_back")
    own, other, grad_down = near_and_grad(
        tie(grads, *sent), w_gate_up, near_order[:CORES], product, upstream_all, rows_dev,
        "near_and_down",
    )
    grad_hidden, low_own, sums_two = closing_rows(
        [(own, other)], tie(arriving, grad_down), hidden, grad_output[0], gain_two,
        seq_size, fsdp_size, True, 3,
    )
    low_far = [from_chip(low_own, chips, ahead) for ahead in far]
    low_near = [low_own, core_swap(low_own, chips)]

    normed_late, product_late = tie((normed_second, product), low_own)
    grad_gate_up = weight_grad(normed_late, grads, "grad_gate_up")
    product_late = tie(product_late, grad_gate_up)

    layer_parts = chip_matmul(product_late, w_down, near_order, rows_dev, False, "feed_down")
    (layer_own, layer_other), layer_far = layer_parts[0], layer_parts[1:]
    low_far = tie(low_far, layer_own)
    layer_far = tie(layer_far, low_far)
    grad_down_piece = scatter_fsdp(tie(grad_down, arriving))
    grad_gate_up_piece = scatter_fsdp(tie(grad_gate_up, low_far))
    low_blocks = low_near
    for block in low_far:
        low_blocks = low_blocks + [block, core_swap(block, chips)]
    layer_sent = [
        (own.astype(F32) + core_swap(other, chips).astype(F32)).astype(BF16)
        for own, other in layer_far
    ]
    layer_arriving = [to_chip(s, chips, ahead) for s, ahead in zip(layer_sent, far)]
    grad_attended, low_hidden = blocks_matmul(low_blocks, w_out, order)
    grad_out = dot_first(attended, low_hidden).astype(BF16)
    grad_attended = tie(grad_attended, grad_out, layer_sent)

    grad_qkv = attend_back(ends, qkv, qx, grad_attended, attended, cosine, sine)
    grad_qkv = tie(grad_qkv, layer_arriving)
    sent, arriving = send_far(grad_qkv, w_in, order, "project_back")
    grad_late = tie(grad_qkv, *sent)
    own, other, grad_in = near_and_grad(
        grad_late, w_in, order[:CORES], normed_first, grad_late, rows_dev, "near_and_project_in"
    )
    arriving = tie(arriving, grad_in)
    grad_in_piece = scatter_fsdp(tie(grad_in, arriving))
    input_gradient, sums_one = closing_rows(
        [(own, other)], arriving, tokens[0], grad_hidden, gain_one,
        seq_size, fsdp_size, False, 4,
    )
    layer_rows = hidden + scatter_end(
        (layer_arriving, layer_own, core_swap(layer_other, chips), None)
    )

    sums = jnp.concatenate([sums_one[:2], sums_two[:2], sums_one[2:6]])
    all_gate_up, all_down, all_out, sums = sum_and_share(
        grad_out, sums, [grad_gate_up_piece, grad_down_piece], seq_size, fsdp_size, 5
    )
    (all_in,) = share_pieces([tie(grad_in_piece, all_out)], seq_size, fsdp_size, 6)
    if spread:
        grad_in = whole_heads_spread(all_in)
        grad_out = all_out.reshape(project_out.shape).astype(F32)
    else:
        grad_in = all_in.reshape(seq_size, shard_rows, own_pairs, 3, LANES)
        grad_in = jnp.transpose(grad_in, (1, 3, 0, 2, 4)).reshape(shard_rows, 3 * width)
        grad_in = grad_in.astype(F32)
        whole = jnp.zeros((width, width), F32)
        whole = lax.dynamic_update_slice_in_dim(
            whole, grad_out.astype(F32), me * (width // seq_size), 0
        )
        grad_out = lax.psum(scatter_fsdp(whole), "seq")
    grad_gate, grad_up = whole_columns(all_gate_up, fsdp_size)
    return (
        layer_rows.astype(BF16)[None],
        input_gradient[None],
        grad_in,
        grad_out,
        grad_gate,
        grad_up,
        all_down.reshape(down_weight.shape).astype(F32),
        sums[0],
        sums[1],
        sums[2],
        sums[3],
    )


def solution(mesh):
    return jax.shard_map(
        local,
        mesh=mesh,
        in_specs=(
            P("fsdp", "seq", None),
            P("fsdp", None),
            P("fsdp", None),
            P("fsdp", None),
            P("fsdp", None),
            P("fsdp", None),
            P("fsdp", None),
            P("fsdp"),
            P("fsdp"),
            P("fsdp"),
            P("fsdp"),
            P("fsdp", "seq", None),
        ),
        out_specs=(
            P("fsdp", "seq", None),
            P("fsdp", "seq", None),
            P("fsdp", None),
            P("fsdp", None),
            P("fsdp", None),
            P("fsdp", None),
            P("fsdp", None),
            P("fsdp"),
            P("fsdp"),
            P("fsdp"),
            P("fsdp"),
        ),
        check_vma=False,
    )
```

```python
import functools

import jax
import jax.numpy as jnp
from jax import lax
from jax.experimental import pallas as pl
from jax.experimental.pallas import tpu as pltpu
from jax.sharding import PartitionSpec as P

HEAD_DIM = 64
ROT = 16
PROMPT = 2048
LANES = 128

epsilon = 1e-05
rope_base = 10000.0

BF16 = jnp.bfloat16
F32 = jnp.float32
CORES = 2
VMEM_LIMIT = 56 * 1024 * 1024


def dot_last(left_side, right_side):
    return lax.dot_general(
        left_side, right_side, (((1,), (1,)), ((), ())), preferred_element_type=F32
    )


def dot_first(left_side, right_side):
    return lax.dot_general(
        left_side, right_side, (((0,), (0,)), ((), ())), preferred_element_type=F32
    )


def dot(left_side, right_side):
    return jnp.dot(left_side, right_side, preferred_element_type=F32)


def cont_ends(lengths):
    count = lengths.shape[0]
    before = jnp.arange(count)[None, :] <= jnp.arange(count)[:, None]
    return jnp.sum(jnp.where(before, lengths[None, :], 0), axis=1)


def rope_tables(lengths, total_rows):
    ends = cont_ends(lengths)
    starts = ends - lengths
    indices = jnp.arange(total_rows, dtype=jnp.int32)
    offset = indices - PROMPT
    inside = (offset[:, None] >= starts[None, :]) & (offset[:, None] < ends[None, :])
    seg_begin = jnp.sum(jnp.where(inside, starts[None, :], 0), axis=1)
    position = jnp.where(indices < PROMPT, indices, PROMPT + offset - seg_begin)
    half = ROT // 2
    within = jnp.arange(LANES, dtype=jnp.int32) % HEAD_DIM
    frequency = rope_base ** (-2.0 * (within % half).astype(F32) / ROT)
    angles = position.astype(F32)[:, None] * frequency[None, :]
    turning = (within < ROT)[None, :]
    sign = jnp.where(within < half, -1.0, 1.0)[None, :]
    cosine = jnp.where(turning, jnp.cos(angles), 1.0)
    sine = jnp.where(turning, sign * jnp.sin(angles), 0.0)
    return cosine, sine, ends


def turn(rows_in, cosine, sine):
    half = ROT // 2
    lane = lax.broadcasted_iota(jnp.int32, rows_in.shape, 1) % HEAD_DIM
    partner = jnp.where(
        lane < half,
        pltpu.roll(rows_in, LANES - half, 1),
        pltpu.roll(rows_in, half, 1),
    )
    return rows_in * cosine + partner * sine


def project_kernel(x_ref, w_ref, gain_ref, bias_ref, cos_ref, sin_ref, out_ref, normed_ref):
    cosine = cos_ref[...]
    sine = sin_ref[...]
    pairs = out_ref.shape[1] // (3 * LANES)
    x = x_ref[...].astype(F32)
    x = x - jnp.mean(x, axis=1, keepdims=True)
    x = x * lax.rsqrt(jnp.mean(x * x, axis=1, keepdims=True) + epsilon)
    x = (x * gain_ref[0:1, :] + bias_ref[0:1, :]).astype(BF16)
    normed_ref[...] = x
    for first in range(0, pairs, 2):
        begin = 3 * LANES * first
        mixed = dot(x, w_ref[:, begin : begin + 6 * LANES])
        for pair in range(2):
            base = 3 * LANES * pair
            query = turn(mixed[:, base : base + LANES], cosine, sine) * HEAD_DIM ** (-0.5)
            key = turn(mixed[:, base + LANES : base + 2 * LANES], cosine, sine)
            value = mixed[:, base + 2 * LANES : base + 3 * LANES]
            base = base + begin
            out_ref[:, base : base + LANES] = query.astype(BF16)
            out_ref[:, base + LANES : base + 2 * LANES] = key.astype(BF16)
            out_ref[:, base + 2 * LANES : base + 3 * LANES] = value.astype(BF16)


def project(x, weight, gain, bias, cosine, sine):
    rows, depth = x.shape
    columns = weight.shape[1]
    block = 512
    vector = pl.BlockSpec((8, depth), lambda i: (0, 0))
    return pl.pallas_call(
        project_kernel,
        grid=(rows // block,),
        in_specs=[
            pl.BlockSpec((block, depth), lambda i: (i, 0)),
            pl.BlockSpec((depth, columns), lambda i: (0, 0), pipeline_mode=pl.Buffered(1)),
            vector,
            vector,
            pl.BlockSpec((block, LANES), lambda i: (i, 0)),
            pl.BlockSpec((block, LANES), lambda i: (i, 0)),
        ],
        out_specs=[
            pl.BlockSpec((block, columns), lambda i: (i, 0)),
            pl.BlockSpec((block, depth), lambda i: (i, 0)),
        ],
        out_shape=[
            jax.ShapeDtypeStruct((rows, columns), BF16),
            jax.ShapeDtypeStruct((rows, depth), BF16),
        ],
        compiler_params=pltpu.CompilerParams(vmem_limit_bytes=VMEM_LIMIT),
        cost_estimate=pl.CostEstimate(
            flops=2 * rows * depth * columns,
            bytes_accessed=2 * (rows * depth + depth * columns + rows * columns),
            transcendentals=0,
        ),
        name="project_in_rope",
    )(
        x,
        weight,
        jnp.broadcast_to(gain[None], (8, depth)),
        jnp.broadcast_to(bias[None], (8, depth)),
        cosine,
        sine,
    )


BLOCK = 512
NEG = -1e30


def segment_of(index, ends_ref):
    count = jnp.zeros_like(index)
    for c in range(ends_ref.shape[0] - 1):
        count = count + (index >= PROMPT + ends_ref[c]).astype(jnp.int32)
    return count


def attend_kernel(ends_ref, *refs):
    held = len(refs) // 3
    q_refs, k_refs, v_refs = refs[:held], refs[held : 2 * held], refs[2 * held : 3 * held]
    o_ref, qx_ref = refs[3 * held :]
    rows = k_refs[0].shape[0]
    lane = lax.broadcasted_iota(jnp.int32, (BLOCK, LANES), 1)
    inside = [lane < HEAD_DIM, lane >= HEAD_DIM]

    def one_block(number):
        start = number * BLOCK
        end = start + BLOCK
        full = min(start, PROMPT)
        row = lax.broadcasted_iota(jnp.int32, (BLOCK, 1), 0) + start
        col = lax.broadcasted_iota(jnp.int32, (1, end - full), 1) + full
        visible = col <= row
        if end > PROMPT:
            visible = visible & (segment_of(row, ends_ref) == segment_of(col, ends_ref))
        for pair in range(held):
            q = q_refs[pair][...]
            outs = []
            for h in range(2):
                q_head = jnp.where(inside[h], q, jnp.zeros_like(q))
                v = v_refs[pair][:end, :]
                lane_v = lax.broadcasted_iota(jnp.int32, v.shape, 1)
                own_v = (lane_v < HEAD_DIM) if h == 0 else (lane_v >= HEAD_DIM)
                v_one = jnp.where(own_v, v, jnp.ones_like(v))
                near = dot_last(q_head, k_refs[pair][full:end, :])
                near = jnp.where(visible, near, NEG)
                peak = jnp.max(near, axis=1, keepdims=True)
                if full:
                    early = dot_last(q_head, k_refs[pair][:full, :])
                    peak = jnp.maximum(peak, jnp.max(early, axis=1, keepdims=True))
                acc = dot(jnp.exp(near - peak).astype(BF16), v_one[full:])
                if full:
                    acc = acc + dot(jnp.exp(early - peak).astype(BF16), v_one[:full])
                outs.append(acc / pltpu.roll(acc, HEAD_DIM, 1))
                minus = -(peak + jnp.log(jnp.where(inside[h], 1.0, acc)))
                high = minus.astype(BF16)
                rest = minus - high.astype(F32)
                mid = rest.astype(BF16)
                low = (rest - mid.astype(F32)).astype(BF16)
                base = HEAD_DIM * (1 - h)
                spare = jnp.where(
                    lane == base, high, jnp.where(lane == base + 1, mid, jnp.zeros_like(high))
                )
                spare = jnp.where(lane == base + 2, low, spare)
                qx_ref[2 * pair + h] = jnp.where(inside[h], q, spare)
            o_ref[:, pair * LANES : (pair + 1) * LANES] = jnp.where(
                inside[0], outs[0], outs[1]
            ).astype(BF16)

    for number in range(rows // BLOCK):
        pl.when(pl.program_id(1) == number)(functools.partial(one_block, number))


def attend(ends, qkv):
    rows, columns = qkv.shape
    pairs = columns // (3 * LANES)
    held = 2
    work = rows * rows // 2 * pairs * 2

    def part(which, height, pair):
        return pl.BlockSpec(
            (height, LANES),
            lambda p, i, e: (i if height == BLOCK else 0, 3 * (p * held + pair) + which),
        )

    return pl.pallas_call(
        attend_kernel,
        grid_spec=pltpu.PrefetchScalarGridSpec(
            num_scalar_prefetch=1,
            grid=(pairs // held, rows // BLOCK),
            in_specs=[
                part(which, BLOCK if which == 0 else rows, pair)
                for which in range(3)
                for pair in range(held)
            ],
            out_specs=[
                pl.BlockSpec((BLOCK, held * LANES), lambda p, i, e: (i, p)),
                pl.BlockSpec((2 * held, BLOCK, LANES), lambda p, i, e: (p, i, 0)),
            ],
        ),
        out_shape=[
            jax.ShapeDtypeStruct((rows, pairs * LANES), BF16),
            jax.ShapeDtypeStruct((2 * pairs, rows, LANES), BF16),
        ],
        compiler_params=pltpu.CompilerParams(vmem_limit_bytes=VMEM_LIMIT),
        cost_estimate=pl.CostEstimate(
            flops=work * 1024, bytes_accessed=2 * rows * columns, transcendentals=0
        ),
        name="attend",
    )(ends, *([qkv] * (3 * held)))


def attend_back_kernel(
    ends_ref, qx_ref, k_ref, v_ref, g_ref, o_ref, cos_ref, sin_ref, out_ref,
    gx_ref, dq_ref, dk_ref, dv_ref,
):
    number = pl.program_id(1)
    blocks = pl.num_programs(1)
    rows = qx_ref.shape[1]
    lane = lax.broadcasted_iota(jnp.int32, (BLOCK, LANES), 1)
    inside = [lane < HEAD_DIM, lane >= HEAD_DIM]

    @pl.when(number == 0)
    def _():
        dq_ref[...] = jnp.zeros_like(dq_ref)

        @pl.loop(0, rows // BLOCK)
        def _(j):
            here = pl.ds(pl.multiple_of(j * BLOCK, BLOCK), BLOCK)
            g = g_ref[here, :]
            both = g.astype(F32) * o_ref[here, :].astype(F32)
            for h in range(2):
                minus = -jnp.sum(jnp.where(inside[h], both, 0.0), axis=1, keepdims=True)
                high = minus.astype(BF16)
                rest = minus - high.astype(F32)
                mid = rest.astype(BF16)
                low = (rest - mid.astype(F32)).astype(BF16)
                base = HEAD_DIM * (1 - h)
                spare = jnp.where(
                    lane == base, high, jnp.where(lane == base + 1, mid, jnp.zeros_like(g))
                )
                spare = jnp.where(lane == base + 2, low, spare)
                gx_ref[h, here, :] = jnp.where(inside[h], g, spare)

    k = k_ref[...]
    v = v_ref[...]
    k_one = [jnp.where(inside[h], k, jnp.ones_like(k)) for h in range(2)]
    v_one = [jnp.where(inside[h], v, jnp.ones_like(v)) for h in range(2)]
    k_turned = [jnp.where(inside[h], k, jnp.zeros_like(k)).T for h in range(2)]
    dk_ref[...] = jnp.zeros_like(dk_ref)
    dv_ref[...] = jnp.zeros_like(dv_ref)

    def step(start, masked, keys=(0, BLOCK), size=BLOCK):
        here = pl.ds(start, size)
        first, end = keys
        if masked:
            row = lax.broadcasted_iota(jnp.int32, (1, size), 1) + start
            col = lax.broadcasted_iota(jnp.int32, (end - first, 1), 0) + number * BLOCK + first
            visible = (col <= row) & (segment_of(row, ends_ref) == segment_of(col, ends_ref))
        total = None
        for h in range(2):
            qx = qx_ref[h, here, :]
            gx = gx_ref[h, here, :]
            chances = jnp.exp(dot_last(k_one[h][first:end], qx))
            if masked:
                chances = jnp.where(visible, chances, 0.0)
            dv_ref[h, first:end] += dot(chances.astype(BF16), gx)
            grad_scores = (chances * dot_last(v_one[h][first:end], gx)).astype(BF16)
            dk_ref[h, first:end] += dot(grad_scores, qx)
            part = dot(k_turned[h][:, first:end], grad_scores)
            total = part if total is None else total + part
        dq_ref[:, here] += total

    half = BLOCK // 2
    step(pl.multiple_of(number * BLOCK, BLOCK), True, (0, half))
    step(pl.multiple_of(number * BLOCK + half, half), True, (half, BLOCK), half)

    @pl.loop(number + 1, blocks)
    def _(j):
        step(pl.multiple_of(j * BLOCK, BLOCK), False)

    here = pl.ds(pl.multiple_of(number * BLOCK, BLOCK), BLOCK)
    dk = jnp.where(inside[0], dk_ref[0], dk_ref[1])
    dk = turn(dk, cos_ref[here, :], -sin_ref[here, :])
    out_ref[here, LANES : 2 * LANES] = dk.astype(BF16)
    out_ref[here, 2 * LANES :] = jnp.where(inside[0], dv_ref[0], dv_ref[1]).astype(BF16)

    @pl.when(number == blocks - 1)
    def _():
        for j in range(rows // BLOCK):
            here = slice(j * BLOCK, (j + 1) * BLOCK)
            dq = dq_ref[:, here].T * HEAD_DIM ** (-0.5)
            dq = turn(dq, cos_ref[here, :], -sin_ref[here, :])
            out_ref[here, :LANES] = dq.astype(BF16)


def attend_back(ends, qkv, qx, grad, attended, cosine, sine):
    rows, columns = qkv.shape
    pairs = columns // (3 * LANES)
    blocks = rows // BLOCK
    work = rows * rows // 2 * pairs * 2
    return pl.pallas_call(
        attend_back_kernel,
        grid_spec=pltpu.PrefetchScalarGridSpec(
            num_scalar_prefetch=1,
            grid=(pairs, blocks),
            in_specs=[
                pl.BlockSpec((2, rows, LANES), lambda p, i, e: (p, 0, 0)),
                pl.BlockSpec((BLOCK, LANES), lambda p, i, e: (i, 3 * p + 1)),
                pl.BlockSpec((BLOCK, LANES), lambda p, i, e: (i, 3 * p + 2)),
                pl.BlockSpec((rows, LANES), lambda p, i, e: (0, p)),
                pl.BlockSpec((rows, LANES), lambda p, i, e: (0, p)),
                pl.BlockSpec((rows, LANES), lambda p, i, e: (0, 0)),
                pl.BlockSpec((rows, LANES), lambda p, i, e: (0, 0)),
            ],
            out_specs=pl.BlockSpec((rows, 3 * LANES), lambda p, i, e: (0, p)),
            scratch_shapes=[
                pltpu.VMEM((2, rows, LANES), BF16),
                pltpu.VMEM((LANES, rows), F32),
                pltpu.VMEM((2, BLOCK, LANES), F32),
                pltpu.VMEM((2, BLOCK, LANES), F32),
            ],
        ),
        out_shape=jax.ShapeDtypeStruct((rows, columns), BF16),
        compiler_params=pltpu.CompilerParams(vmem_limit_bytes=VMEM_LIMIT),
        cost_estimate=pl.CostEstimate(
            flops=work * 2560, bytes_accessed=2 * rows * columns, transcendentals=0
        ),
        name="attend_back",
    )(ends, qx, qkv, qkv, grad, attended, cosine, sine)


def params():
    return pltpu.CompilerParams(vmem_limit_bytes=VMEM_LIMIT)


def cost(rows, depth, columns):
    return pl.CostEstimate(
        flops=2 * rows * depth * columns,
        bytes_accessed=2 * (rows * depth + depth * columns + rows * columns),
        transcendentals=0,
    )


def chip_matmul(x, weight, order, rows, turned, name):
    depth = x.shape[1]
    columns = weight.shape[0] if turned else weight.shape[1]
    half = rows // 2
    count = order.shape[0]

    def kernel(order_ref, x_ref, w_ref, *outs):
        multiply = dot_last if turned else dot
        made = multiply(x_ref[...], w_ref[...]).astype(BF16)
        for b in range(count):

            @pl.when(pl.program_id(0) // 2 == b)
            def _(b=b):
                outs[b][...] = made

    made = pl.pallas_call(
        kernel,
        grid_spec=pltpu.PrefetchScalarGridSpec(
            num_scalar_prefetch=1,
            grid=(2 * count,),
            in_specs=[
                pl.BlockSpec((half, depth), lambda i, o: (o[i // 2] * 2 + i % 2, 0)),
                pl.BlockSpec(weight.shape, lambda i, o: (0, 0), pipeline_mode=pl.Buffered(1)),
            ],
            out_specs=[
                pl.BlockSpec((half, columns), lambda i, o, b=b: (jnp.clip(i - 2 * b, 0, 1), 0))
                for b in range(count)
            ],
        ),
        out_shape=[jax.ShapeDtypeStruct((rows, columns), BF16)] * count,
        compiler_params=params(),
        cost_estimate=cost(count * rows, depth, columns),
        name=name,
    )(order, x, weight)
    return [(made[2 * i], made[2 * i + 1]) for i in range(count // 2)]


def buffers(steps):
    return pl.Buffered(1 if steps == 1 else 2)


def weight_grad(x, g, name):
    rows, columns = g.shape
    height = x.shape[1]
    tile = 256 if height % 256 == 0 else height
    part = columns if height % 256 == 0 else 512

    def kernel(x_ref, g_ref, out_ref):
        out_ref[...] = dot_first(x_ref[...], g_ref[...]).astype(BF16)

    return pl.pallas_call(
        kernel,
        grid=(height // tile, columns // part),
        in_specs=[
            pl.BlockSpec((rows, tile), lambda i, j: (0, i), pipeline_mode=buffers(height // tile)),
            pl.BlockSpec((rows, part), lambda i, j: (0, j), pipeline_mode=buffers(columns // part)),
        ],
        out_specs=pl.BlockSpec((tile, part), lambda i, j: (i, j)),
        out_shape=jax.ShapeDtypeStruct((height, columns), BF16),
        compiler_params=params(),
        cost_estimate=cost(height, rows, columns),
        name=name,
    )(x, g)


def own_heads(project_in, me, pairs):
    rows, columns = project_in.shape
    every = columns // 3 // LANES

    def kernel(first_ref, in_ref, out_ref):
        out_ref[...] = in_ref[...]

    return pl.pallas_call(
        kernel,
        grid_spec=pltpu.PrefetchScalarGridSpec(
            num_scalar_prefetch=1,
            grid=(3, pairs),
            in_specs=[
                pl.BlockSpec((rows, LANES), lambda part, p, f: (0, part * every + f[0] + p))
            ],
            out_specs=pl.BlockSpec((rows, LANES), lambda part, p, f: (0, 3 * p + part)),
        ),
        out_shape=jax.ShapeDtypeStruct((rows, 3 * pairs * LANES), BF16),
        compiler_params=params(),
        name="own_heads",
    )(jnp.full((1,), me * pairs, jnp.int32), project_in)


def feed(normed, upstream, w_gate_up, w_down):
    count, rows, width = normed.shape
    units = w_down.shape[0]
    half = rows // 2
    total = rows * count

    def kernel(x_ref, *refs):
        ups, refs = refs[:count], refs[count:]
        wgu_ref, wd_ref, product_ref, grads_ref, normed_ref, upstream_ref = refs
        for b in range(count):

            @pl.when(pl.program_id(0) // 2 == b)
            def _(b=b):
                upstream_ref[...] = ups[b][...]

        x = x_ref[0]
        normed_ref[...] = x
        both = dot(x, wgu_ref[...])
        mid = dot_last(upstream_ref[...], wd_ref[...])
        gate = both[:, :units]
        up = both[:, units:]
        sigmoid = 1.0 / (1.0 + jnp.exp(-gate))
        silu = gate * sigmoid
        product_ref[...] = (silu * up).astype(BF16)
        slope = sigmoid * (1.0 + gate * (1.0 - sigmoid))
        grads_ref[:, :units] = (mid * up * slope).astype(BF16)
        grads_ref[:, units:] = (mid * silu).astype(BF16)

    def here(i):
        return (i, 0)

    def block_spec(b):
        return pl.BlockSpec((half, width), lambda i: (jnp.clip(i - 2 * b, 0, 1), 0))

    return pl.pallas_call(
        kernel,
        grid=(2 * count,),
        in_specs=[pl.BlockSpec((1, half, width), lambda i: (i // 2, i % 2, 0))]
        + [block_spec(b) for b in range(count)]
        + [
            pl.BlockSpec(w_gate_up.shape, lambda i: (0, 0), pipeline_mode=pl.Buffered(1)),
            pl.BlockSpec(w_down.shape, lambda i: (0, 0), pipeline_mode=pl.Buffered(1)),
        ],
        out_specs=[
            pl.BlockSpec((half, units), here),
            pl.BlockSpec((half, 2 * units), here),
            pl.BlockSpec((half, width), here),
            pl.BlockSpec((half, width), here),
        ],
        out_shape=[
            jax.ShapeDtypeStruct((total, units), BF16),
            jax.ShapeDtypeStruct((total, 2 * units), BF16),
            jax.ShapeDtypeStruct((total, width), BF16),
            jax.ShapeDtypeStruct((total, width), BF16),
        ],
        compiler_params=params(),
        cost_estimate=cost(total, 3 * width, units),
        name="feed",
    )(normed, *upstream, w_gate_up, w_down)


def near_and_grad(x, weight, order, left, right, rows, name):
    columns = x.shape[1]
    total, height = left.shape
    width = weight.shape[0]
    breadth = right.shape[1]
    half = rows // 2
    tile = 512 if breadth % 512 == 0 else 256

    def kernel(order_ref, x_ref, w_ref, left_ref, right_ref, own_ref, other_ref, out_ref):
        step = pl.program_id(0)

        @pl.when(step < 4)
        def _():
            made = dot_last(x_ref[...], w_ref[...]).astype(BF16)

            @pl.when(step < 2)
            def _():
                own_ref[...] = made

            @pl.when(step >= 2)
            def _():
                other_ref[...] = made

        @pl.when(step >= 4)
        def _():
            out_ref[...] = dot_first(left_ref[...], right_ref[...]).astype(BF16)

    def late(i):
        return jnp.maximum(i - 4, 0)

    def near(i, o):
        step = jnp.minimum(i, 3)
        return (o[step // 2] * 2 + step % 2, 0)

    return pl.pallas_call(
        kernel,
        grid_spec=pltpu.PrefetchScalarGridSpec(
            num_scalar_prefetch=1,
            grid=(4 + breadth // tile,),
            in_specs=[
                pl.BlockSpec((half, columns), near),
                pl.BlockSpec(weight.shape, lambda i, o: (0, 0), pipeline_mode=pl.Buffered(1)),
                pl.BlockSpec(left.shape, lambda i, o: (0, 0), pipeline_mode=pl.Buffered(1)),
                pl.BlockSpec((total, tile), lambda i, o: (0, late(i))),
            ],
            out_specs=[
                pl.BlockSpec((half, width), lambda i, o: (jnp.minimum(i, 1), 0)),
                pl.BlockSpec((half, width), lambda i, o: (jnp.clip(i - 2, 0, 1), 0)),
                pl.BlockSpec((height, tile), lambda i, o: (0, late(i))),
            ],
        ),
        out_shape=[
            jax.ShapeDtypeStruct((rows, width), BF16),
            jax.ShapeDtypeStruct((rows, width), BF16),
            jax.ShapeDtypeStruct((height, breadth), BF16),
        ],
        compiler_params=params(),
        cost_estimate=cost(total + rows, width, columns),
        name=name,
    )(order, x, weight, left, right)


def blocks_matmul(blocks, weight, order):
    rows, depth = blocks[0].shape
    columns = weight.shape[0]
    half = rows // 2
    count = len(blocks)

    def kernel(order_ref, *refs):
        ins, (w_ref, out_ref, copy_ref) = refs[:count], refs[count:]
        for b in range(count):

            @pl.when(pl.program_id(0) // 2 == b)
            def _(b=b):
                copy_ref[...] = ins[b][...]

        out_ref[...] = dot_last(copy_ref[...], w_ref[...]).astype(BF16)

    def block_spec(b):
        return pl.BlockSpec((half, depth), lambda i, o: (jnp.clip(i - 2 * b, 0, 1), 0))

    return pl.pallas_call(
        kernel,
        grid_spec=pltpu.PrefetchScalarGridSpec(
            num_scalar_prefetch=1,
            grid=(2 * count,),
            in_specs=[block_spec(b) for b in range(count)]
            + [pl.BlockSpec(weight.shape, lambda i, o: (0, 0), pipeline_mode=pl.Buffered(1))],
            out_specs=[
                pl.BlockSpec((half, columns), lambda i, o: (o[i // 2] * 2 + i % 2, 0)),
                pl.BlockSpec((half, depth), lambda i, o: (o[i // 2] * 2 + i % 2, 0)),
            ],
        ),
        out_shape=[
            jax.ShapeDtypeStruct((rows * count, columns), BF16),
            jax.ShapeDtypeStruct((rows * count, depth), BF16),
        ],
        compiler_params=params(),
        cost_estimate=cost(rows * count, depth, columns),
        name="grad_attended",
    )(order, *blocks, weight)


def tie(value, *others):
    return lax.optimization_barrier((value, others))[0]


def from_chip(value, chips, ahead):
    size = chips * CORES
    return lax.ppermute(value, "seq", [(i, (i - ahead * CORES) % size) for i in range(size)])


def to_chip(value, chips, ahead):
    return from_chip(value, chips, chips - ahead)


def core_swap(value, chips):
    return lax.ppermute(value, "seq", [(i, i ^ 1) for i in range(chips * CORES)])


def seq_order(chips):
    me = lax.axis_index("seq")
    core, chip = me % CORES, me // CORES
    found = []
    for ahead in range(chips):
        base = (chip + ahead) % chips * CORES
        found += [base + core, base + 1 - core]
    return jnp.stack(found).astype(jnp.int32)


def planes(size):
    return 4 if size % 4 == 0 else 1


def remote(src, dst, send, recv, **where):
    return pltpu.make_async_remote_copy(
        src_ref=src, dst_ref=dst, send_sem=send, recv_sem=recv, device_id=where,
        device_id_type=pl.DeviceIdType.MESH,
    )


def rows_at(ref, index, rows):
    return ref.at[pl.ds(pl.multiple_of(index * rows, rows), rows)]


class Place:
    def __init__(self, seq_size, fsdp_size):
        self.chips = seq_size // CORES
        self.seq_size, self.fsdp_size = seq_size, fsdp_size
        self.deep = planes(fsdp_size)
        self.across = fsdp_size // self.deep
        self.seq = lax.axis_index("seq")
        self.fsdp = lax.axis_index("fsdp")
        self.core, self.chip = self.seq % CORES, self.seq // CORES
        self.z, self.y = self.fsdp // self.across, self.fsdp % self.across

    def along_x(self, k):
        return (self.chip + k) % self.chips * CORES + self.core

    def other(self):
        return self.chip * CORES + 1 - self.core

    def along_z(self, k):
        return (self.z + k) % self.deep * self.across + self.y

    def along_y(self, k):
        return self.z * self.across + (self.y + k) % self.across

    def shard(self, kz, ky):
        return (self.z + kz) % self.deep * self.across + (self.y + ky) % self.across


def greet_device(**where):
    pl.semaphore_signal(
        pltpu.get_barrier_semaphore(),
        inc=1,
        device_id=where,
        device_id_type=pl.DeviceIdType.MESH,
    )


def greet(place, over_fsdp):
    count = place.chips
    for k in range(1, place.chips):
        greet_device(seq=place.along_x(k))
    greet_device(seq=place.other())
    if over_fsdp:
        count += place.fsdp_size - 1
        for k in range(1, place.fsdp_size):
            greet_device(fsdp=(place.fsdp + k) % place.fsdp_size)
    pl.semaphore_wait(pltpu.get_barrier_semaphore(), count)


def greet_all(place):
    for k in range(1, place.seq_size):
        greet_device(seq=(place.seq + k) % place.seq_size)
    for k in range(1, place.fsdp_size):
        greet_device(fsdp=(place.fsdp + k) % place.fsdp_size)
    count = place.seq_size + place.fsdp_size - 2
    pl.semaphore_wait(pltpu.get_barrier_semaphore(), count)


class FsdpGather:
    def __init__(self, place, own, whole, sems):
        self.place, self.own, self.whole = place, own, whole
        self.rows = own.shape[0]
        self.send_z, self.recv_z, self.send_y, self.recv_y = sems

    def slot(self, index):
        return rows_at(self.whole, index, self.rows)

    def z(self, up, d):
        p = self.place
        sign = 1 if up else -1
        slot = self.slot(p.shard(sign * (1 - d), 0))
        index = (0 if up else p.deep) + d
        return remote(
            self.own if d == 1 else slot, slot,
            self.send_z.at[index], self.recv_z.at[index], fsdp=p.along_z(sign),
        )

    def sends(self, up, d):
        z, deep = self.place.z, self.place.deep
        return (z >= d - 1) & (z + 1 < deep) if up else (z + d - 1 < deep) & (z >= 1)

    def gets(self, up, d):
        z, deep = self.place.z, self.place.deep
        return z >= d if up else z + d < deep

    def y(self, kz, ky):
        p = self.place
        slot = self.slot(p.shard(-kz, 0))
        return remote(
            self.own if kz == 0 else slot, slot,
            self.send_y.at[kz, ky], self.recv_y.at[kz, ky], fsdp=p.along_y(ky),
        )

    def start(self):
        for up in (True, False):
            pl.when(self.sends(up, 1))(lambda up=up: self.z(up, 1).start())
        for ky in range(1, self.place.across):
            self.y(0, ky).start()

    def pass_on(self, d):
        deep = self.place.deep
        for up in (True, False):

            @pl.when(self.gets(up, d))
            def _(up=up):
                self.z(up, d).wait_recv()
                for ky in range(1, self.place.across):
                    self.y(d if up else deep - d, ky).start()

            if d + 1 < deep:
                pl.when(self.sends(up, d + 1))(lambda up=up: self.z(up, d + 1).start())

    def finish(self):
        deep, across = self.place.deep, self.place.across
        for kz in range(deep):
            for ky in range(1, across):
                self.y(kz, ky).wait()
        for d in range(1, deep):
            for up in (True, False):
                pl.when(self.sends(up, d))(lambda up=up, d=d: self.z(up, d).wait_send())


def fsdp_sems(place_deep, place_across):
    return [pltpu.SemaphoreType.DMA((2 * place_deep,))] * 2 + [
        pltpu.SemaphoreType.DMA((place_deep, place_across))
    ] * 2


def opening(tokens, in_part, vectors, seq_size, fsdp_size):
    rows, width = tokens.shape
    chips = seq_size // CORES
    deep = planes(fsdp_size)
    across = fsdp_size // deep
    dma = pltpu.SemaphoreType.DMA

    def kernel(
        tok_ref, in_ref, vec_ref, tok_all, w_in, vec_all,
        here, x_send, x_recv, c_send, c_recv, v_send, v_recv, *sems,
    ):
        p = Place(seq_size, fsdp_size)
        greet(p, True)

        def tok_slot(index):
            return rows_at(tok_all, index, rows)

        def tok_x(k):
            return remote(
                tok_ref, tok_slot(p.seq), x_send.at[k], x_recv.at[k], seq=p.along_x(k)
            )

        def tok_core(k):
            slot = tok_slot(p.along_x(-k))
            return remote(
                tok_ref if k == 0 else slot, slot, c_send.at[k], c_recv.at[k], seq=p.other()
            )

        def vec(k):
            return remote(
                vec_ref, vec_all.at[p.fsdp], v_send.at[k], v_recv.at[k],
                fsdp=(p.fsdp + k) % fsdp_size,
            )

        into = FsdpGather(p, in_ref, w_in, sems)
        own = [
            pltpu.make_async_copy(tok_ref, tok_slot(p.seq), here.at[0]),
            pltpu.make_async_copy(in_ref, into.slot(p.fsdp), here.at[1]),
            pltpu.make_async_copy(vec_ref, vec_all.at[p.fsdp], here.at[2]),
        ]
        for k in range(1, fsdp_size):
            vec(k).start()
        for k in range(1, chips):
            tok_x(k).start()
        into.start()
        tok_core(0).start()
        for copy in own:
            copy.start()
        for d in range(1, deep):
            into.pass_on(d)
        for k in range(1, chips):
            tok_x(k).wait_recv()
            tok_core(k).start()
        into.finish()
        for k in range(chips):
            tok_core(k).wait()
        for k in range(1, chips):
            tok_x(k).wait_send()
        for k in range(1, fsdp_size):
            vec(k).wait()
        for copy in own:
            copy.wait()

    any_space = pl.BlockSpec(memory_space=pl.ANY)
    return pl.pallas_call(
        kernel,
        in_specs=[pl.BlockSpec(memory_space=pltpu.VMEM)] * 3,
        out_specs=[any_space] * 3,
        out_shape=[
            jax.ShapeDtypeStruct((rows * seq_size, width), BF16),
            jax.ShapeDtypeStruct((in_part.shape[0] * fsdp_size, in_part.shape[1]), BF16),
            jax.ShapeDtypeStruct((fsdp_size,) + vectors.shape, F32),
        ],
        scratch_shapes=[
            dma((3,)), dma((chips,)), dma((chips,)), dma((chips,)), dma((chips,)),
            dma((fsdp_size,)), dma((fsdp_size,)),
        ]
        + fsdp_sems(deep, across),
        compiler_params=talking(1),
        name="opening",
    )(tokens, in_part, vectors)


def talking(collective_id):
    return pltpu.CompilerParams(
        collective_id=collective_id, has_side_effects=True, vmem_limit_bytes=VMEM_LIMIT
    )


CHUNKS = 4


def hidden_rows(parts, residual, gain, bias, carry, seq_size, fsdp_size):
    rows, width = residual.shape
    chips = seq_size // CORES
    deep = planes(fsdp_size)
    part = rows // CHUNKS
    dma = pltpu.SemaphoreType.DMA

    def kernel(*refs):
        own = refs[0 : 2 * chips : 2]
        other = refs[1 : 2 * chips : 2]
        refs = refs[2 * chips :]
        res_ref, gain_ref, bias_ref, carry_ref, hidden_ref, normed_ref, carried_all = refs[:7]
        (
            from_core, total, from_x, mine,
            c_send, c_recv, x_send, x_recv, g_send, g_recv, f_send, f_recv, here,
        ) = refs[7:20]
        p = Place(seq_size, fsdp_size)
        greet(p, True)
        carried = FsdpGather(p, carry_ref, carried_all, refs[20:])

        def span(c):
            return pl.ds(c * part, part)

        def to_core(k, c):
            return remote(
                other[k].at[span(c)], from_core.at[k, span(c)],
                c_send.at[k, c], c_recv.at[k, c], seq=p.other(),
            )

        def along(k, c):
            return remote(
                total.at[k - 1, span(c)], from_x.at[k - 1, span(c)],
                x_send.at[k, c], x_recv.at[k, c], seq=p.along_x(k),
            )

        def share(k, c):
            return remote(
                mine.at[span(c)], normed_ref.at[2 * k, span(c)],
                g_send.at[k, c], g_recv.at[k, c], seq=p.along_x(-k),
            )

        def pass_on(k, c):
            return remote(
                mine.at[span(c)] if k == 0 else normed_ref.at[2 * k, span(c)],
                normed_ref.at[2 * k + 1, span(c)],
                f_send.at[k, c], f_recv.at[k, c], seq=p.other(),
            )

        far = range(1, chips)
        for k in [*far, 0]:
            for c in range(CHUNKS):
                to_core(k, c).start()
        for c in range(CHUNKS):
            for k in far:
                to_core(k, c).wait_recv()
                both = own[k][span(c)].astype(F32) + from_core[k, span(c)].astype(F32)
                total[k - 1, span(c)] = both.astype(BF16)
                along(k, c).start()
        carried.start()
        carry_here = pltpu.make_async_copy(carry_ref, carried.slot(p.fsdp), here.at[1])
        carry_here.start()
        for c in range(CHUNKS):
            to_core(0, c).wait_recv()
            rows_here = own[0][span(c)].astype(F32) + from_core[0, span(c)].astype(F32)
            for k in far:
                along(k, c).wait_recv()
                rows_here = rows_here + from_x[k - 1, span(c)].astype(F32)
            rows_here = rows_here + res_ref[span(c)].astype(F32)
            hidden_ref[span(c)] = rows_here
            unit = rows_here - jnp.mean(rows_here, axis=1, keepdims=True)
            unit = unit * lax.rsqrt(jnp.mean(unit * unit, axis=1, keepdims=True) + epsilon)
            mine[span(c)] = (unit * gain_ref[0:1, :] + bias_ref[0:1, :]).astype(BF16)
            for k in far:
                share(k, c).start()
            pass_on(0, c).start()
            if c % 2 == 1 and c // 2 + 1 < deep:
                carried.pass_on(c // 2 + 1)
        keep = pltpu.make_async_copy(mine, normed_ref.at[0], here.at[0])
        keep.start()
        for c in range(CHUNKS):
            for k in far:
                share(k, c).wait_recv()
                pass_on(k, c).start()
            if c == 1:
                for d in range(CHUNKS // 2 + 1, deep):
                    carried.pass_on(d)
        for c in range(CHUNKS):
            for k in range(chips):
                to_core(k, c).wait_send()
                pass_on(k, c).wait()
            for k in far:
                along(k, c).wait_send()
                share(k, c).wait_send()
        keep.wait()
        carried.finish()
        carry_here.wait()

    vmem = pl.BlockSpec(memory_space=pltpu.VMEM)
    any_space = pl.BlockSpec(memory_space=pl.ANY)
    block = (rows, width)
    several = (max(chips - 1, 1),) + block
    return pl.pallas_call(
        kernel,
        in_specs=[vmem] * (2 * chips + 4),
        out_specs=[vmem, any_space, any_space],
        out_shape=[
            jax.ShapeDtypeStruct(block, F32),
            jax.ShapeDtypeStruct((2 * chips,) + block, BF16),
            jax.ShapeDtypeStruct((carry.shape[0] * fsdp_size, carry.shape[1]), BF16),
        ],
        scratch_shapes=[
            pltpu.VMEM((chips,) + block, BF16),
            pltpu.VMEM(several, BF16),
            pltpu.VMEM(several, BF16),
            pltpu.VMEM(block, BF16),
        ]
        + [dma((chips, CHUNKS))] * 8
        + [dma((2,))]
        + fsdp_sems(deep, fsdp_size // deep),
        compiler_params=talking(2),
        name="hidden_rows",
    )(
        *[value for pair in parts for value in pair],
        residual,
        jnp.broadcast_to(gain[None], (8, width)),
        jnp.broadcast_to(bias[None], (8, width)),
        carry,
    )


def closing_rows(parts, arriving, base, prior, gain, seq_size, fsdp_size, low, collective_id):
    rows, width = base.shape
    chips = seq_size // CORES
    held = len(parts)
    part = rows // CHUNKS
    dma = pltpu.SemaphoreType.DMA
    far = range(1, held)

    def kernel(*refs):
        own, other = refs[0 : 2 * held : 2], refs[1 : 2 * held : 2]
        refs = refs[2 * held :]
        came, refs = refs[: len(arriving)], refs[len(arriving) :]
        base_ref, prior_ref, gain_ref, grad_ref = refs[:4]
        refs = refs[4:]
        if low:
            low_ref, refs = refs[0], refs[1:]
        sums_ref, from_core, total, from_x, c_send, c_recv, x_send, x_recv = refs
        p = Place(seq_size, fsdp_size)
        greet(p, False)

        def span(c):
            return pl.ds(c * part, part)

        def to_core(k, c):
            return remote(
                other[k].at[span(c)], from_core.at[k, span(c)],
                c_send.at[k, c], c_recv.at[k, c], seq=p.other(),
            )

        def along(k, c):
            return remote(
                total.at[k - 1, span(c)], from_x.at[k - 1, span(c)],
                x_send.at[k, c], x_recv.at[k, c], seq=p.along_x(k),
            )

        for k in [*far, 0]:
            for c in range(CHUNKS):
                to_core(k, c).start()
        for c in range(CHUNKS):
            for k in far:
                to_core(k, c).wait_recv()
                both = own[k][span(c)].astype(F32) + from_core[k, span(c)].astype(F32)
                total[k - 1, span(c)] = both.astype(BF16)
                along(k, c).start()
        gained = jnp.zeros((1, width), F32)
        biased = jnp.zeros((1, width), F32)
        for c in range(CHUNKS):
            to_core(0, c).wait_recv()
            gradient = own[0][span(c)].astype(F32) + from_core[0, span(c)].astype(F32)
            for k in far:
                along(k, c).wait_recv()
                gradient = gradient + from_x[k - 1, span(c)].astype(F32)
            for ref in came:
                gradient = gradient + ref[span(c)].astype(F32)
            unit = base_ref[span(c)].astype(F32)
            unit = unit - jnp.mean(unit, axis=1, keepdims=True)
            inverse = lax.rsqrt(jnp.mean(unit * unit, axis=1, keepdims=True) + epsilon)
            unit = unit * inverse
            gained = gained + jnp.sum(gradient * unit, axis=0, keepdims=True)
            biased = biased + jnp.sum(gradient, axis=0, keepdims=True)
            scaled = gradient * gain_ref[0:1, :]
            middle = jnp.mean(scaled, axis=1, keepdims=True)
            tilt = jnp.mean(scaled * unit, axis=1, keepdims=True)
            result = prior_ref[span(c)].astype(F32) + inverse * (scaled - middle - unit * tilt)
            grad_ref[span(c)] = result
            if low:
                low_ref[span(c)] = result.astype(BF16)
        which = lax.broadcasted_iota(jnp.int32, (8, width), 0)
        sums_ref[...] = jnp.where(which == 0, gained, jnp.where(which == 1, biased, 0.0))
        for c in range(CHUNKS):
            for k in range(held):
                to_core(k, c).wait_send()
            for k in far:
                along(k, c).wait_send()

    vmem = pl.BlockSpec(memory_space=pltpu.VMEM)
    block = (rows, width)
    several = (max(held - 1, 1),) + (block if held > 1 else (8, LANES))
    kinds = [(block, F32)] + ([(block, BF16)] if low else []) + [((8, width), F32)]
    operands = [value for pair in parts for value in pair] + list(arriving)
    operands += [base, prior, jnp.broadcast_to(gain[None], (8, width))]
    return pl.pallas_call(
        kernel,
        in_specs=[vmem] * len(operands),
        out_specs=[vmem] * len(kinds),
        out_shape=[jax.ShapeDtypeStruct(*kind) for kind in kinds],
        scratch_shapes=[
            pltpu.VMEM((held,) + block, BF16),
            pltpu.VMEM(several, BF16),
            pltpu.VMEM(several, BF16),
        ]
        + [dma((held, CHUNKS))] * 4,
        compiler_params=talking(collective_id),
        name="closing_rows",
    )(*operands)


class SeqShare:
    def __init__(self, place, piece, whole, sems, number):
        self.place, self.piece, self.whole = place, piece, whole
        self.x_send, self.x_recv, self.c_send, self.c_recv, self.here = (
            [sem.at[number] for sem in sems]
        )

    def x(self, k):
        p = self.place
        return remote(
            self.piece, self.whole.at[p.seq], self.x_send.at[k], self.x_recv.at[k],
            seq=p.along_x(k),
        )

    def core(self, k):
        p = self.place
        slot = self.whole.at[p.along_x(-k)]
        return remote(
            self.piece if k == 0 else slot, slot, self.c_send.at[k], self.c_recv.at[k],
            seq=p.other(),
        )

    def keep(self):
        return pltpu.make_async_copy(self.piece, self.whole.at[self.place.seq], self.here)

    def start(self):
        for k in range(1, self.place.chips):
            self.x(k).start()
        self.core(0).start()
        self.keep().start()

    def finish(self):
        for k in range(1, self.place.chips):
            self.x(k).wait_recv()
            self.core(k).start()
        for k in range(self.place.chips):
            self.core(k).wait()
        for k in range(1, self.place.chips):
            self.x(k).wait_send()
        self.keep().wait()


def share_sems(chips, count):
    dma = pltpu.SemaphoreType.DMA
    return [dma((count, chips))] * 4 + [dma((count,))]


def share_pieces(pieces, seq_size, fsdp_size, collective_id):
    chips = seq_size // CORES
    count = len(pieces)

    def kernel(*refs):
        ins, outs, sems = refs[:count], refs[count : 2 * count], refs[2 * count :]
        p = Place(seq_size, fsdp_size)
        greet(p, False)
        shares = [SeqShare(p, ins[i], outs[i], sems, i) for i in range(count)]
        for share in shares:
            share.start()
        for share in shares:
            share.finish()

    return pl.pallas_call(
        kernel,
        in_specs=[pl.BlockSpec(memory_space=pltpu.VMEM)] * count,
        out_specs=[pl.BlockSpec(memory_space=pl.ANY)] * count,
        out_shape=[jax.ShapeDtypeStruct((seq_size,) + v.shape, v.dtype) for v in pieces],
        scratch_shapes=share_sems(chips, count),
        compiler_params=talking(collective_id),
        name="share_pieces",
    )(*pieces)


def sum_and_share(partial, vectors, pieces, seq_size, fsdp_size, collective_id):
    chips = seq_size // CORES
    deep = planes(fsdp_size)
    across = fsdp_size // deep
    rows, width = partial.shape[0] // fsdp_size, partial.shape[1]
    lanes = vectors.shape[1] // fsdp_size
    count = len(pieces) + 1
    dma = pltpu.SemaphoreType.DMA

    def kernel(part_ref, vec_ref, *refs):
        ins, refs = refs[: count - 1], refs[count - 1 :]
        outs, refs = refs[:count], refs[count:]
        (
            vec_out, from_y, over_y, from_z, piece, vec_cut, vec_f, vec_s, vec_sum,
            y_send, y_recv, z_send, z_recv, f_send, f_recv, s_send, s_recv,
        ) = refs[:17]
        sems = refs[17:]
        p = Place(seq_size, fsdp_size)
        greet_all(p)

        def block(z, y):
            return pl.ds(pl.multiple_of((z * across + y) * rows, rows), rows)

        def to_y(z, k):
            return remote(
                part_ref.at[block(z, (p.y + k) % across)], from_y.at[k, z],
                y_send.at[k, z], y_recv.at[k, z], fsdp=p.along_y(k),
            )

        def to_z(k):
            return remote(
                over_y.at[(p.z + k) % deep], from_z.at[k],
                z_send.at[k], z_recv.at[k], fsdp=p.along_z(k),
            )

        def vec_to(k):
            return remote(
                vec_cut.at[(p.fsdp + k) % fsdp_size], vec_f.at[k],
                f_send.at[k], f_recv.at[k], fsdp=(p.fsdp + k) % fsdp_size,
            )

        def vec_over(k):
            return remote(
                vec_sum, vec_s.at[k], s_send.at[k], s_recv.at[k], seq=(p.seq + k) % seq_size
            )

        for f in range(fsdp_size):
            vec_cut[f] = vec_ref[:, f * lanes : (f + 1) * lanes]
        for k in range(1, fsdp_size):
            vec_to(k).start()
        for z in range(deep):
            for k in range(1, across):
                to_y(z, k).start()
        shares = [SeqShare(p, ins[i], outs[i], sems, i) for i in range(count - 1)]
        for share in shares:
            share.start()
        for z in range(deep):
            total = part_ref[block(z, p.y)].astype(F32)
            for k in range(1, across):
                to_y(z, k).wait_recv()
                total = total + from_y[k, z].astype(F32)
            over_y[z] = total.astype(BF16)
        for k in range(1, deep):
            to_z(k).start()
        vec_total = vec_cut[p.fsdp]
        for k in range(1, fsdp_size):
            vec_to(k).wait_recv()
            vec_total = vec_total + vec_f[k]
        vec_sum[...] = vec_total
        for k in range(1, seq_size):
            vec_over(k).start()
        total = over_y[p.z].astype(F32)
        for k in range(1, deep):
            to_z(k).wait_recv()
            total = total + from_z[k].astype(F32)
        piece[...] = total.astype(BF16)
        shares.append(SeqShare(p, piece, outs[-1], sems, count - 1))
        shares[-1].start()
        for k in range(1, seq_size):
            vec_over(k).wait_recv()
            vec_total = vec_total + vec_s[k]
        vec_out[...] = vec_total
        for share in shares:
            share.finish()
        for z in range(deep):
            for k in range(1, across):
                to_y(z, k).wait_send()
        for k in range(1, deep):
            to_z(k).wait_send()
        for k in range(1, fsdp_size):
            vec_to(k).wait_send()
        for k in range(1, seq_size):
            vec_over(k).wait_send()

    vmem = pl.BlockSpec(memory_space=pltpu.VMEM)
    shapes = [v.shape for v in pieces] + [(rows, width)]
    cut = (8, lanes)
    return pl.pallas_call(
        kernel,
        in_specs=[vmem] * (count + 1),
        out_specs=[pl.BlockSpec(memory_space=pl.ANY)] * count + [vmem],
        out_shape=[jax.ShapeDtypeStruct((seq_size,) + shape, BF16) for shape in shapes]
        + [jax.ShapeDtypeStruct(cut, F32)],
        scratch_shapes=[
            pltpu.VMEM((across, deep, rows, width), BF16),
            pltpu.VMEM((deep, rows, width), BF16),
            pltpu.VMEM((deep, rows, width), BF16),
            pltpu.VMEM((rows, width), BF16),
            pltpu.VMEM((fsdp_size,) + cut, F32),
            pltpu.VMEM((fsdp_size,) + cut, F32),
            pltpu.VMEM((seq_size,) + cut, F32),
            pltpu.VMEM(cut, F32),
        ]
        + [dma((across, deep))] * 2
        + [dma((deep,))] * 2
        + [dma((fsdp_size,))] * 2
        + [dma((seq_size,))] * 2
        + share_sems(chips, count),
        compiler_params=talking(collective_id),
        name="sum_and_share",
    )(partial, vectors, *pieces)


def own_columns(gate, up, me, seq_size, fsdp_size):
    rows, columns = gate.shape
    shard = columns // fsdp_size
    chunk = shard // seq_size

    def kernel(me_ref, gate_ref, up_ref, out_ref):
        for s in range(seq_size):

            @pl.when(me_ref[0] == s)
            def _(s=s):
                for which, ref in enumerate((gate_ref, up_ref)):
                    taken = [
                        ref[:, f * shard + s * chunk : f * shard + (s + 1) * chunk]
                        for f in range(fsdp_size)
                    ]
                    at = which * chunk * fsdp_size
                    out_ref[:, at : at + chunk * fsdp_size] = jnp.concatenate(taken, axis=1)

    return pl.pallas_call(
        kernel,
        grid_spec=pltpu.PrefetchScalarGridSpec(
            num_scalar_prefetch=1,
            grid=(1,),
            in_specs=[pl.BlockSpec((rows, columns), lambda i, m: (0, 0))] * 2,
            out_specs=pl.BlockSpec((rows, 2 * chunk * fsdp_size), lambda i, m: (0, 0)),
        ),
        out_shape=jax.ShapeDtypeStruct((rows, 2 * chunk * fsdp_size), BF16),
        compiler_params=params(),
        cost_estimate=cost(rows, 1, 2 * columns),
        name="own_columns",
    )(jnp.full((1,), me, jnp.int32), gate, up)


def whole_columns(pieces, fsdp_size):
    seq_size, rows, columns = pieces.shape
    units = columns // 2
    chunk = units // fsdp_size

    def kernel(in_ref, gate_ref, up_ref):
        for which, ref in enumerate((gate_ref, up_ref)):
            for f in range(fsdp_size):
                at = which * units + f * chunk
                taken = [in_ref[s, :, at : at + chunk].astype(F32) for s in range(seq_size)]
                whole = jnp.concatenate(taken, axis=1)
                ref[:, f * chunk * seq_size : (f + 1) * chunk * seq_size] = whole

    tile = rows // 4
    out = pl.BlockSpec((tile, units * seq_size), lambda i: (i, 0))
    return pl.pallas_call(
        kernel,
        grid=(4,),
        in_specs=[pl.BlockSpec((seq_size, tile, columns), lambda i: (0, i, 0))],
        out_specs=[out, out],
        out_shape=[jax.ShapeDtypeStruct((rows, units * seq_size), F32)] * 2,
        compiler_params=params(),
        cost_estimate=cost(rows, 1, 2 * columns * seq_size),
        name="whole_columns",
    )(pieces)


def own_heads_spread(project_in, me, pairs, seq_size):
    rows, columns = project_in.shape
    step = seq_size // 2

    def kernel(me_ref, in_ref, out_ref):
        lane = lax.broadcasted_iota(jnp.int32, (rows, LANES), 1)
        odd = me_ref[0] % 2 == 1

        def take(part, place):
            for p in range(pairs):
                at = (2 * p * step + place) * LANES
                first = in_ref[:, at : at + LANES].astype(F32)
                at = at + step * LANES
                second = in_ref[:, at : at + LANES].astype(F32)
                first = jnp.where(odd, pltpu.roll(first, HEAD_DIM, 1), first)
                second = jnp.where(odd, second, pltpu.roll(second, HEAD_DIM, 1))
                both = jnp.where(lane < HEAD_DIM, first, second).astype(BF16)
                at = (3 * p + part) * LANES
                out_ref[:, at : at + LANES] = both

        for part in range(3):
            for place in range(step):
                here = (pl.program_id(0) == part) & (me_ref[0] // 2 == place)
                pl.when(here)(functools.partial(take, part, place))

    return pl.pallas_call(
        kernel,
        grid_spec=pltpu.PrefetchScalarGridSpec(
            num_scalar_prefetch=1,
            grid=(3,),
            in_specs=[pl.BlockSpec((rows, columns // 3), lambda part, m: (0, part))],
            out_specs=pl.BlockSpec((rows, 3 * pairs * LANES), lambda part, m: (0, 0)),
        ),
        out_shape=jax.ShapeDtypeStruct((rows, 3 * pairs * LANES), BF16),
        compiler_params=params(),
        name="own_heads",
    )(jnp.full((1,), me, jnp.int32), project_in)


def whole_heads_spread(pieces):
    seq_size, rows, columns = pieces.shape
    each = columns * seq_size // 3
    step = seq_size // 2

    def kernel(in_ref, out_ref):
        lane = lax.broadcasted_iota(jnp.int32, (rows // 4, LANES), 1)
        for part in range(3):
            for b in range(each // LANES):
                shard, seq = b // step, 2 * (b % step)
                at = (3 * (shard // 2) + part) * LANES
                first = in_ref[seq, :, at : at + LANES].astype(F32)
                second = in_ref[seq + 1, :, at : at + LANES].astype(F32)
                if shard % 2:
                    first = pltpu.roll(first, HEAD_DIM, 1)
                else:
                    second = pltpu.roll(second, HEAD_DIM, 1)
                start = part * each + b * LANES
                out_ref[:, start : start + LANES] = jnp.where(lane < HEAD_DIM, first, second)

    return pl.pallas_call(
        kernel,
        grid=(4,),
        in_specs=[pl.BlockSpec((seq_size, rows // 4, columns), lambda i: (0, i, 0))],
        out_specs=pl.BlockSpec((rows // 4, 3 * each), lambda i: (i, 0)),
        out_shape=jax.ShapeDtypeStruct((rows, 3 * each), F32),
        compiler_params=params(),
        cost_estimate=cost(rows, 1, 3 * each),
        name="whole_heads",
    )(pieces)


def gather_fsdp(value):
    return lax.all_gather(value, "fsdp", axis=0, tiled=True)


def scatter_fsdp(value):
    return lax.psum_scatter(value, "fsdp", scatter_dimension=0, tiled=True)


def local(
    tokens,
    cont_lengths,
    project_in,
    project_out,
    gate_weight,
    up_weight,
    down_weight,
    first_gain,
    first_bias,
    second_gain,
    second_bias,
    grad_output,
):
    rows_dev, width = tokens.shape[1:]
    seq_size = lax.axis_size("seq")
    fsdp_size = lax.axis_size("fsdp")
    chips = seq_size // CORES
    total_rows = rows_dev * seq_size
    me = lax.axis_index("seq")
    order = seq_order(chips)
    shard_rows = project_in.shape[0]
    own_pairs = width // LANES // seq_size
    pieces_out = project_out.shape[0] // seq_size
    pieces_down = down_weight.shape[0] // seq_size
    far = range(1, chips)

    spread = pieces_out == HEAD_DIM
    if spread:
        in_part = own_heads_spread(project_in, me, own_pairs, seq_size)
    else:
        in_part = own_heads(project_in, me, own_pairs)
    vectors = jnp.stack([first_gain, first_bias, second_gain, second_bias]).astype(F32)
    all_tokens, w_in, vectors = opening(
        tokens[0],
        in_part,
        jnp.concatenate([vectors, vectors]),
        seq_size,
        fsdp_size,
    )
    down_late, out_late = tie((down_weight, project_out), w_in)
    if spread:
        w_out = gather_fsdp(lax.dynamic_slice_in_dim(out_late, me * pieces_out, pieces_out, 0))
    else:
        own_rows = width // seq_size
        w_out = lax.dynamic_slice_in_dim(gather_fsdp(project_out), me * own_rows, own_rows, 0)
    vectors = jnp.transpose(vectors[:, :4], (1, 0, 2)).reshape(4, width)
    gain_one, bias_one, gain_two, bias_two = [vectors[i] for i in range(4)]
    upstream_own = tie(grad_output[0], all_tokens)
    upstream_far = [from_chip(upstream_own, chips, ahead) for ahead in far]
    w_down = gather_fsdp(lax.dynamic_slice_in_dim(down_late, me * pieces_down, pieces_down, 0))
    gate_up_part = own_columns(gate_weight, up_weight, me, seq_size, fsdp_size)

    cosine, sine, ends = rope_tables(cont_lengths[0], total_rows)

    qkv, normed_first = project(all_tokens, w_in, gain_one, bias_one, cosine, sine)
    attended, qx = attend(ends, qkv)
    upstream_blocks = [grad_output[0], core_swap(grad_output[0], chips)]
    for block in upstream_far:
        block = tie(block, attended)
        upstream_blocks += [block, core_swap(block, chips)]

    def scatter_end(started):
        arriving, own, other, _ = started
        total = own.astype(F32) + other.astype(F32)
        for part in arriving:
            total = total + part.astype(F32)
        return total

    attended = tie(attended, upstream_blocks)
    parts = chip_matmul(attended, w_out, order, rows_dev, False, "attention_out")
    hidden, normed_blocks, w_gate_up = hidden_rows(
        parts, tokens[0], gain_two, bias_two, gate_up_part, seq_size, fsdp_size
    )
    product, grads, normed_second, upstream_all = feed(
        normed_blocks, upstream_blocks, w_gate_up, w_down
    )

    near_order = jnp.arange(chips * CORES, dtype=jnp.int32)

    def send_far(x, weight, x_order, name):
        sent = [
            (own.astype(F32) + core_swap(other, chips).astype(F32)).astype(BF16)
            for own, other in chip_matmul(x, weight, x_order[CORES:], rows_dev, True, name)
        ]
        return sent, [to_chip(value, chips, ahead) for value, ahead in zip(sent, far)]

    sent, arriving = send_far(grads, w_gate_up, near_order, "feed_back")
    own, other, grad_down = near_and_grad(
        tie(grads, *sent), w_gate_up, near_order[:CORES], product, upstream_all, rows_dev,
        "near_and_down",
    )
    grad_hidden, low_own, sums_two = closing_rows(
        [(own, other)], tie(arriving, grad_down), hidden, grad_output[0], gain_two,
        seq_size, fsdp_size, True, 3,
    )
    low_far = [from_chip(low_own, chips, ahead) for ahead in far]
    low_near = [low_own, core_swap(low_own, chips)]

    normed_late, product_late = tie((normed_second, product), low_own)
    grad_gate_up = weight_grad(normed_late, grads, "grad_gate_up")
    product_late = tie(product_late, grad_gate_up)

    layer_parts = chip_matmul(product_late, w_down, near_order, rows_dev, False, "feed_down")
    (layer_own, layer_other), layer_far = layer_parts[0], layer_parts[1:]
    low_far = tie(low_far, layer_own)
    layer_far = tie(layer_far, low_far)
    grad_down_piece = scatter_fsdp(tie(grad_down, arriving))
    grad_gate_up_piece = scatter_fsdp(tie(grad_gate_up, low_far))
    low_blocks = low_near
    for block in low_far:
        low_blocks = low_blocks + [block, core_swap(block, chips)]
    layer_sent = [
        (own.astype(F32) + core_swap(other, chips).astype(F32)).astype(BF16)
        for own, other in layer_far
    ]
    layer_arriving = [to_chip(s, chips, ahead) for s, ahead in zip(layer_sent, far)]
    grad_attended, low_hidden = blocks_matmul(low_blocks, w_out, order)
    grad_out = dot_first(attended, low_hidden).astype(BF16)
    grad_attended = tie(grad_attended, grad_out, layer_sent)

    grad_qkv = attend_back(ends, qkv, qx, grad_attended, attended, cosine, sine)
    grad_qkv = tie(grad_qkv, layer_arriving)
    sent, arriving = send_far(grad_qkv, w_in, order, "project_back")
    grad_late = tie(grad_qkv, *sent)
    own, other, grad_in = near_and_grad(
        grad_late, w_in, order[:CORES], normed_first, grad_late, rows_dev, "near_and_project_in"
    )
    arriving = tie(arriving, grad_in)
    grad_in_piece = scatter_fsdp(tie(grad_in, arriving))
    input_gradient, sums_one = closing_rows(
        [(own, other)], arriving, tokens[0], grad_hidden, gain_one,
        seq_size, fsdp_size, False, 4,
    )
    layer_rows = hidden + scatter_end(
        (layer_arriving, layer_own, core_swap(layer_other, chips), None)
    )

    sums = jnp.concatenate([sums_one[:2], sums_two[:2], sums_one[2:6]])
    all_gate_up, all_down, all_out, sums = sum_and_share(
        grad_out, sums, [grad_gate_up_piece, grad_down_piece], seq_size, fsdp_size, 5
    )
    (all_in,) = share_pieces([tie(grad_in_piece, all_out)], seq_size, fsdp_size, 6)
    if spread:
        grad_in = whole_heads_spread(all_in)
        grad_out = all_out.reshape(project_out.shape).astype(F32)
    else:
        grad_in = all_in.reshape(seq_size, shard_rows, own_pairs, 3, LANES)
        grad_in = jnp.transpose(grad_in, (1, 3, 0, 2, 4)).reshape(shard_rows, 3 * width)
        grad_in = grad_in.astype(F32)
        whole = jnp.zeros((width, width), F32)
        whole = lax.dynamic_update_slice_in_dim(
            whole, grad_out.astype(F32), me * (width // seq_size), 0
        )
        grad_out = lax.psum(scatter_fsdp(whole), "seq")
    grad_gate, grad_up = whole_columns(all_gate_up, fsdp_size)
    return (
        layer_rows.astype(BF16)[None],
        input_gradient[None],
        grad_in,
        grad_out,
        grad_gate,
        grad_up,
        all_down.reshape(down_weight.shape).astype(F32),
        sums[0],
        sums[1],
        sums[2],
        sums[3],
    )


def solution(mesh):
    return jax.shard_map(
        local,
        mesh=mesh,
        in_specs=(
            P("fsdp", "seq", None),
            P("fsdp", None),
            P("fsdp", None),
            P("fsdp", None),
            P("fsdp", None),
            P("fsdp", None),
            P("fsdp", None),
            P("fsdp"),
            P("fsdp"),
            P("fsdp"),
            P("fsdp"),
            P("fsdp", "seq", None),
        ),
        out_specs=(
            P("fsdp", "seq", None),
            P("fsdp", "seq", None),
            P("fsdp", None),
            P("fsdp", None),
            P("fsdp", None),
            P("fsdp", None),
            P("fsdp", None),
            P("fsdp"),
            P("fsdp"),
            P("fsdp"),
            P("fsdp"),
        ),
        check_vma=False,
    )
```
